32 devices in a mesh: dp: 8 (over y, x, core), tensor: 4 (over z).
Axes of the slice: x: 2, y: 2, z: 4, core: 2. Of those that a mesh axis runs over, the one named last changes fastest.
Arguments:
- tokens: bfloat16 [12288, 2048], P(('dp', 'tensor')), may hold values from -6 to 6
- norm_attn: bfloat16 [2048], P('dp'), may hold values from 0.099609375 to 1.8984375
- w_query: bfloat16 [2048, 2048], P('dp', 'tensor'), may hold values from -0.125 to 0.125
- w_key: bfloat16 [2048, 128], P('dp'), may hold values from -0.125 to 0.125
- w_value: bfloat16 [2048, 128], P('dp'), may hold values from -0.125 to 0.125
- w_out: bfloat16 [2048, 2048], P('tensor', 'dp'), may hold values from -0.75 to 0.75
- norm_ffn: bfloat16 [2048], P('dp'), may hold values from 0.099609375 to 1.8984375
- w_gate: bfloat16 [2048, 5632], P('dp', 'tensor'), may hold values from -0.125 to 0.125
- w_up: bfloat16 [2048, 5632], P('dp', 'tensor'), may hold values from -0.125 to 0.125
- w_down: bfloat16 [5632, 2048], P('tensor', 'dp'), may hold values from -0.078125 to 0.078125
- segment_ids: int32 [12288], P('dp'), may hold values from 0 to 103, as said below
- parents: int32 [104], replicated, may hold values from 0 to 95, as said below
- positions: int32 [12288], P('dp'), may hold values from 0 to 927, as said below
- d_out: bfloat16 [12288, 2048], P(('dp', 'tensor')), may hold values from -6 to 6
- d_keys: bfloat16 [12288, 128], P(('dp', 'tensor')), may hold values from -6 to 6
- d_values: bfloat16 [12288, 128], P(('dp', 'tensor')), may hold values from -6 to 6
Outputs:
- out: bfloat16 [12288, 2048], P(('dp', 'tensor'))
- keys: bfloat16 [12288, 128], P('dp')
- values: bfloat16 [12288, 128], P('dp')
- d_x: float32 [12288, 2048], P(('dp', 'tensor'))
- g_norm_attn: float32 [2048], P('dp')
- g_query: float32 [2048, 2048], P('dp', 'tensor')
- g_key: float32 [2048, 128], P('dp')
- g_value: float32 [2048, 128], P('dp')
- g_out: float32 [2048, 2048], P('tensor', 'dp')
- g_norm_ffn: float32 [2048], P('dp')
- g_gate: float32 [2048, 5632], P('dp', 'tensor')
- g_up: float32 [2048, 5632], P('dp', 'tensor')
- g_down: float32 [5632, 2048], P('tensor', 'dp')
The draws below stay inside these ranges and needn't reach their ends.
Inputs may be any that keep to these rules, and one draw needn't show every extreme that they name: `segment_ids`: tree t holds tokens t * 1536 to (t + 1) * 1536 - 1 and segments 13 t to 13 t + 12 in this order: a trunk of 768 tokens, four branches of 64 tokens, eight leaves whose two of each branch have lengths summing to 128, each leaf 64 // 2 tokens or more; ids never fall. `parents`: A trunk is its own parent, a branch's parent is its tree's trunk, a leaf's parent is a branch of its tree, and each branch is the parent of exactly two leaves. `positions`: counts up by one within a segment from 0 at a trunk's first token, from 768 at a branch's first token and from 832 at a leaf's first token.
All inputs are finite; a program needn't handle non-finite values.
Results may differ from the reference program's by a relative error of at most 0.022.
Values may be sent and summed in bfloat16 or wider, within the bound.
No kernel may reach another device: no remote copies, remote signals or barrier semaphores. Data moves between devices by JAX's collectives and lax.ppermute only.
A program may use at most 256 MiB of HBM per device.

```python
import jax
import jax.numpy as jnp
from jax import lax

D = 2048
HQ = 16
HD = 128
FF = 5632
TRUNK = 768
BRANCH = 64
LEAF = 64
QBLOCK = 512
GROUP = 1536
TREES = 8
TOKENS = 12288
N_DP = 8


def tree_tables(key):
    key = jax.random.fold_in(key, 11)
    tree_keys = jax.random.split(key, TREES)

    def one_tree(tree_key, tree):
        key_order, key_delta, key_long = jax.random.split(tree_key, 3)
        order = jax.random.permutation(key_order, 8)
        owner = order // 2
        leading = order % 2 == 0
        deltas = jax.random.randint(key_delta, (4,), 0, LEAF // 2 + 1)
        longest = jax.random.randint(key_long, (), 0, 4)
        deltas = jnp.where(jnp.arange(4) == longest, LEAF // 2, deltas)
        own_delta = jnp.sum(jnp.where(owner[:, None] == jnp.arange(4)[None, :], deltas[None, :], 0), axis=1)
        lengths = LEAF + jnp.where(leading, own_delta, -own_delta)
        ends = jnp.cumsum(lengths)
        starts = ends - lengths
        place = jnp.arange(GROUP)
        branch_off = place - TRUNK
        leaf_off = place - TRUNK - 4 * BRANCH
        slot = jnp.sum((leaf_off[:, None] >= ends[None, :]).astype(jnp.int32), axis=1)
        slot = jnp.minimum(slot, 7)
        slot_start = jnp.sum(jnp.where(slot[:, None] == jnp.arange(8)[None, :], starts[None, :], 0), axis=1)
        in_trunk = place < TRUNK
        in_branch = (place >= TRUNK) & (leaf_off < 0)
        local = jnp.where(in_trunk, 0, jnp.where(in_branch, 1 + branch_off // BRANCH, 5 + slot))
        depth = jnp.where(in_trunk, place, jnp.where(in_branch, TRUNK + branch_off % BRANCH, TRUNK + BRANCH + leaf_off - slot_start))
        parent_local = jnp.concatenate([jnp.zeros((5,), jnp.int32), (1 + owner).astype(jnp.int32)])
        base = 13 * tree
        return ((base + local).astype(jnp.int32), (base + parent_local).astype(jnp.int32), depth.astype(jnp.int32))
    segment, parent, depth = jax.vmap(one_tree)(tree_keys, jnp.arange(TREES))
    return (segment.reshape(-1), parent.reshape(-1), depth.reshape(-1))


def draw_segment_ids(key, part):
    return tree_tables(key)[0]


def draw_parents(key, part):
    return tree_tables(key)[1]


def draw_positions(key, part):
    return tree_tables(key)[2]


def steps_of(rng, shape, cuts, least, top_value):
    level = 1.0
    for axis_at, blocks in cuts:
        heights = jax.random.uniform(jax.random.fold_in(jax.random.fold_in(rng, 6), axis_at), (blocks,), jnp.float32, least / len(cuts), top_value / len(cuts))
        level = level * jnp.repeat(jnp.exp(heights), shape[axis_at] // blocks).reshape((-1,) + (1,) * (len(shape) - 1 - axis_at))
    return level


def bell_draw(key, shape, deviation, reach, cuts=(), kind=jnp.bfloat16):
    drawn = jax.random.normal(key, shape, jnp.float32) * deviation
    if len(cuts) > 0:
        drawn = steps_of(key, shape, cuts, -0.22, 0.18) * drawn
    return jnp.clip(drawn, min=-reach, max=reach).astype(kind)


def setup_inputs(seed: int = 0) -> dict:
    arg_keys = jax.random.split(jax.random.key(seed), 17)
    return {
        "tokens": bell_draw(arg_keys[0], (TOKENS, D), 1.0, 6.0, ((0, 32),)),
        "norm_attn": jnp.clip(1.0 + 0.18 * jax.random.normal(arg_keys[1], (D,), jnp.float32), 0.099609375, 1.8984375).astype(jnp.bfloat16),
        "w_query": bell_draw(arg_keys[2], (D, HQ * HD), D ** -0.5, 0.125, ((0, 8), (1, 4))),
        "w_key": bell_draw(arg_keys[3], (D, HD), D ** -0.5, 0.125, ((0, 8),)),
        "w_value": bell_draw(arg_keys[4], (D, HD), D ** -0.5, 0.125, ((0, 8),)),
        "w_out": bell_draw(arg_keys[5], (HQ * HD, D), (HQ * HD // 32) ** -0.5, 0.75, ((0, 4), (1, 8))),
        "norm_ffn": jnp.clip(1.0 + 0.18 * jax.random.normal(arg_keys[6], (D,), jnp.float32), 0.099609375, 1.8984375).astype(jnp.bfloat16),
        "w_gate": bell_draw(arg_keys[7], (D, FF), D ** -0.5, 0.125, ((0, 8), (1, 4))),
        "w_up": bell_draw(arg_keys[8], (D, FF), D ** -0.5, 0.125, ((0, 8), (1, 4))),
        "w_down": bell_draw(arg_keys[9], (FF, D), FF ** -0.5, 0.078125, ((0, 4), (1, 8))),
        "segment_ids": draw_segment_ids(jax.random.fold_in(arg_keys[16], 71), 0),
        "parents": draw_parents(jax.random.fold_in(arg_keys[16], 71), 0),
        "positions": draw_positions(jax.random.fold_in(arg_keys[16], 71), 0),
        "d_out": bell_draw(arg_keys[13], (TOKENS, D), 1.0, 6.0, ((0, 32),)),
        "d_keys": bell_draw(arg_keys[14], (TOKENS, HD), 1.0, 6.0, ((0, 32),)),
        "d_values": bell_draw(arg_keys[15], (TOKENS, HD), 1.0, 6.0, ((0, 32),)),
    }


norm_eps = 1e-05

@jax.custom_vjp
def low(v):
    return lax.optimization_barrier(v.astype(jnp.bfloat16)).astype(jnp.float32)

@jax.custom_vjp
def low_back(v):
    return v

def low_keep(v):
    return (low(v), None)

def low_pass(kept, grad):
    return (grad,)

def back_keep(v):
    return (v, None)

def back_low(kept, grad):
    return (low(grad),)
low.defvjp(low_keep, low_pass)
low_back.defvjp(back_keep, back_low)

def matmul(left, right):
    return jnp.dot(left, right, preferred_element_type=jnp.float32, precision=lax.Precision.HIGHEST)

def rms(value, gain):
    return value * lax.rsqrt(lax.optimization_barrier(jnp.mean(value * value, axis=-1, keepdims=True)) + norm_eps) * gain

def layer(residual, attn_gain, query_w, key_w, value_w, out_w, ffn_gain, gate_w, up_w, down_w, segment, first_up, second_up, place):
    normed = low(rms(residual, attn_gain))
    query = low_back(low(matmul(normed, query_w)))
    keys = low_back(low(matmul(normed, key_w)))
    values = low_back(low(matmul(normed, value_w)))
    score_scale = HD ** (-0.5)
    blocks = GROUP // QBLOCK

    def attend(operand):
        query_block, segment_block, first_block, second_block, place_block = operand
        linked = (segment[None, :] == segment_block[:, None]) | (segment[None, :] == first_block[:, None]) | (segment[None, :] == second_block[:, None])
        mask = linked & (place[None, :] <= place_block[:, None])
        scores = jnp.einsum('qhd,kd->hqk', query_block, keys, precision=lax.Precision.HIGHEST) * score_scale
        scores = low_back(scores)
        scores = jnp.where(mask[None], scores, -1e+30)
        shares = low(jax.nn.softmax(scores, axis=-1))
        mixed_block = jnp.einsum('hqk,kd->qhd', shares, values, precision=lax.Precision.HIGHEST)
        return mixed_block.reshape(QBLOCK, HQ * HD)
    mixed = lax.map(jax.checkpoint(attend), (query.reshape(blocks, QBLOCK, HQ, HD), segment.reshape(blocks, QBLOCK), first_up.reshape(blocks, QBLOCK), second_up.reshape(blocks, QBLOCK), place.reshape(blocks, QBLOCK)))
    mixed = low_back(low(mixed.reshape(GROUP, HQ * HD)))
    after_attn = residual + low_back(matmul(mixed, out_w))
    ffn_normed = low(rms(after_attn, ffn_gain))
    gate = low_back(matmul(ffn_normed, gate_w))
    upward = low_back(matmul(ffn_normed, up_w))
    hidden = low(jax.nn.silu(gate) * upward)
    return (after_attn + matmul(hidden, down_w), keys, values)

def reference(tokens, norm_attn, w_query, w_key, w_value, w_out, norm_ffn, w_gate, w_up, w_down, segment_ids, parents, positions, d_out, d_keys, d_values):
    params = (norm_attn.astype(jnp.float32), w_query.astype(jnp.float32), w_key.astype(jnp.float32), w_value.astype(jnp.float32), w_out.astype(jnp.float32), norm_ffn.astype(jnp.float32), w_gate.astype(jnp.float32), w_up.astype(jnp.float32), w_down.astype(jnp.float32))
    up_one = parents[segment_ids]
    up_two = parents[up_one]

    def per_tree(totals, operand):
        residual, segment, first_up, second_up, place, grad_out, grad_keys, grad_values = operand

        def forward(resid_in, attn_gain, query_w, key_w, value_w, out_w, ffn_gain, gate_w, up_w, down_w):
            return layer(resid_in, attn_gain, query_w, key_w, value_w, out_w, ffn_gain, gate_w, up_w, down_w, segment, first_up, second_up, place)
        outputs, pullback = jax.vjp(forward, residual, *params)
        grads = pullback((grad_out, grad_keys, grad_values))
        totals = tuple((left + right for left, right in zip(totals, grads[1:])))
        return (totals, (outputs[0], outputs[1], outputs[2], grads[0]))
    initial = tuple((jnp.zeros(item.shape, jnp.float32) for item in params))
    operands = (tokens.astype(jnp.float32).reshape(N_DP, GROUP, D), segment_ids.reshape(N_DP, GROUP), up_one.reshape(N_DP, GROUP), up_two.reshape(N_DP, GROUP), positions.reshape(N_DP, GROUP), d_out.astype(jnp.float32).reshape(N_DP, GROUP, D), d_keys.astype(jnp.float32).reshape(N_DP, GROUP, HD), d_values.astype(jnp.float32).reshape(N_DP, GROUP, HD))
    totals, stacked = lax.scan(per_tree, initial, operands)
    return (stacked[0].reshape(TOKENS, D).astype(jnp.bfloat16), stacked[1].reshape(TOKENS, HD).astype(jnp.bfloat16), stacked[2].reshape(TOKENS, HD).astype(jnp.bfloat16), stacked[3].reshape(TOKENS, D), totals[0], totals[1], totals[2], totals[3], totals[4], totals[5], totals[6], totals[7], totals[8])
```

```python
import functools

import jax
import jax.numpy as jnp
from jax import lax
from jax.sharding import PartitionSpec as P

HD = 128
norm_eps = 1e-05
F32 = jnp.float32
BF16 = jnp.bfloat16


def dot(left, right, dims):
    return lax.dot_general(left, right, ((dims[0], dims[1]), ((), ())), preferred_element_type=F32)


def nn(left, right):
    return dot(left, right, ((1,), (0,)))


def nt(left, right):
    return dot(left, right, ((1,), (1,)))


def tn(left, right):
    return dot(left, right, ((0,), (0,)))


def lookup(ids, table):
    hits = ids[:, None] == jnp.arange(table.shape[0], dtype=jnp.int32)[None, :]
    return jnp.sum(jnp.where(hits, table[None, :], 0), axis=1)


def norm_back(value, scale, gain, grad):
    weighted = grad * gain
    return scale * weighted - value * (scale * scale * scale) * jnp.mean(
        weighted * value, axis=-1, keepdims=True
    )


def bit_orders(ndp):
    bits = []
    bit = 2
    while bit < ndp:
        bits.append(bit)
        bit *= 2
    return bits, bits[::-1]


def plane_swap(array, ndp, step):
    orders = bit_orders(ndp)
    return lax.ppermute(array, "dp", [(d, d ^ orders[d & 1][step]) for d in range(ndp)])


def core_swap(array, ndp):
    return lax.ppermute(array, "dp", [(d, d ^ 1) for d in range(ndp)])


def slice_table(me, ndp):
    orders = bit_orders(ndp)
    count = len(orders[0])
    table = []
    for place in range(ndp):
        base = me ^ (place // (ndp // 2))
        even = base % 2 == 0
        owner = base
        for step in range(count):
            if (place >> step) & 1:
                owner = owner ^ jnp.where(even, orders[0][step], orders[1][step])
        table.append(owner)
    return table


def gather_plane(shard, ndp):
    steps = len(bit_orders(ndp)[0])
    pieces = [jnp.concatenate([shard, plane_swap(shard, ndp, 0)], axis=0)]
    for step in range(1, steps):
        pieces = pieces + [plane_swap(piece, ndp, step) for piece in pieces]
    return pieces + [core_swap(piece, ndp) for piece in pieces]


def add_low(left, right):
    return (left.astype(F32) + right.astype(F32)).astype(BF16)


def scatter_plane(pieces, ndp):
    steps = len(bit_orders(ndp)[0])
    half = len(pieces) // 2
    moved = [core_swap(piece, ndp) for piece in pieces[half:]]
    pieces = [add_low(keep, come) for keep, come in zip(pieces[:half], moved)]
    for step in range(steps - 1, 0, -1):
        half = len(pieces) // 2
        moved = [plane_swap(piece, ndp, step) for piece in pieces[half:]]
        pieces = [add_low(keep, come) for keep, come in zip(pieces[:half], moved)]
    piece = pieces[0]
    rows = piece.shape[0] // 2
    return add_low(piece[:rows], plane_swap(piece[rows:], ndp, 0))


def ring_next(array, nt_):
    return lax.ppermute(array, "tensor", [(i, (i + 1) % nt_) for i in range(nt_)])


def shift(array, nt_, by):
    return lax.ppermute(array, "tensor", [(i, (i + by) % nt_) for i in range(nt_)])


def ring_gather(array, nt_):
    blocks = [array]
    for _ in range(nt_ - 1):
        blocks.append(ring_next(blocks[-1], nt_))
    return blocks


def ring_scatter(parts, nt_):
    moving = parts[1]
    for place in range(2, nt_):
        moving = add_low(ring_next(moving, nt_), parts[place])
    return ring_next(moving, nt_).astype(F32) + parts[0].astype(F32)


def stack_rows(pieces):
    return jnp.concatenate(pieces, axis=0)


def take_columns(array, table, width):
    return jnp.concatenate(
        [lax.dynamic_slice_in_dim(array, owner * width, width, axis=1) for owner in table], axis=1
    )


def put_columns(array, table, width):
    out = jnp.zeros_like(array)
    for place, owner in enumerate(table):
        out = lax.dynamic_update_slice_in_dim(
            out, array[:, place * width : (place + 1) * width], owner * width, axis=1
        )
    return out


def attend(query, keys, values, bias):
    tokens = query.shape[0]
    heads = query.shape[1] // HD
    scale = HD ** (-0.5)
    mixed, totals = [], []
    for head in range(heads):
        scores = nt(keys, query[:, head * HD : (head + 1) * HD]) * scale + bias
        peak = jnp.max(scores, axis=0, keepdims=True)
        raised = jnp.exp(scores - peak)
        sums = jnp.sum(raised, axis=0, keepdims=True)
        shares = (raised / sums).astype(BF16)
        mixed.append(tn(shares, values).astype(BF16))
        totals.append(peak + jnp.log(sums))
    return jnp.concatenate(mixed, axis=1), jnp.concatenate(totals, axis=0)


def attend_back(query, keys, values, bias, totals, mixed_grad):
    heads = query.shape[1] // HD
    scale = HD ** (-0.5)
    key_acc, value_acc, query_grad = 0.0, 0.0, []
    for head in range(heads):
        cols = slice(head * HD, (head + 1) * HD)
        scores = nt(keys, query[:, cols]) * scale + bias
        shares = jnp.exp(scores - totals[head : head + 1])
        low_shares = shares.astype(BF16)
        share_grad = nt(values, mixed_grad[:, cols])
        value_acc = value_acc + nn(low_shares, mixed_grad[:, cols])
        inner = jnp.sum(shares * share_grad, axis=0, keepdims=True)
        score_grad = (shares * (share_grad - inner)).astype(BF16)
        query_grad.append((scale * tn(score_grad, keys)).astype(BF16))
        key_acc = key_acc + scale * nn(score_grad, query[:, cols])
    return jnp.concatenate(query_grad, axis=1), key_acc, value_acc


def ffn_block(normed, grad, pieces):
    whole = stack_rows(pieces)
    hidden_units = whole.shape[1] // 3
    gate_w = whole[:, :hidden_units]
    up_w = whole[:, hidden_units : 2 * hidden_units]
    down_w = whole[:, 2 * hidden_units :]
    gate = nn(normed, gate_w)
    upward = nn(normed, up_w)
    sigma = jax.nn.sigmoid(gate)
    hidden = (gate * sigma * upward).astype(BF16)
    part = nt(hidden, down_w).astype(BF16)
    hidden_grad = nn(grad, down_w)
    gate_grad = (hidden_grad * upward * sigma * (1.0 + gate * (1.0 - sigma))).astype(BF16)
    up_grad = (hidden_grad * gate * sigma).astype(BF16)
    back = (nt(gate_grad, gate_w) + nt(up_grad, up_w)).astype(BF16)
    return hidden, gate_grad, up_grad, part, back


def on_device(
    ndp,
    nz,
    tokens,
    norm_attn,
    w_query,
    w_key,
    w_value,
    w_out,
    norm_ffn,
    w_gate,
    w_up,
    w_down,
    segment_ids,
    parents,
    positions,
    d_out,
    d_keys,
    d_values,
):
    me = lax.axis_index("dp")
    place_z = lax.axis_index("tensor")
    table = slice_table(me, ndp)
    own, width = tokens.shape[0], tokens.shape[1]
    rows = width // ndp
    heads_w = w_query.shape[1]
    hidden_units = w_gate.shape[1]

    gains = jnp.concatenate(
        [norm_attn[:, None], norm_ffn[:, None], jnp.zeros((rows, HD - 2), BF16)], axis=1
    )
    small = gather_plane(jnp.concatenate([w_key, w_value, gains], axis=1), ndp)
    attn_ring = ring_gather(jnp.concatenate([w_query, w_out.T], axis=1), nz)
    attn_w = [gather_plane(block, ndp) for block in attn_ring]
    ffn_w = gather_plane(jnp.concatenate([w_gate, w_up, w_down.T], axis=1), ndp)

    small_w = stack_rows(small)
    gain_rows = small_w[:, 2 * HD : 2 * HD + 2].astype(F32).T
    attn_gain, ffn_gain = gain_rows[0:1], gain_rows[1:2]
    kv_w = small_w[:, : 2 * HD]

    residual = take_columns(tokens, table, rows).astype(F32)
    grad_low = take_columns(d_out, table, rows)
    grad_ring = ring_gather(grad_low, nz)

    attn_scale = lax.rsqrt(jnp.mean(residual * residual, axis=-1, keepdims=True) + norm_eps)
    normed = (residual * attn_scale * attn_gain).astype(BF16)
    kv_own = nn(normed, kv_w).astype(BF16)
    kv_ring = [kv_own] + [shift(kv_own, nz, by) for by in range(1, nz)]
    kv = stack_rows(kv_ring)
    keys, values = kv[:, :HD], kv[:, HD:]

    first_up = lookup(segment_ids, parents)
    second_up = lookup(first_up, parents)

    def own_rows(vector):
        return lax.dynamic_slice_in_dim(vector, place_z * own, own, axis=0)

    def ring_rows(vector):
        return jnp.concatenate(
            [
                lax.dynamic_slice_in_dim(vector, ((place_z - r) % nz) * own, own, axis=0)
                for r in range(nz)
            ],
            axis=0,
        )

    key_segment, key_place = ring_rows(segment_ids)[:, None], ring_rows(positions)[:, None]
    linked = (
        (key_segment == own_rows(segment_ids)[None])
        | (key_segment == own_rows(first_up)[None])
        | (key_segment == own_rows(second_up)[None])
    )
    bias = jnp.where(linked & (key_place <= own_rows(positions)[None]), 0.0, -1e30).astype(F32)

    queries, mixes, totals = [], [], []
    attn_sum = 0.0
    for block in range(nz):
        whole = stack_rows(attn_w[block])
        query = nn(normed, whole[:, :heads_w]).astype(BF16)
        mixed, total = attend(query, keys, values, bias)
        attn_sum = attn_sum + nt(mixed, whole[:, heads_w:])
        queries.append(query)
        mixes.append(mixed)
        totals.append(total)
    after_attn = residual + attn_sum
    ffn_scale = lax.rsqrt(jnp.mean(after_attn * after_attn, axis=-1, keepdims=True) + norm_eps)
    ffn_own = (after_attn * ffn_scale * ffn_gain).astype(BF16)

    ffn_ring = ring_gather(ffn_own, nz)
    hiddens, gate_grads, up_grads, parts, backs = [], [], [], [], []
    for block in range(nz):
        hidden, gate_grad, up_grad, part, back = ffn_block(
            ffn_ring[block], grad_ring[block], ffn_w
        )
        hiddens.append(hidden)
        gate_grads.append(gate_grad)
        up_grads.append(up_grad)
        parts.append(part)
        backs.append(back)
    ffn_normed_grad = ring_scatter(backs, nz)
    output = (after_attn + ring_scatter(parts, nz)).astype(BF16)

    ffn_all, grad_all = stack_rows(ffn_ring), stack_rows(grad_ring)
    hidden_all = stack_rows(hiddens)
    gate_up_grad = jnp.concatenate([stack_rows(gate_grads), stack_rows(up_grads)], axis=1)
    pieces = []
    step = width // len(ffn_w)
    for piece in range(len(ffn_w)):
        cols = slice(piece * step, (piece + 1) * step)
        pieces.append(
            jnp.concatenate(
                [tn(ffn_all[:, cols], gate_up_grad), tn(grad_all[:, cols], hidden_all)], axis=1
            ).astype(BF16)
        )
    ffn_w_grad = scatter_plane(pieces, ndp).astype(F32)

    after_grad = grad_low.astype(F32) + norm_back(after_attn, ffn_scale, ffn_gain, ffn_normed_grad)
    ffn_gain_term = jnp.sum(ffn_normed_grad * after_attn * ffn_scale, axis=0)
    branch = after_grad.astype(BF16)

    key_acc, value_acc = 0.0, 0.0
    normed_grad = 0.0
    attn_grads = []
    for block in range(nz):
        whole = stack_rows(attn_w[block])
        mixed_grad = nn(branch, whole[:, heads_w:]).astype(BF16)
        query_grad, key_part, value_part = attend_back(
            queries[block], keys, values, bias, totals[block], mixed_grad
        )
        key_acc, value_acc = key_acc + key_part, value_acc + value_part
        normed_grad = normed_grad + nt(query_grad, whole[:, :heads_w])
        pieces = []
        for piece in range(len(ffn_w)):
            cols = slice(piece * step, (piece + 1) * step)
            pieces.append(
                jnp.concatenate(
                    [tn(normed[:, cols], query_grad), tn(branch[:, cols], mixes[block])], axis=1
                ).astype(BF16)
            )
        attn_grads.append(scatter_plane(pieces, ndp))
    attn_w_grad = ring_scatter(attn_grads, nz)

    kv_acc = jnp.concatenate([key_acc, value_acc], axis=1).astype(BF16)
    kv_sum = kv_acc[:own].astype(F32)
    for by in range(1, nz):
        kv_sum = kv_sum + shift(kv_acc[by * own : (by + 1) * own], nz, -by).astype(F32)
    kv_given = jnp.concatenate([d_keys, d_values], axis=1).astype(F32)
    kv_grad = (kv_sum + kv_given).astype(BF16)
    normed_grad = normed_grad + nt(kv_grad, kv_w)
    input_grad = after_grad + norm_back(residual, attn_scale, attn_gain, normed_grad)
    attn_gain_term = jnp.sum(normed_grad * residual * attn_scale, axis=0)

    small_grad = jnp.concatenate(
        [
            tn(normed, kv_grad),
            attn_gain_term[:, None],
            ffn_gain_term[:, None],
            jnp.zeros((width, HD - 2), F32),
        ],
        axis=1,
    ).astype(BF16)
    small_sum = scatter_plane(
        [small_grad[p * step : (p + 1) * step] for p in range(len(ffn_w))], ndp
    )
    total = small_sum.astype(F32)
    for by in range(1, nz):
        total = total + shift(small_sum, nz, by).astype(F32)

    kv_out = jnp.zeros((nz * own, 2 * HD), BF16)
    for r in range(nz):
        kv_out = lax.dynamic_update_slice_in_dim(
            kv_out, kv_ring[r], ((place_z - r) % nz) * own, axis=0
        )
    return (
        put_columns(output, table, rows),
        kv_out[:, :HD],
        kv_out[:, HD:],
        put_columns(input_grad, table, rows),
        total[:, 2 * HD],
        attn_w_grad[:, :heads_w],
        total[:, :HD],
        total[:, HD : 2 * HD],
        attn_w_grad[:, heads_w:].T,
        total[:, 2 * HD + 1],
        ffn_w_grad[:, :hidden_units],
        ffn_w_grad[:, hidden_units : 2 * hidden_units],
        ffn_w_grad[:, 2 * hidden_units :].T,
    )


def solution(mesh):
    in_specs = (
        P(("dp", "tensor"), None),
        P("dp"),
        P("dp", "tensor"),
        P("dp", None),
        P("dp", None),
        P("tensor", "dp"),
        P("dp"),
        P("dp", "tensor"),
        P("dp", "tensor"),
        P("tensor", "dp"),
        P("dp"),
        P(),
        P("dp"),
        P(("dp", "tensor"), None),
        P(("dp", "tensor"), None),
        P(("dp", "tensor"), None),
    )
    out_specs = (
        P(("dp", "tensor"), None),
        P("dp", None),
        P("dp", None),
        P(("dp", "tensor"), None),
        P("dp"),
        P("dp", "tensor"),
        P("dp", None),
        P("dp", None),
        P("tensor", "dp"),
        P("dp"),
        P("dp", "tensor"),
        P("dp", "tensor"),
        P("tensor", "dp"),
    )
    body = functools.partial(on_device, mesh.shape["dp"], mesh.shape["tensor"])
    return jax.shard_map(
        body, mesh=mesh, in_specs=in_specs, out_specs=out_specs, check_vma=False
    )
```

```python
import functools

import jax
import jax.numpy as jnp
from jax import lax
from jax.experimental import pallas as pl
from jax.experimental.pallas import tpu as pltpu
from jax.sharding import PartitionSpec as P

HD = 128
norm_eps = 1e-05
F32 = jnp.float32
BF16 = jnp.bfloat16


def dot(left, right, dims):
    return lax.dot_general(left, right, ((dims[0], dims[1]), ((), ())), preferred_element_type=F32)


def nn(left, right):
    return dot(left, right, ((1,), (0,)))


def nt(left, right):
    return dot(left, right, ((1,), (1,)))


def tn(left, right):
    return dot(left, right, ((0,), (0,)))


def lookup(ids, table):
    hits = ids[:, None] == jnp.arange(table.shape[0], dtype=jnp.int32)[None, :]
    return jnp.sum(jnp.where(hits, table[None, :], 0), axis=1)


def norm_back(value, scale, gain, grad):
    weighted = grad * gain
    return scale * weighted - value * (scale * scale * scale) * jnp.mean(
        weighted * value, axis=-1, keepdims=True
    )


def bit_orders(ndp):
    bits = []
    bit = 2
    while bit < ndp:
        bits.append(bit)
        bit *= 2
    return bits, bits[::-1]


def plane_swap(array, ndp, step):
    orders = bit_orders(ndp)
    return lax.ppermute(array, "dp", [(d, d ^ orders[d & 1][step]) for d in range(ndp)])


def core_swap(array, ndp):
    return lax.ppermute(array, "dp", [(d, d ^ 1) for d in range(ndp)])


def slice_table(me, ndp):
    orders = bit_orders(ndp)
    count = len(orders[0])
    table = []
    for place in range(ndp):
        base = me ^ (place // (ndp // 2))
        even = base % 2 == 0
        owner = base
        for step in range(count):
            if (place >> step) & 1:
                owner = owner ^ jnp.where(even, orders[0][step], orders[1][step])
        table.append(owner)
    return table


def gather_steps(shard, ndp):
    moved = yield [plane_swap(shard, ndp, 0)]
    pieces = [jnp.concatenate([shard, moved[0]], axis=0)]
    for step in range(1, len(bit_orders(ndp)[0])):
        pieces = pieces + (yield [plane_swap(piece, ndp, step) for piece in pieces])
    pieces = pieces + (yield [core_swap(piece, ndp) for piece in pieces])
    yield tuple(pieces)


def ring_gather_steps(block, nt_):
    blocks = [block]
    for _ in range(nt_ - 1):
        blocks += yield [ring_next(blocks[-1], nt_)]
    yield tuple(blocks)


def add_low(left, right):
    return (left.astype(F32) + right.astype(F32)).astype(BF16)


def scatter_steps(keep, send, ndp):
    (come,) = yield [core_swap(send, ndp)]
    rows = keep.shape[0] // 2
    low, high = add_low(keep[:rows], come[:rows]), add_low(keep[rows:], come[rows:])
    yield from chip_steps(low, high, ndp)


def chip_steps(low, high, ndp):
    for step in range(len(bit_orders(ndp)[0]) - 1, 0, -1):
        (come,) = yield [plane_swap(high, ndp, step)]
        rows = low.shape[0] // 2
        low, high = add_low(low[:rows], come[:rows]), add_low(low[rows:], come[rows:])
    (come,) = yield [plane_swap(high, ndp, 0)]
    yield (low, come)


def ring_steps(parts, nt_):
    moving = yield [ring_next(parts[1], nt_)]
    for place in range(2, nt_):
        moving = yield [ring_next(add_low(moving[0], parts[place]), nt_)]
    yield (moving[0], parts[0])


class Flow:
    def __init__(self, name, steps):
        self.name, self.steps = name, steps
        with jax.named_scope(name):
            self.held = next(steps)

    def moving(self):
        return isinstance(self.held, list)

    def go(self, times=1):
        for _ in range(times):
            if self.moving():
                with jax.named_scope(self.name):
                    self.held = self.steps.send(self.held)

    def finish(self):
        while self.moving():
            self.go()
        return self.held


def meet(values, flows, others=()):
    going = [flow for flow in flows if flow.moving()]
    flows = going + [flow for flow in others if flow.moving()]
    held = [item for flow in flows for item in flow.held]
    count = len(values)
    tied = list(tie(*values, *held))
    values, held = tied[:count], tied[count:]
    for flow in flows:
        flow.held, held = held[: len(flow.held)], held[len(flow.held) :]
    for flow in going:
        flow.go()
    return values


def ring_next(array, nt_):
    return lax.ppermute(array, "tensor", [(i, (i + 1) % nt_) for i in range(nt_)])


def shift(array, nt_, by):
    return lax.ppermute(array, "tensor", [(i, (i + by) % nt_) for i in range(nt_)])


def stack_rows(pieces):
    return jnp.concatenate(pieces, axis=0)


def scoped(name, function, *items):
    with jax.named_scope(name):
        return function(*items)


def tie(*values):
    return lax.optimization_barrier(values)


LOG2E = 1.4426950408889634
TILE = 512


def params(count=1):
    return pltpu.CompilerParams(
        dimension_semantics=("arbitrary",) * count, vmem_limit_bytes=58 * 1024 * 1024
    )


def whole(array):
    zeros = (0,) * array.ndim
    return pl.BlockSpec(array.shape, lambda *_: zeros, pipeline_mode=pl.Buffered(1))


def move_kernel(table_ref, in_ref, out_ref):
    out_ref[...] = in_ref[...]


def move_columns(array, table, width, back=False):
    tokens = array.shape[0]

    def far(k, table_ref):
        return (0, table_ref[k])

    def near(k, table_ref):
        return (0, k)

    return pl.pallas_call(
        move_kernel,
        out_shape=jax.ShapeDtypeStruct(array.shape, array.dtype),
        grid_spec=pltpu.PrefetchScalarGridSpec(
            num_scalar_prefetch=1,
            grid=(array.shape[1] // width,),
            in_specs=[pl.BlockSpec((tokens, width), near if back else far)],
            out_specs=pl.BlockSpec((tokens, width), far if back else near),
        ),
        cost_estimate=pl.CostEstimate(flops=0, transcendentals=0, bytes_accessed=2 * array.nbytes),
        compiler_params=params(),
        name="put_columns" if back else "take_columns",
    )(jnp.stack(table).astype(jnp.int32), array)


def pack_attn_kernel(query_ref, out_ref, key_ref, value_ref, gains_ref, near_ref, ring_ref):
    heads_w = query_ref.shape[1]
    turned = out_ref[...].T
    for ref in (near_ref, ring_ref):
        ref[:, :heads_w] = query_ref[...]
        ref[:, heads_w : 2 * heads_w] = turned
    for k, ref in enumerate((key_ref, value_ref, gains_ref)):
        near_ref[:, 2 * heads_w + k * HD : 2 * heads_w + (k + 1) * HD] = ref[...]


def pack_attn(w_query, w_out, w_key, w_value, gains):
    rows, heads_w = w_query.shape
    return pl.pallas_call(
        pack_attn_kernel,
        out_shape=(
            jax.ShapeDtypeStruct((rows, 2 * heads_w + 3 * HD), BF16),
            jax.ShapeDtypeStruct((rows, 2 * heads_w), BF16),
        ),
        cost_estimate=pl.CostEstimate(flops=0, transcendentals=0, bytes_accessed=2_000_000),
        compiler_params=params(0),
        name="pack_attn",
    )(w_query, w_out, w_key, w_value, gains)


def plain_pack_attn(w_query, w_out, w_key, w_value, gains):
    ring = jnp.concatenate([w_query, w_out.T], axis=1)
    return jnp.concatenate([ring, w_key, w_value, gains], axis=1), ring


def pack_ffn_kernel(gate_ref, up_ref, down_ref, out_ref):
    units = gate_ref.shape[1]
    for at in range(0, units, TILE):
        size = min(TILE, units - at)
        out_ref[:, 3 * at : 3 * at + size] = gate_ref[:, at : at + size]
        out_ref[:, 3 * at + size : 3 * at + 2 * size] = up_ref[:, at : at + size]
        out_ref[:, 3 * at + 2 * size : 3 * at + 3 * size] = down_ref[at : at + size, :].T


def pack_ffn(w_gate, w_up, w_down):
    rows, units = w_gate.shape
    return pl.pallas_call(
        pack_ffn_kernel,
        out_shape=jax.ShapeDtypeStruct((rows, 3 * units), BF16),
        cost_estimate=pl.CostEstimate(flops=0, transcendentals=0, bytes_accessed=12 * rows * units),
        compiler_params=params(0),
        name="pack_ffn",
    )(w_gate, w_up, w_down)


def plain_pack_ffn(w_gate, w_up, w_down):
    return jnp.concatenate([w_gate, w_up, w_down.T], axis=1)


def enter_kernel(count, tail, table_ref, tokens_ref, *refs):
    key_refs, value_refs, gain_refs = refs[:count], refs[count : 2 * count], refs[2 * count : tail]
    low_ref, normed_ref, turned_ref, kv_ref, gains_ref = refs[tail:]
    rows = key_refs[0].shape[0]
    slices = table_ref.shape[0]
    size = low_ref.shape[1] // slices
    squares = 0.0
    for k in range(slices):
        start = pl.multiple_of(table_ref[k] * size, size)
        block = tokens_ref[:, pl.ds(start, size)]
        low_ref[:, k * size : (k + 1) * size] = block
        block = block.astype(F32)
        squares = squares + jnp.sum(block * block, axis=-1, keepdims=True)
    scale = lax.rsqrt(squares / low_ref.shape[1] + norm_eps)
    kv = 0.0
    for i in range(count):
        part = slice(i * rows, (i + 1) * rows)
        gains = gain_refs[i][...].astype(F32).T
        gains_ref[:, part] = gains[:8]
        normed = (low_ref[:, part].astype(F32) * scale * gains[0:1]).astype(BF16)
        normed_ref[:, part] = normed
        turned_ref[part, :] = normed.T
        weights = jnp.concatenate([key_refs[i][...], value_refs[i][...]], axis=1)
        kv = kv + nn(normed, weights)
    kv_ref[...] = kv.astype(BF16)


def enter(tokens, table, near, at):
    own, width = tokens.shape
    count, rows = len(near), near[0].shape[0]

    def columns(place):
        return [pl.BlockSpec((rows, HD), lambda i, table_ref: (0, at // HD + place))] * count

    def full(shape):
        return pl.BlockSpec(shape, lambda i, table_ref: (0, 0))

    return pl.pallas_call(
        functools.partial(enter_kernel, count, 3 * count),
        out_shape=(
            jax.ShapeDtypeStruct((own, width), BF16),
            jax.ShapeDtypeStruct((own, width), BF16),
            jax.ShapeDtypeStruct((width, own), BF16),
            jax.ShapeDtypeStruct((own, 2 * HD), BF16),
            jax.ShapeDtypeStruct((8, width), F32),
        ),
        grid_spec=pltpu.PrefetchScalarGridSpec(
            num_scalar_prefetch=1,
            grid=(1,),
            in_specs=[full(tokens.shape)] + columns(0) + columns(1) + columns(2),
            out_specs=[full((own, width))] * 2
            + [full((width, own)), full((own, 2 * HD)), full((8, width))],
        ),
        cost_estimate=pl.CostEstimate(
            flops=4 * own * width * HD, transcendentals=0, bytes_accessed=6_000_000
        ),
        compiler_params=params(),
        name="enter",
    )(jnp.stack(table).astype(jnp.int32), tokens, *near, *near, *near)


def plain_enter(tokens, table, near, at):
    rows = tokens.shape[1] // len(table)
    low = move_columns(tokens, table, rows)
    weights = stack_rows([piece[:, at:] for piece in near])
    gains = weights[:, 2 * HD : 2 * HD + 8].astype(F32).T
    value = low.astype(F32)
    scale = lax.rsqrt(jnp.mean(value * value, axis=-1, keepdims=True) + norm_eps)
    normed = (value * scale * gains[0:1]).astype(BF16)
    return low, normed, normed.T, nn(normed, weights[:, : 2 * HD]).astype(BF16), gains


def pair_up(block):
    return jnp.concatenate([block[:, :HD], block[:, HD:]], axis=0)


def pair_off(block):
    tokens = block.shape[0] // 2
    return jnp.concatenate([block[:tokens], block[tokens:]], axis=1)


def attend_kernel(count, blocks, refs):
    normed_ref, bias_ref, acc_ref = refs[:3]
    kv_refs = refs[3 : 3 + blocks]
    wq_refs = refs[3 + blocks : 3 + blocks + count]
    wo_refs = refs[3 + blocks + count : 3 + blocks + 2 * count]
    query_ref, mixed_ref, total_ref, sum_ref, score_ref = refs[3 + blocks + 2 * count :]
    rows = wq_refs[0].shape[0]
    tokens = normed_ref.shape[0]

    query = sum(
        nn(normed_ref[:, i * rows : (i + 1) * rows], wq_refs[i][...]) for i in range(count)
    ).astype(BF16)
    query_ref[...] = query
    query = pair_up(query)
    peak = None
    for b in range(blocks):
        bias = bias_ref[b * tokens : (b + 1) * tokens, :]
        scores = nt(kv_refs[b][:, :HD], query) * (HD ** (-0.5) * LOG2E)
        scores = scores + jnp.concatenate([bias, bias], axis=1)
        score_ref[b] = scores
        top = jnp.max(scores, axis=0, keepdims=True)
        peak = top if peak is None else jnp.maximum(peak, top)
    sums, mixed = 0.0, 0.0
    for b in range(blocks):
        raised = jnp.exp2(score_ref[b] - peak)
        sums = sums + jnp.sum(raised, axis=0, keepdims=True)
        mixed = mixed + tn(kv_refs[b][:, HD:], raised.astype(BF16))
    total_ref[0] = peak + jnp.log2(sums)
    mixed = pair_off((mixed / sums).T.astype(BF16))
    mixed_ref[...] = mixed

    @pl.when(pl.program_id(0) == 0)
    def _():
        sum_ref[...] = acc_ref[...].astype(F32)

    for i in range(count):
        sum_ref[:, i * rows : (i + 1) * rows] += nt(mixed, wo_refs[i][...])


def attend_block(normed, bias, acc, kv_ring, pieces, many):
    tokens, width = normed.shape
    count, blocks = len(pieces), len(kv_ring)
    rows = pieces[0].shape[0]
    pairs = width // blocks // (2 * HD)
    heads_w = many * width // blocks

    def query_at(j):
        return (0, j // pairs * (2 * pairs) + j % pairs)

    def out_at(j):
        return (0, j // pairs * (2 * pairs) + pairs + j % pairs)

    total = blocks * tokens
    flops = 2 * tokens * heads_w * (2 * width + 2 * total)
    return pl.pallas_call(
        lambda *refs: attend_kernel(count, blocks, refs),
        out_shape=(
            jax.ShapeDtypeStruct((tokens, heads_w), BF16),
            jax.ShapeDtypeStruct((tokens, heads_w), BF16),
            jax.ShapeDtypeStruct((many * pairs, 1, 2 * tokens), F32),
            jax.ShapeDtypeStruct((tokens, width), F32),
        ),
        grid=(many * pairs,),
        in_specs=[whole(normed), whole(bias), whole(acc)]
        + [whole(kv) for kv in kv_ring]
        + [pl.BlockSpec((rows, 2 * HD), query_at)] * count
        + [pl.BlockSpec((rows, 2 * HD), out_at)] * count,
        out_specs=(
            pl.BlockSpec((tokens, 2 * HD), lambda j: (0, j)),
            pl.BlockSpec((tokens, 2 * HD), lambda j: (0, j)),
            pl.BlockSpec((1, 1, 2 * tokens), lambda j: (j, 0, 0)),
            pl.BlockSpec((tokens, width), lambda j: (0, 0)),
        ),
        scratch_shapes=[pltpu.VMEM((blocks, tokens, 2 * tokens), F32)],
        cost_estimate=pl.CostEstimate(
            flops=flops, transcendentals=tokens * total * heads_w // HD, bytes_accessed=14_000_000
        ),
        compiler_params=params(),
        name="attend",
    )(normed, bias, acc, *kv_ring, *pieces, *pieces)


def attend_back_kernel(count, blocks, first, refs):
    branch_ref, bias_ref = refs[:2]
    refs = refs[2:]
    if not first:
        kv_in_ref, normed_in_ref = refs[:2]
        refs = refs[2:]
    query_ref, mixed_ref, total_ref = refs[:3]
    refs = refs[3:]
    kv_refs, refs = refs[:blocks], refs[blocks:]
    wq_refs, refs = refs[:count], refs[count:]
    wo_refs, refs = refs[:count], refs[count:]
    query_grad_ref, kv_grad_ref, normed_grad_ref = refs
    rows = wq_refs[0].shape[0]
    tokens = branch_ref.shape[0]
    scale = HD ** (-0.5)

    @pl.when(pl.program_id(0) == 0)
    def _():
        if first:
            kv_grad_ref[...] = jnp.zeros_like(kv_grad_ref)
            normed_grad_ref[...] = jnp.zeros_like(normed_grad_ref)
        else:
            kv_grad_ref[...] = kv_in_ref[...]
            normed_grad_ref[...] = normed_in_ref[...]

    grad = sum(
        nn(branch_ref[:, i * rows : (i + 1) * rows], wo_refs[i][...]) for i in range(count)
    ).astype(BF16)
    product = pair_up(grad.astype(F32) * mixed_ref[...].astype(F32))
    inner = jnp.sum(product.T, axis=0, keepdims=True)
    grad = pair_up(grad)
    query = pair_up(query_ref[...])
    totals = total_ref[0]
    query_grad = 0.0
    for b in range(blocks):
        keys, values = kv_refs[b][:, :HD], kv_refs[b][:, HD:]
        bias = bias_ref[b * tokens : (b + 1) * tokens, :]
        scores = nt(keys, query) * (scale * LOG2E) + jnp.concatenate([bias, bias], axis=1)
        shares = jnp.exp2(scores - totals)
        score_grad = (shares * (nt(values, grad) - inner)).astype(BF16)
        query_grad = query_grad + tn(keys, score_grad)
        at = slice(b * tokens, (b + 1) * tokens)
        kv_grad_ref[at, :HD] += scale * nn(score_grad, query)
        kv_grad_ref[at, HD:] += nn(shares.astype(BF16), grad)
    query_grad = pair_off((scale * query_grad).T.astype(BF16))
    query_grad_ref[...] = query_grad
    for i in range(count):
        normed_grad_ref[:, i * rows : (i + 1) * rows] += nt(query_grad, wq_refs[i][...])


def attend_back_block(branch, bias, sums, query, mixed, total, kv_ring, pieces, at):
    tokens, width = branch.shape
    first = sums is None
    count, blocks = len(pieces), len(kv_ring)
    rows = pieces[0].shape[0]
    heads_w = width // blocks
    pairs = heads_w // (2 * HD)
    base = 2 * pairs * at
    two = pl.BlockSpec((tokens, 2 * HD), lambda j: (0, j))
    kept = pl.BlockSpec((tokens, 2 * HD), lambda j: (0, pairs * at + j))
    sums = [] if first else list(sums)
    keys = blocks * tokens
    return pl.pallas_call(
        lambda *refs: attend_back_kernel(count, blocks, first, refs),
        out_shape=(
            jax.ShapeDtypeStruct((tokens, heads_w), BF16),
            jax.ShapeDtypeStruct((keys, 2 * HD), F32),
            jax.ShapeDtypeStruct((tokens, width), F32),
        ),
        grid=(pairs,),
        in_specs=[whole(branch), whole(bias)]
        + [whole(item) for item in sums]
        + [kept, kept, pl.BlockSpec((1, 1, 2 * tokens), lambda j: (pairs * at + j, 0, 0))]
        + [whole(kv) for kv in kv_ring]
        + [pl.BlockSpec((rows, 2 * HD), lambda j: (0, base + j))] * count
        + [pl.BlockSpec((rows, 2 * HD), lambda j: (0, base + pairs + j))] * count,
        out_specs=(
            two,
            pl.BlockSpec((keys, 2 * HD), lambda j: (0, 0)),
            pl.BlockSpec((tokens, width), lambda j: (0, 0)),
        ),
        cost_estimate=pl.CostEstimate(
            flops=2 * tokens * heads_w * (2 * width + 5 * keys),
            transcendentals=tokens * keys * heads_w // HD,
            bytes_accessed=16_000_000,
        ),
        compiler_params=params(),
        name="attend_back",
    )(branch, bias, *sums, query, mixed, total, *kv_ring, *pieces, *pieces)


def attend_weights_kernel(sends, keeps, refs):
    outs = refs[len(refs) - sends - keeps :]

    def work(normed_ref, branch_ref, query_grad_ref, mixed_ref, out_ref, come_ref):
        half = query_grad_ref.shape[1]
        left = nn(normed_ref[...], query_grad_ref[...])
        right = nn(branch_ref[...], mixed_ref[...])
        if come_ref is not None:
            come = come_ref[...].astype(F32)
            left, right = left + come[:, :half], right + come[:, half:]
        out_ref[:, :half] = left.astype(BF16)
        out_ref[:, half:] = right.astype(BF16)

    if sends:
        work(*refs[:4], outs[0], None)
    if keeps:
        refs = refs[4 * sends :]
        work(*refs[:4], outs[-1], refs[4])


def attend_weights(normed, branch, send=None, keep=None):
    width, tokens = normed.shape
    steps = 4
    rows = width // 2 // steps
    specs, arrays, out_shape = [], [], []
    for item, first in ((send, steps), (keep, 0)):
        if item is None:
            continue
        query_grad, mixed, at, *come = item
        heads_w = query_grad.shape[1]
        left = pl.BlockSpec((rows, tokens), lambda i, first=first: (first + i, 0))
        right = pl.BlockSpec(
            (tokens, heads_w), lambda i, at=at: (0, at), pipeline_mode=pl.Buffered(1)
        )
        out = pl.BlockSpec((rows, 2 * heads_w), lambda i: (i, 0))
        specs += [left, left, whole(query_grad), right] + [out] * len(come)
        arrays += [normed, branch, query_grad, mixed, *come]
        out_shape.append(jax.ShapeDtypeStruct((width // 2, 2 * heads_w), BF16))
    return pl.pallas_call(
        lambda *refs: attend_weights_kernel(int(send is not None), int(keep is not None), refs),
        out_shape=out_shape,
        grid=(steps,),
        in_specs=specs,
        out_specs=[out] * len(out_shape),
        cost_estimate=pl.CostEstimate(
            flops=2 * tokens * width * heads_w * len(out_shape),
            transcendentals=0,
            bytes_accessed=6_000_000,
        ),
        compiler_params=params(),
        name="attend_weights",
    )(*arrays)


def ffn_kernel(count, steps, last, refs):
    normed_ref, grad_ref = refs[:2]
    w_refs = refs[2 : 2 + count]
    act_ref, part_ref, back_ref, part_acc, back_acc = refs[2 + count :]
    rows = w_refs[0].shape[0]
    step = pl.program_id(0)

    @pl.when(step == 0)
    def _():
        part_acc[...] = jnp.zeros_like(part_acc)
        back_acc[...] = jnp.zeros_like(back_acc)

    def work(tile):
        parts = [slice(i * rows, (i + 1) * rows) for i in range(count)]
        gate = sum(nn(normed_ref[:, p], w[:, :tile]) for p, w in zip(parts, w_refs))
        upward = sum(nn(normed_ref[:, p], w[:, tile : 2 * tile]) for p, w in zip(parts, w_refs))
        hidden_grad = sum(
            nn(grad_ref[:, p], w[:, 2 * tile : 3 * tile]) for p, w in zip(parts, w_refs)
        )
        sigma = jax.nn.sigmoid(gate)
        silu = gate * sigma
        hidden = (silu * upward).astype(BF16)
        up_grad = (hidden_grad * silu).astype(BF16)
        gate_grad = (hidden_grad * upward * sigma * (1.0 + gate * (1.0 - sigma))).astype(BF16)
        act_ref[:, :tile] = gate_grad
        act_ref[:, tile : 2 * tile] = up_grad
        act_ref[:, 2 * tile : 3 * tile] = hidden
        both = jnp.concatenate([gate_grad, up_grad], axis=1)
        for p, w in zip(parts, w_refs):
            part_acc[:, p] += nt(hidden, w[:, 2 * tile : 3 * tile])
            back_acc[:, p] += nt(both, w[:, : 2 * tile])

    if steps > 1:
        pl.when(step < steps - 1)(lambda: work(TILE))
    pl.when(step == steps - 1)(lambda: work(last))

    @pl.when(step == steps - 1)
    def _():
        part_ref[...] = part_acc[...].astype(BF16)
        back_ref[...] = back_acc[...].astype(BF16)


def ffn_block(normed, grad, pieces):
    tokens, width = normed.shape
    count, rows = len(pieces), pieces[0].shape[0]
    units = pieces[0].shape[1] // 3
    steps = -(-units // TILE)
    last = units - (steps - 1) * TILE
    full = pl.BlockSpec((tokens, width), lambda j: (0, 0))
    out = jax.ShapeDtypeStruct((tokens, width), BF16)
    return pl.pallas_call(
        lambda *refs: ffn_kernel(count, steps, last, refs),
        out_shape=(jax.ShapeDtypeStruct((tokens, 3 * units), BF16), out, out),
        grid=(steps,),
        in_specs=[whole(normed), whole(grad)]
        + [pl.BlockSpec((rows, 3 * TILE), lambda j: (0, j))] * count,
        out_specs=(pl.BlockSpec((tokens, 3 * TILE), lambda j: (0, j)), full, full),
        scratch_shapes=[pltpu.VMEM((tokens, width), F32)] * 2,
        cost_estimate=pl.CostEstimate(
            flops=12 * tokens * width * units,
            transcendentals=tokens * units,
            bytes_accessed=6 * width * units + 12 * tokens * width,
        ),
        compiler_params=params(),
        name="ffn_block",
    )(normed, grad, *pieces)


def ffn_weights_kernel(blocks, count, steps, last, adds, refs):
    normed_refs, refs = refs[:blocks], refs[blocks:]
    grad_refs, refs = refs[:blocks], refs[blocks:]
    act_refs, refs = refs[:blocks], refs[blocks:]
    added_refs, out_refs = refs[: adds * count], refs[adds * count :]

    def work(piece, tile):
        both = sum(tn(normed_refs[b][...], act_refs[b][:, : 2 * tile]) for b in range(blocks))
        down = sum(
            tn(grad_refs[b][...], act_refs[b][:, 2 * tile : 3 * tile]) for b in range(blocks)
        )
        for k in range(adds):
            added = added_refs[k * count + piece]
            both = both + added[:, : 2 * tile].astype(F32)
            down = down + added[:, 2 * tile : 3 * tile].astype(F32)
        out_refs[piece][:, : 2 * tile] = both.astype(BF16)
        out_refs[piece][:, 2 * tile : 3 * tile] = down.astype(BF16)

    turn, step = pl.program_id(0), pl.program_id(1)
    for at in range(count):
        if steps > 1:
            pl.when((turn == at) & (step < steps - 1))(functools.partial(work, at, TILE))
        pl.when((turn == at) & (step == steps - 1))(functools.partial(work, at, last))


def ffn_weights(normed_ring, grad_ring, acts, first, count, rows, added=()):
    tokens = normed_ring[0].shape[0]
    units = acts[0].shape[1] // 3
    blocks = len(acts)
    steps = -(-units // TILE)
    last = units - (steps - 1) * TILE
    left = pl.BlockSpec((tokens, rows), lambda i, j: (0, first + i))

    def piece_spec(piece, block):
        def place(i, j):
            return (block, jnp.where(i < piece, 0, jnp.where(i > piece, steps - 1, j)))

        return pl.BlockSpec((rows, 3 * TILE), place)

    wide = [piece_spec(piece, 0) for piece in range(count)]
    specs, arrays = [], []
    for item in added:
        if isinstance(item, (list, tuple)):
            specs, arrays = specs + wide, arrays + list(item)
        else:
            specs = specs + [piece_spec(piece, piece) for piece in range(count)]
            arrays = arrays + [item] * count
    return pl.pallas_call(
        lambda *refs: ffn_weights_kernel(blocks, count, steps, last, len(added), refs),
        out_shape=[jax.ShapeDtypeStruct((rows, 3 * units), BF16)] * count,
        grid=(count, steps),
        in_specs=[left] * (2 * blocks)
        + [pl.BlockSpec((tokens, 3 * TILE), lambda i, j: (0, j))] * blocks
        + specs,
        out_specs=wide,
        cost_estimate=pl.CostEstimate(
            flops=6 * tokens * blocks * count * rows * units,
            transcendentals=0,
            bytes_accessed=6 * tokens * blocks * units * count + 6 * count * rows * units,
        ),
        compiler_params=params(2),
        name="ffn_weights",
    )(*normed_ring, *grad_ring, *acts, *arrays)


def turn_kernel(come_ref, part_ref, given_ref, value_ref, gain_ref, *refs):
    after_ref, low_ref, turned_ref, term_ref = refs
    value = value_ref[...]
    grad = come_ref[...].astype(F32) + part_ref[...].astype(F32)
    scale = lax.rsqrt(jnp.mean(value * value, axis=-1, keepdims=True) + norm_eps)
    term_ref[...] = jnp.sum(grad * value * scale, axis=0, keepdims=True)
    after = given_ref[...].astype(F32) + norm_back(value, scale, gain_ref[1:2, :], grad)
    after_ref[...] = after
    low = after.astype(BF16)
    low_ref[...] = low
    turned_ref[...] = low.T


def turn(come, part, given, value, gains):
    own, width = value.shape
    return pl.pallas_call(
        turn_kernel,
        out_shape=(
            jax.ShapeDtypeStruct((own, width), F32),
            jax.ShapeDtypeStruct((own, width), BF16),
            jax.ShapeDtypeStruct((width, own), BF16),
            jax.ShapeDtypeStruct((1, width), F32),
        ),
        cost_estimate=pl.CostEstimate(
            flops=0, transcendentals=0, bytes_accessed=20 * own * width
        ),
        compiler_params=params(0),
        name="turn",
    )(come, part, given, value, gains)


def plain_turn(come, part, given, value, gains):
    grad = come.astype(F32) + part.astype(F32)
    scale = lax.rsqrt(jnp.mean(value * value, axis=-1, keepdims=True) + norm_eps)
    term = jnp.sum(grad * value * scale, axis=0, keepdims=True)
    after = given.astype(F32) + norm_back(value, scale, gains[1:2], grad)
    low = after.astype(BF16)
    return after, low, low.T, term


def leave_kernel(come_count, count, slices, table_ref, *refs):
    kv_ref, refs = refs[0], refs[1:]
    come_refs, refs = refs[:come_count], refs[come_count:]
    d_key_ref, d_value_ref, grad_ref, normed_ref, low_ref, after_ref, gain_ref, ffn_ref = refs[:8]
    refs = refs[8:]
    key_refs, value_refs, refs = refs[:count], refs[count : 2 * count], refs[2 * count :]
    out_ref, keep_ref, send_ref, total_ref = refs
    rows = key_refs[0].shape[0]
    width = low_ref.shape[1]
    size = width // slices
    kv_grad = kv_ref[...]
    for ref in come_refs:
        kv_grad = kv_grad + ref[...].astype(F32)
    given = jnp.concatenate([d_key_ref[...], d_value_ref[...]], axis=1)
    kv_grad = (kv_grad + given.astype(F32)).astype(BF16)
    squares, inner = 0.0, 0.0
    for i in range(count):
        part = slice(i * rows, (i + 1) * rows)
        weights = jnp.concatenate([key_refs[i][...], value_refs[i][...]], axis=1)
        total = grad_ref[:, part] + nt(kv_grad, weights)
        total_ref[:, part] = total
        value = low_ref[:, part].astype(F32)
        squares = squares + jnp.sum(value * value, axis=-1, keepdims=True)
        inner = inner + jnp.sum(total * gain_ref[0:1, part] * value, axis=-1, keepdims=True)
    scale = lax.rsqrt(squares / width + norm_eps)
    shrink = scale * scale * scale * (inner / width)
    for i in range(count):
        part = slice(i * rows, (i + 1) * rows)
        total, value = total_ref[:, part], low_ref[:, part].astype(F32)
        gain_term = jnp.sum(total * value * scale, axis=0, keepdims=True)
        terms = jnp.concatenate(
            [gain_term, ffn_ref[:, part], jnp.zeros((HD - 2, rows), F32)], axis=0
        )
        block = jnp.concatenate([tn(normed_ref[:, part], kv_grad), terms.T], axis=1).astype(BF16)
        half = count // 2
        ref = keep_ref if i < half else send_ref
        ref[(i % half) * rows : (i % half + 1) * rows, :] = block
    for k in range(slices):
        part = slice(k * size, (k + 1) * size)
        value = low_ref[:, part].astype(F32)
        grad = scale * (total_ref[:, part] * gain_ref[0:1, part]) - value * shrink
        start = pl.multiple_of(table_ref[k] * size, size)
        out_ref[:, pl.ds(start, size)] = after_ref[:, part] + grad


def leave(table, kv_acc, kv_come, d_keys, d_values, normed_grad, normed, low, after_grad, gains,
          ffn_term, near, at):
    own, width = normed.shape
    count, rows = len(near), near[0].shape[0]

    def columns(place):
        return [pl.BlockSpec((rows, HD), lambda i, table_ref: (0, at // HD + place))] * count

    def full(shape):
        return pl.BlockSpec(shape, lambda i, table_ref: (0, 0))

    given = [*kv_come, d_keys, d_values, normed_grad, normed, low, after_grad, gains, ffn_term]
    half = jax.ShapeDtypeStruct((width // 2, 3 * HD), BF16)
    return pl.pallas_call(
        functools.partial(leave_kernel, len(kv_come), count, len(table)),
        out_shape=(jax.ShapeDtypeStruct((own, width), F32), half, half),
        grid_spec=pltpu.PrefetchScalarGridSpec(
            num_scalar_prefetch=1,
            grid=(1,),
            in_specs=[full((own, 2 * HD))]
            + [full(item.shape) for item in given]
            + columns(0)
            + columns(1),
            out_specs=[full((own, width)), full(half.shape), full(half.shape)],
            scratch_shapes=[pltpu.VMEM((own, width), F32)],
        ),
        cost_estimate=pl.CostEstimate(
            flops=8 * own * width * HD, transcendentals=0, bytes_accessed=16_000_000
        ),
        compiler_params=params(),
        name="leave",
    )(jnp.stack(table).astype(jnp.int32), kv_acc, *given, *near, *near)


def leave_out_kernel(slices, table_ref, after_ref, come_ref, part_ref, out_ref):
    size = after_ref.shape[1] // slices
    for k in range(slices):
        part = slice(k * size, (k + 1) * size)
        total = come_ref[:, part].astype(F32) + part_ref[:, part].astype(F32)
        start = pl.multiple_of(table_ref[k] * size, size)
        out_ref[:, pl.ds(start, size)] = (after_ref[:, part] + total).astype(BF16)


def leave_out(table, after_attn, come, part):
    def full(shape):
        return pl.BlockSpec(shape, lambda i, table_ref: (0, 0))

    return pl.pallas_call(
        functools.partial(leave_out_kernel, len(table)),
        out_shape=jax.ShapeDtypeStruct(after_attn.shape, BF16),
        grid_spec=pltpu.PrefetchScalarGridSpec(
            num_scalar_prefetch=1,
            grid=(1,),
            in_specs=[full(after_attn.shape)] * 3,
            out_specs=full(after_attn.shape),
        ),
        cost_estimate=pl.CostEstimate(flops=0, transcendentals=0, bytes_accessed=8_000_000),
        compiler_params=params(),
        name="leave_out",
    )(jnp.stack(table).astype(jnp.int32), after_attn, come, part)


def unpack_ffn_kernel(keep_ref, come_ref, gate_ref, up_ref, down_ref):
    units = gate_ref.shape[1]
    for at in range(0, units, TILE):
        size = min(TILE, units - at)

        def take(k):
            cols = slice(3 * at + k * size, 3 * at + (k + 1) * size)
            return keep_ref[:, cols].astype(F32) + come_ref[:, cols].astype(F32)

        gate_ref[:, at : at + size] = take(0)
        up_ref[:, at : at + size] = take(1)
        down_ref[at : at + size, :] = take(2).T


def unpack_ffn(keep, come):
    rows, units = keep.shape[0], keep.shape[1] // 3
    flat = jax.ShapeDtypeStruct((rows, units), F32)
    return pl.pallas_call(
        unpack_ffn_kernel,
        out_shape=(flat, flat, jax.ShapeDtypeStruct((units, rows), F32)),
        cost_estimate=pl.CostEstimate(flops=0, transcendentals=0, bytes_accessed=24 * rows * units),
        compiler_params=params(0),
        name="unpack_ffn",
    )(keep, come)


def unpack_attn_kernel(moving_ref, keep_ref, come_ref, query_ref, out_ref):
    heads_w = query_ref.shape[1]
    total = keep_ref[...].astype(F32) + come_ref[...].astype(F32) + moving_ref[...].astype(F32)
    query_ref[...] = total[:, :heads_w]
    out_ref[...] = total[:, heads_w:].T


def unpack_attn(moving, keep, come):
    rows, heads_w = keep.shape[0], keep.shape[1] // 2
    return pl.pallas_call(
        unpack_attn_kernel,
        out_shape=(
            jax.ShapeDtypeStruct((rows, heads_w), F32),
            jax.ShapeDtypeStruct((heads_w, rows), F32),
        ),
        cost_estimate=pl.CostEstimate(flops=0, transcendentals=0, bytes_accessed=4_000_000),
        compiler_params=params(0),
        name="unpack_attn",
    )(moving, keep, come)


def place_kv_kernel(count, place_ref, *refs):
    kv_refs, (key_ref, value_ref) = refs[:count], refs[count:]
    own = kv_refs[0].shape[0]
    for r in range(count):
        start = pl.multiple_of(place_ref[r] * own, own)
        key_ref[pl.ds(start, own), :] = kv_refs[r][:, :HD]
        value_ref[pl.ds(start, own), :] = kv_refs[r][:, HD:]


def place_kv(places, kv_ring):
    own, count = kv_ring[0].shape[0], len(kv_ring)
    out = jax.ShapeDtypeStruct((count * own, HD), BF16)
    return pl.pallas_call(
        functools.partial(place_kv_kernel, count),
        out_shape=(out, out),
        grid_spec=pltpu.PrefetchScalarGridSpec(
            num_scalar_prefetch=1,
            grid=(1,),
            in_specs=[pl.BlockSpec((own, 2 * HD), lambda i, place_ref: (0, 0))] * count,
            out_specs=[pl.BlockSpec(out.shape, lambda i, place_ref: (0, 0))] * 2,
        ),
        cost_estimate=pl.CostEstimate(flops=0, transcendentals=0, bytes_accessed=1_600_000),
        compiler_params=params(),
        name="place_kv",
    )(jnp.stack(places).astype(jnp.int32), *kv_ring)


def plain_attend_block(normed, bias, acc, kv_ring, pieces, many):
    step = normed.shape[1] // len(kv_ring)
    heads_w = many * step
    weights = stack_rows(pieces)
    blocks = [weights[:, at * step : (at + 1) * step] for at in range(2 * many)]
    weights = jnp.concatenate(blocks[::2] + blocks[1::2], axis=1)
    kv = stack_rows(kv_ring)
    query = nn(normed, weights[:, :heads_w]).astype(BF16)
    mixed, totals = [], []
    for head in range(heads_w // HD):
        scores = nt(kv[:, :HD], query[:, head * HD : (head + 1) * HD]) * (HD ** (-0.5)) + bias
        peak = jnp.max(scores, axis=0, keepdims=True)
        raised = jnp.exp(scores - peak)
        sums = jnp.sum(raised, axis=0, keepdims=True)
        mixed.append(tn((raised / sums).astype(BF16), kv[:, HD:]).astype(BF16))
        totals.append(peak + jnp.log(sums))
    mixed = jnp.concatenate(mixed, axis=1)
    return query, mixed, jnp.concatenate(totals, axis=0), acc + nt(mixed, weights[:, heads_w:])


def plain_attend_back_block(branch, bias, sums, query, mixed, total, kv_ring, pieces, at):
    heads_w = branch.shape[1] // len(kv_ring)
    weights = stack_rows(pieces)[:, 2 * at * heads_w : 2 * (at + 1) * heads_w]
    query = query[:, at * heads_w : (at + 1) * heads_w]
    total = total[at * heads_w // HD : (at + 1) * heads_w // HD]
    kv = stack_rows(kv_ring)
    keys, values = kv[:, :HD], kv[:, HD:]
    scale = HD ** (-0.5)
    grad = nn(branch, weights[:, heads_w:]).astype(BF16)
    key_acc, value_acc, query_grad = 0.0, 0.0, []
    for head in range(heads_w // HD):
        cols = slice(head * HD, (head + 1) * HD)
        scores = nt(keys, query[:, cols]) * scale + bias
        shares = jnp.exp(scores - total[head : head + 1])
        share_grad = nt(values, grad[:, cols])
        value_acc = value_acc + nn(shares.astype(BF16), grad[:, cols])
        inner = jnp.sum(shares * share_grad, axis=0, keepdims=True)
        score_grad = (shares * (share_grad - inner)).astype(BF16)
        query_grad.append((scale * tn(score_grad, keys)).astype(BF16))
        key_acc = key_acc + scale * nn(score_grad, query[:, cols])
    query_grad = jnp.concatenate(query_grad, axis=1)
    kv_grad = jnp.concatenate([key_acc, value_acc], axis=1)
    normed_grad = nt(query_grad, weights[:, :heads_w])
    if sums is not None:
        kv_grad, normed_grad = kv_grad + sums[0], normed_grad + sums[1]
    return query_grad, kv_grad, normed_grad


def plain_attend_weights(normed, branch, send=None, keep=None):
    half = normed.shape[0] // 2
    outs = []
    for item, first in ((send, half), (keep, 0)):
        if item is None:
            continue
        query_grad, mixed, at, *come = item
        heads_w = query_grad.shape[1]
        mixed = mixed[:, at * heads_w : (at + 1) * heads_w]
        part = slice(first, first + half)
        out = jnp.concatenate([nn(normed[part], query_grad), nn(branch[part], mixed)], axis=1)
        outs.append((out + come[0].astype(F32) if come else out).astype(BF16))
    return outs


def plain_ffn_block(normed, grad, pieces):
    weights = stack_rows(pieces)
    units = weights.shape[1] // 3
    gate_w, up_w, down_w = jnp.split(weights, 3, axis=1)
    gate = nn(normed, gate_w)
    upward = nn(normed, up_w)
    sigma = jax.nn.sigmoid(gate)
    hidden = (gate * sigma * upward).astype(BF16)
    part = nt(hidden, down_w).astype(BF16)
    hidden_grad = nn(grad, down_w)
    gate_grad = (hidden_grad * upward * sigma * (1.0 + gate * (1.0 - sigma))).astype(BF16)
    up_grad = (hidden_grad * gate * sigma).astype(BF16)
    back = (nt(gate_grad, gate_w) + nt(up_grad, up_w)).astype(BF16)
    return jnp.concatenate([gate_grad, up_grad, hidden], axis=1), part, back


def plain_ffn_weights(normed_ring, grad_ring, acts, first, count, rows, added=()):
    normed, grad, acts = stack_rows(normed_ring), stack_rows(grad_ring), stack_rows(acts)
    units = acts.shape[1] // 3
    pieces = []
    for piece in range(count):
        cols = slice((first + piece) * rows, (first + piece + 1) * rows)
        out = [tn(normed[:, cols], acts[:, : 2 * units]), tn(grad[:, cols], acts[:, 2 * units :])]
        out = jnp.concatenate(out, axis=1)
        for item in added:
            single = isinstance(item, (list, tuple))
            out = out + (item[piece] if single else item[piece * rows :][:rows]).astype(F32)
        pieces.append(out.astype(BF16))
    return pieces


def plain_leave(table, kv_acc, kv_come, d_keys, d_values, normed_grad, normed, low, after_grad,
                gains, ffn_term, near, at):
    own, width = normed.shape
    kv_grad = kv_acc[:own]
    for come in kv_come:
        kv_grad = kv_grad + come.astype(F32)
    kv_grad = kv_grad + jnp.concatenate([d_keys, d_values], axis=1).astype(F32)
    kv_grad = kv_grad.astype(BF16)
    kv_w = stack_rows([piece[:, at : at + 2 * HD] for piece in near])
    normed_grad = normed_grad + nt(kv_grad, kv_w)
    value = low.astype(F32)
    scale = lax.rsqrt(jnp.mean(value * value, axis=-1, keepdims=True) + norm_eps)
    grad = after_grad + norm_back(value, scale, gains[0:1], normed_grad)
    gain_term = jnp.sum(normed_grad * value * scale, axis=0)
    small = [tn(normed, kv_grad), gain_term[:, None], ffn_term.T, jnp.zeros((width, HD - 2), F32)]
    small = jnp.concatenate(small, axis=1).astype(BF16)
    grad = move_columns(grad, table, width // len(table), back=True)
    return grad, small[: width // 2], small[width // 2 :]


def plain_leave_out(table, after_attn, come, part):
    out = (after_attn + (come.astype(F32) + part.astype(F32))).astype(BF16)
    return move_columns(out, table, out.shape[1] // len(table), back=True)


def plain_unpack_ffn(keep, come):
    gate, up, down = jnp.split(keep.astype(F32) + come.astype(F32), 3, axis=1)
    return gate, up, down.T


def plain_unpack_attn(moving, keep, come):
    total = keep.astype(F32) + come.astype(F32) + moving.astype(F32)
    heads_w = total.shape[1] // 2
    return total[:, :heads_w], total[:, heads_w:].T


def plain_place_kv(places, kv_ring):
    own = kv_ring[0].shape[0]
    out = jnp.zeros((len(kv_ring) * own, 2 * HD), BF16)
    for start, block in zip(places, kv_ring):
        out = lax.dynamic_update_slice_in_dim(out, block, start * own, axis=0)
    return out[:, :HD], out[:, HD:]


KERNELS = (
    pack_attn,
    pack_ffn,
    enter,
    attend_block,
    attend_back_block,
    attend_weights,
    ffn_block,
    ffn_weights,
    turn,
    leave,
    leave_out,
    unpack_ffn,
    unpack_attn,
    place_kv,
)
PLAIN = (
    plain_pack_attn,
    plain_pack_ffn,
    plain_enter,
    plain_attend_block,
    plain_attend_back_block,
    plain_attend_weights,
    plain_ffn_block,
    plain_ffn_weights,
    plain_turn,
    plain_leave,
    plain_leave_out,
    plain_unpack_ffn,
    plain_unpack_attn,
    plain_place_kv,
)


def on_device(
    ndp,
    nz,
    tokens,
    norm_attn,
    w_query,
    w_key,
    w_value,
    w_out,
    norm_ffn,
    w_gate,
    w_up,
    w_down,
    segment_ids,
    parents,
    positions,
    d_out,
    d_keys,
    d_values,
):
    me = lax.axis_index("dp")
    place_z = lax.axis_index("tensor")
    table = slice_table(me, ndp)
    own, width = tokens.shape[0], tokens.shape[1]
    rows = width // ndp
    heads_w = w_query.shape[1]
    units = w_gate.shape[1]
    fits = own % HD == 0 and rows % HD == 0 and units % HD == 0 and heads_w % (2 * HD) == 0
    (
        do_pack_attn,
        do_pack_ffn,
        do_enter,
        do_attend,
        do_attend_back,
        do_attend_weights,
        do_ffn,
        do_ffn_weights,
        do_turn,
        do_leave,
        do_leave_out,
        do_unpack_ffn,
        do_unpack_attn,
        do_place_kv,
    ) = KERNELS if fits else PLAIN

    gains = jnp.concatenate(
        [norm_attn[:, None], norm_ffn[:, None], jnp.zeros((rows, HD - 2), BF16)], axis=1
    )
    first_up = lookup(segment_ids, parents)
    second_up = lookup(first_up, parents)

    def own_rows(vector):
        return lax.dynamic_slice_in_dim(vector, place_z * own, own, axis=0)

    def ring_rows(vector):
        return jnp.concatenate(
            [
                lax.dynamic_slice_in_dim(vector, ((place_z - r) % nz) * own, own, axis=0)
                for r in range(nz)
            ],
            axis=0,
        )

    key_segment, key_place = ring_rows(segment_ids)[:, None], ring_rows(positions)[:, None]
    linked = (
        (key_segment == own_rows(segment_ids)[None])
        | (key_segment == own_rows(first_up)[None])
        | (key_segment == own_rows(second_up)[None])
    )
    bias = jnp.where(linked & (key_place <= own_rows(positions)[None]), 0.0, -1e30).astype(F32)

    near_item, ring_item = do_pack_attn(w_query, w_out, w_key, w_value, gains)
    near_flow = Flow("attn_w_near", gather_steps(near_item, ndp))
    attn_flow = Flow("attn_w_ring", ring_gather_steps(ring_item, nz))
    grad_low = move_columns(d_out, table, rows)
    (ring_item,) = meet([ring_item], [near_flow, attn_flow])
    near_flow.go(len(bit_orders(ndp)[0]) - 2)
    ffn_pack = do_pack_ffn(w_gate, w_up, w_down)
    grad_low, bias, ffn_pack = meet([grad_low, bias, ffn_pack], [near_flow, attn_flow])
    ffn_flow = Flow("ffn_w", gather_steps(ffn_pack, ndp))
    near = list(near_flow.finish())
    near = meet(near, [attn_flow])
    tokens_low, normed, normed_turned, kv_own, gain_rows = do_enter(
        tokens, table, near, 2 * heads_w
    )
    ffn_gain = gain_rows[1:2]
    kv_ring = [kv_own] + [scoped("kv", shift, kv_own, nz, by) for by in range(1, nz)]
    *kv_ring, grad_low = meet(kv_ring + [grad_low], [attn_flow])
    attn_ring = attn_flow.finish()[1:]
    far_flow = Flow("attn_w_far", gather_steps(jnp.concatenate(attn_ring, axis=1), ndp))
    grad_flow = Flow("grad_ring", ring_gather_steps(grad_low, nz))

    normed, *kv_ring = meet([normed] + kv_ring, [far_flow], [ffn_flow])
    *kept_near, after_attn = do_attend(normed, bias, tokens_low, kv_ring, near, 1)
    grad_first = grad_flow.held[0]
    (after_attn,) = meet([after_attn], [grad_flow])
    (after_attn,) = meet([after_attn], [far_flow, ffn_flow])
    far = far_flow.finish()
    *kept_far, after_attn = do_attend(normed, bias, after_attn, kv_ring, far, nz - 1)
    (after_attn,) = meet([after_attn], [ffn_flow, grad_flow])
    ffn_w = ffn_flow.finish()
    grad_ring = [grad_low, grad_first]
    ffn_scale = lax.rsqrt(jnp.mean(after_attn * after_attn, axis=-1, keepdims=True) + norm_eps)
    ffn_own = (after_attn * ffn_scale * ffn_gain).astype(BF16)

    ring_flow = Flow("ffn_ring", ring_gather_steps(ffn_own, nz))
    ffn_ring, acts, parts, backs = [ffn_own], [], [], []
    early = nz // 2 + 1
    backs_flow = None
    for block in range(nz):
        if block > 0:
            come, acts[-1], *ring_flow.held = tie(ring_flow.held[0], acts[-1])
            ring_flow.held = [come]
            ring_flow.go()
            ffn_ring.append(come)
            if block == 2:
                (ffn_ring[-1],) = meet(ffn_ring[-1:], [], [grad_flow])
                grad_ring = grad_flow.finish()
        if block == early:
            first = (ffn_ring[:early], grad_ring[:early], acts[:early])
            (send,) = do_ffn_weights(*first, 1, 1, width // 2)
            kept = do_ffn_weights(*first, 0, 2, width // 4)
            (send,) = meet([send], [backs_flow] if block > 2 else [])
            ffn_ring[-1], send, *kept = tie(ffn_ring[-1], send, *kept)
        elif block > 2:
            (ffn_ring[-1],) = meet(ffn_ring[-1:], [backs_flow])
        act, part, back = do_ffn(ffn_ring[block], grad_ring[block], ffn_w)
        acts.append(act)
        parts.append(part)
        backs.append(back)
        if block == 1:
            backs_flow = Flow("backs", ring_steps(backs, nz))

    (acts[-1],) = meet([acts[-1]], [backs_flow])
    rest = (ffn_ring[early:], grad_ring[early:], acts[early:])
    (send,) = do_ffn_weights(*rest, 1, 1, width // 2, ([send],))
    come = scoped("ffn_g", core_swap, send, ndp)
    made = do_ffn_weights(*rest, 0, 2, width // 4, (kept, come))
    parts[1], *made = meet([parts[1], *made], [backs_flow])
    after_grad, branch, branch_turned, ffn_term = do_turn(
        *backs_flow.finish(), grad_low, after_attn, gain_rows
    )
    part_flow = Flow("parts", ring_steps(parts, nz))
    ffn_flow = Flow("ffn_g", chip_steps(*made, ndp))

    order = list(range(1, nz)) + [0]
    flows = [None] * nz
    sums = None
    for turn, block in enumerate(order):
        stored, pieces, at = (kept_far, far, block - 1) if block else (kept_near, near, 0)
        if turn > 0:
            branch, *made = meet([branch, *made], [part_flow] + [ffn_flow] * (turn == 1))
            sent = scoped(f"attn_g_{order[turn - 1]}", core_swap, made[0], ndp)
            if turn > 1:
                flow = Flow(f"attn_g_{order[turn - 2]}", chip_steps(*made[1:], ndp))
                flows[order[turn - 2]] = flow
        query_grad, kv_acc, normed_grad = do_attend_back(
            branch, bias, sums, *stored, kv_ring, pieces, at
        )
        sums = (kv_acc, normed_grad)
        due = [flow for flow in flows if flow is not None]
        if turn == 1:
            due.append(ffn_flow)
        if turn == nz - 1:
            due.remove(flow)
        this = (query_grad, stored[1], at)
        if turn == 0:
            made = do_attend_weights(normed_turned, branch_turned, this)
        else:
            query_grad, sent = meet([query_grad, sent], due)
            this = (query_grad, stored[1], at)
            made, both = do_attend_weights(normed_turned, branch_turned, this, (*back, sent))
            made = [made, both[: width // 4], both[width // 4 :]]
        back = this
    kv_low = kv_acc.astype(BF16)
    kv_come = [
        scoped("kv_g", shift, kv_low[by * own : (by + 1) * own], nz, -by) for by in range(1, nz)
    ]
    done = [None] * nz
    for place in range(1, nz - 2):
        done[place] = add_low(*flows[place].finish())
    ring_flow = Flow("attn_g_ring", ring_steps(done, nz))
    for _ in range(nz - 4):
        ring_flow.go()
    tied = meet([*made, *kv_come], [flows[nz - 2], part_flow], [ring_flow])
    (send, *made), kv_come = tied[:3], tied[3:]
    sent = scoped("attn_g_0", core_swap, send, ndp)
    flows[nz - 1] = Flow(f"attn_g_{nz - 1}", chip_steps(*made, ndp))
    input_grad, keep, send = do_leave(
        table,
        kv_acc,
        kv_come,
        d_keys,
        d_values,
        normed_grad,
        normed,
        tokens_low,
        after_grad,
        gain_rows,
        ffn_term,
        near,
        2 * heads_w,
    )
    keep, send, sent = meet([keep, send, sent], [flows[nz - 2], flows[nz - 1]])
    done[nz - 2] = add_low(*flows[nz - 2].finish())
    small_flow = Flow("small_g", scatter_steps(keep, send, ndp))
    (done[nz - 2],) = meet([done[nz - 2]], [ring_flow])
    (both,) = do_attend_weights(normed_turned, branch_turned, None, (*back, sent))
    flows[0] = Flow("attn_g_0", chip_steps(both[: width // 4], both[width // 4 :], ndp))

    meet([], [small_flow, flows[0], flows[nz - 1]])
    done[nz - 1] = add_low(*flows[nz - 1].finish())
    meet([], [ring_flow])
    meet([], [small_flow, flows[0]])
    done[0] = flows[0].finish()
    small_sum = add_low(*small_flow.finish())
    total = small_sum.astype(F32)
    for by in range(1, nz):
        total = total + scoped("small_g_ring", shift, small_sum, nz, by).astype(F32)
    moving, _ = ring_flow.finish()
    query_w_grad, out_w_grad = do_unpack_attn(moving, *done[0])
    gate_grad, up_grad, down_grad = do_unpack_ffn(*ffn_flow.finish())
    keys, values = do_place_kv([(place_z - r) % nz for r in range(nz)], kv_ring)
    return (
        do_leave_out(table, after_attn, *part_flow.finish()),
        keys,
        values,
        input_grad,
        total[:, 2 * HD],
        query_w_grad,
        total[:, :HD],
        total[:, HD : 2 * HD],
        out_w_grad,
        total[:, 2 * HD + 1],
        gate_grad,
        up_grad,
        down_grad,
    )


def solution(mesh):
    in_specs = (
        P(("dp", "tensor"), None),
        P("dp"),
        P("dp", "tensor"),
        P("dp", None),
        P("dp", None),
        P("tensor", "dp"),
        P("dp"),
        P("dp", "tensor"),
        P("dp", "tensor"),
        P("tensor", "dp"),
        P("dp"),
        P(),
        P("dp"),
        P(("dp", "tensor"), None),
        P(("dp", "tensor"), None),
        P(("dp", "tensor"), None),
    )
    out_specs = (
        P(("dp", "tensor"), None),
        P("dp", None),
        P("dp", None),
        P(("dp", "tensor"), None),
        P("dp"),
        P("dp", "tensor"),
        P("dp", None),
        P("dp", None),
        P("tensor", "dp"),
        P("dp"),
        P("dp", "tensor"),
        P("dp", "tensor"),
        P("tensor", "dp"),
    )
    body = functools.partial(on_device, mesh.shape["dp"], mesh.shape["tensor"])
    return jax.shard_map(
        body, mesh=mesh, in_specs=in_specs, out_specs=out_specs, check_vma=False
    )
```

```python
import functools

import jax
import jax.numpy as jnp
from jax import lax
from jax.experimental import pallas as pl
from jax.experimental.pallas import tpu as pltpu
from jax.sharding import PartitionSpec as P

HD = 128
norm_eps = 1e-05
F32 = jnp.float32
BF16 = jnp.bfloat16


def dot(left, right, dims):
    return lax.dot_general(left, right, ((dims[0], dims[1]), ((), ())), preferred_element_type=F32)


def nn(left, right):
    return dot(left, right, ((1,), (0,)))


def nt(left, right):
    return dot(left, right, ((1,), (1,)))


def tn(left, right):
    return dot(left, right, ((0,), (0,)))


def lookup(ids, table):
    hits = ids[:, None] == jnp.arange(table.shape[0], dtype=jnp.int32)[None, :]
    return jnp.sum(jnp.where(hits, table[None, :], 0), axis=1)


def norm_back(value, scale, gain, grad):
    weighted = grad * gain
    return scale * weighted - value * (scale * scale * scale) * jnp.mean(
        weighted * value, axis=-1, keepdims=True
    )


def bit_orders(ndp):
    bits = []
    bit = 2
    while bit < ndp:
        bits.append(bit)
        bit *= 2
    return bits, bits[::-1]


def plane_swap(array, ndp, step):
    orders = bit_orders(ndp)
    return lax.ppermute(array, "dp", [(d, d ^ orders[d & 1][step]) for d in range(ndp)])


def core_swap(array, ndp):
    return lax.ppermute(array, "dp", [(d, d ^ 1) for d in range(ndp)])


def slice_table(me, ndp):
    orders = bit_orders(ndp)
    count = len(orders[0])
    table = []
    for place in range(ndp):
        base = me ^ (place // (ndp // 2))
        even = base % 2 == 0
        owner = base
        for step in range(count):
            if (place >> step) & 1:
                owner = owner ^ jnp.where(even, orders[0][step], orders[1][step])
        table.append(owner)
    return table


def gather_steps(shard, ndp, settle=False):
    moved = yield [plane_swap(shard, ndp, 0)]
    pieces = [jnp.concatenate([shard, moved[0]], axis=0)]
    if settle:
        pieces = yield pieces
    for step in range(1, len(bit_orders(ndp)[0])):
        pieces = pieces + (yield [plane_swap(piece, ndp, step) for piece in pieces])
    pieces = pieces + (yield [core_swap(piece, ndp) for piece in pieces])
    yield tuple(pieces)


def ring_gather_steps(block, nt_):
    blocks = [block]
    for _ in range(nt_ - 1):
        blocks += yield [ring_next(blocks[-1], nt_)]
    yield tuple(blocks)


def add_low(left, right):
    return (left.astype(F32) + right.astype(F32)).astype(BF16)


def scatter_steps(keep, send, ndp):
    (come,) = yield [core_swap(send, ndp)]
    rows = keep.shape[0] // 2
    low, high = add_low(keep[:rows], come[:rows]), add_low(keep[rows:], come[rows:])
    yield from chip_steps(low, high, ndp)


def chip_steps(low, high, ndp):
    for step in range(len(bit_orders(ndp)[0]) - 1, 0, -1):
        (come,) = yield [plane_swap(high, ndp, step)]
        rows = low.shape[0] // 2
        low, high = add_low(low[:rows], come[:rows]), add_low(low[rows:], come[rows:])
    (come,) = yield [plane_swap(high, ndp, 0)]
    yield (low, come)


def ring_steps(parts, nt_, ahead=None):
    moving = yield [ring_next(parts[1], nt_)]
    for place in range(2, nt_):
        total = add_low(moving[0], parts[place])
        if ahead:
            total, ahead[-1] = tie(total, ahead[-1])
        moving = yield [ring_next(total, nt_)]
    yield (moving[0], parts[0])


class Flow:
    def __init__(self, name, steps):
        self.name, self.steps = name, steps
        with jax.named_scope(name):
            self.held = next(steps)

    def moving(self):
        return isinstance(self.held, list)

    def go(self, times=1):
        for _ in range(times):
            if self.moving():
                with jax.named_scope(self.name):
                    self.held = self.steps.send(self.held)

    def finish(self):
        while self.moving():
            self.go()
        return self.held


def meet(values, flows, others=()):
    going = [flow for flow in flows if flow.moving()]
    flows = going + [flow for flow in others if flow.moving()]
    held = [item for flow in flows for item in flow.held]
    count = len(values)
    tied = list(tie(*values, *held))
    values, held = tied[:count], tied[count:]
    for flow in flows:
        flow.held, held = held[: len(flow.held)], held[len(flow.held) :]
    for flow in going:
        flow.go()
    return values


def ring_next(array, nt_):
    return lax.ppermute(array, "tensor", [(i, (i + 1) % nt_) for i in range(nt_)])


def shift(array, nt_, by):
    return lax.ppermute(array, "tensor", [(i, (i + by) % nt_) for i in range(nt_)])


def stack_rows(pieces):
    return jnp.concatenate(pieces, axis=0)


def scoped(name, function, *items):
    with jax.named_scope(name):
        return function(*items)


def tie(*values):
    return lax.optimization_barrier(values)


LOG2E = 1.4426950408889634
TILE = 512


def params(count=1):
    return pltpu.CompilerParams(
        dimension_semantics=("arbitrary",) * count, vmem_limit_bytes=58 * 1024 * 1024
    )


def whole(array):
    zeros = (0,) * array.ndim
    return pl.BlockSpec(array.shape, lambda *_: zeros, pipeline_mode=pl.Buffered(1))


def move_kernel(table_ref, in_ref, out_ref):
    out_ref[...] = in_ref[...]


def move_columns(array, table, width, back=False):
    tokens = array.shape[0]

    def far(k, table_ref):
        return (0, table_ref[k])

    def near(k, table_ref):
        return (0, k)

    return pl.pallas_call(
        move_kernel,
        out_shape=jax.ShapeDtypeStruct(array.shape, array.dtype),
        grid_spec=pltpu.PrefetchScalarGridSpec(
            num_scalar_prefetch=1,
            grid=(array.shape[1] // width,),
            in_specs=[pl.BlockSpec((tokens, width), near if back else far)],
            out_specs=pl.BlockSpec((tokens, width), far if back else near),
        ),
        cost_estimate=pl.CostEstimate(flops=0, transcendentals=0, bytes_accessed=2 * array.nbytes),
        compiler_params=params(),
        name="put_columns" if back else "take_columns",
    )(jnp.stack(table).astype(jnp.int32), array)


def pack_attn_kernel(query_ref, out_ref, key_ref, value_ref, gains_ref, near_ref, ring_ref):
    heads_w = query_ref.shape[1]
    turned = out_ref[...].T
    for ref in (near_ref, ring_ref):
        ref[:, :heads_w] = query_ref[...]
        ref[:, heads_w : 2 * heads_w] = turned
    for k, ref in enumerate((key_ref, value_ref, gains_ref)):
        near_ref[:, 2 * heads_w + k * HD : 2 * heads_w + (k + 1) * HD] = ref[...]


def pack_attn(w_query, w_out, w_key, w_value, gains):
    rows, heads_w = w_query.shape
    return pl.pallas_call(
        pack_attn_kernel,
        out_shape=(
            jax.ShapeDtypeStruct((rows, 2 * heads_w + 3 * HD), BF16),
            jax.ShapeDtypeStruct((rows, 2 * heads_w), BF16),
        ),
        cost_estimate=pl.CostEstimate(flops=0, transcendentals=0, bytes_accessed=2_000_000),
        compiler_params=params(0),
        name="pack_attn",
    )(w_query, w_out, w_key, w_value, gains)


def plain_pack_attn(w_query, w_out, w_key, w_value, gains):
    ring = jnp.concatenate([w_query, w_out.T], axis=1)
    return jnp.concatenate([ring, w_key, w_value, gains], axis=1), ring


def pack_ffn_kernel(gate_ref, up_ref, down_ref, out_ref):
    units = gate_ref.shape[1]
    for at in range(0, units, TILE):
        size = min(TILE, units - at)
        out_ref[:, 3 * at : 3 * at + size] = gate_ref[:, at : at + size]
        out_ref[:, 3 * at + size : 3 * at + 2 * size] = up_ref[:, at : at + size]
        out_ref[:, 3 * at + 2 * size : 3 * at + 3 * size] = down_ref[at : at + size, :].T


def pack_ffn(w_gate, w_up, w_down):
    rows, units = w_gate.shape
    return pl.pallas_call(
        pack_ffn_kernel,
        out_shape=jax.ShapeDtypeStruct((rows, 3 * units), BF16),
        cost_estimate=pl.CostEstimate(flops=0, transcendentals=0, bytes_accessed=12 * rows * units),
        compiler_params=params(0),
        name="pack_ffn",
    )(w_gate, w_up, w_down)


def plain_pack_ffn(w_gate, w_up, w_down):
    return jnp.concatenate([w_gate, w_up, w_down.T], axis=1)


def enter_kernel(count, tail, table_ref, tokens_ref, *refs):
    key_refs, value_refs, gain_refs = refs[:count], refs[count : 2 * count], refs[2 * count : tail]
    low_ref, normed_ref, turned_ref, kv_ref, gains_ref = refs[tail:]
    rows = key_refs[0].shape[0]
    slices = table_ref.shape[0]
    size = low_ref.shape[1] // slices
    squares = 0.0
    for k in range(slices):
        start = pl.multiple_of(table_ref[k] * size, size)
        block = tokens_ref[:, pl.ds(start, size)]
        low_ref[:, k * size : (k + 1) * size] = block
        block = block.astype(F32)
        squares = squares + jnp.sum(block * block, axis=-1, keepdims=True)
    scale = lax.rsqrt(squares / low_ref.shape[1] + norm_eps)
    kv = 0.0
    for i in range(count):
        part = slice(i * rows, (i + 1) * rows)
        gains = gain_refs[i][...].astype(F32).T
        gains_ref[:, part] = gains[:8]
        normed = (low_ref[:, part].astype(F32) * scale * gains[0:1]).astype(BF16)
        normed_ref[:, part] = normed
        turned_ref[part, :] = normed.T
        weights = jnp.concatenate([key_refs[i][...], value_refs[i][...]], axis=1)
        kv = kv + nn(normed, weights)
    kv_ref[...] = kv.astype(BF16)


def enter(tokens, table, near, at):
    own, width = tokens.shape
    count, rows = len(near), near[0].shape[0]

    def columns(place):
        return [pl.BlockSpec((rows, HD), lambda i, table_ref: (0, at // HD + place))] * count

    def full(shape):
        return pl.BlockSpec(shape, lambda i, table_ref: (0, 0))

    return pl.pallas_call(
        functools.partial(enter_kernel, count, 3 * count),
        out_shape=(
            jax.ShapeDtypeStruct((own, width), BF16),
            jax.ShapeDtypeStruct((own, width), BF16),
            jax.ShapeDtypeStruct((width, own), BF16),
            jax.ShapeDtypeStruct((own, 2 * HD), BF16),
            jax.ShapeDtypeStruct((8, width), F32),
        ),
        grid_spec=pltpu.PrefetchScalarGridSpec(
            num_scalar_prefetch=1,
            grid=(1,),
            in_specs=[full(tokens.shape)] + columns(0) + columns(1) + columns(2),
            out_specs=[full((own, width))] * 2
            + [full((width, own)), full((own, 2 * HD)), full((8, width))],
        ),
        cost_estimate=pl.CostEstimate(
            flops=4 * own * width * HD, transcendentals=0, bytes_accessed=6_000_000
        ),
        compiler_params=params(),
        name="enter",
    )(jnp.stack(table).astype(jnp.int32), tokens, *near, *near, *near)


def plain_enter(tokens, table, near, at):
    rows = tokens.shape[1] // len(table)
    low = move_columns(tokens, table, rows)
    weights = stack_rows([piece[:, at:] for piece in near])
    gains = weights[:, 2 * HD : 2 * HD + 8].astype(F32).T
    value = low.astype(F32)
    scale = lax.rsqrt(jnp.mean(value * value, axis=-1, keepdims=True) + norm_eps)
    normed = (value * scale * gains[0:1]).astype(BF16)
    return low, normed, normed.T, nn(normed, weights[:, : 2 * HD]).astype(BF16), gains


def pair_up(block):
    return jnp.concatenate([block[:, :HD], block[:, HD:]], axis=0)


def pair_off(block):
    tokens = block.shape[0] // 2
    return jnp.concatenate([block[:tokens], block[tokens:]], axis=1)


def attend_kernel(count, blocks, refs):
    normed_ref, bias_ref, acc_ref = refs[:3]
    kv_refs = refs[3 : 3 + blocks]
    wq_refs = refs[3 + blocks : 3 + blocks + count]
    wo_refs = refs[3 + blocks + count : 3 + blocks + 2 * count]
    query_ref, mixed_ref, total_ref, sum_ref, score_ref = refs[3 + blocks + 2 * count :]
    rows = wq_refs[0].shape[0]
    tokens = normed_ref.shape[0]

    query = sum(
        nn(normed_ref[:, i * rows : (i + 1) * rows], wq_refs[i][...]) for i in range(count)
    ).astype(BF16)
    query_ref[...] = query
    query = pair_up(query)
    peak = None
    for b in range(blocks):
        bias = bias_ref[b * tokens : (b + 1) * tokens, :]
        scores = nt(kv_refs[b][:, :HD], query) * (HD ** (-0.5) * LOG2E)
        scores = scores + jnp.concatenate([bias, bias], axis=1)
        score_ref[b] = scores
        top = jnp.max(scores, axis=0, keepdims=True)
        peak = top if peak is None else jnp.maximum(peak, top)
    sums, mixed = 0.0, 0.0
    for b in range(blocks):
        raised = jnp.exp2(score_ref[b] - peak)
        sums = sums + jnp.sum(raised, axis=0, keepdims=True)
        mixed = mixed + tn(kv_refs[b][:, HD:], raised.astype(BF16))
    total_ref[0] = peak + jnp.log2(sums)
    mixed = pair_off((mixed / sums).T.astype(BF16))
    mixed_ref[...] = mixed

    @pl.when(pl.program_id(0) == 0)
    def _():
        sum_ref[...] = acc_ref[...].astype(F32)

    for i in range(count):
        sum_ref[:, i * rows : (i + 1) * rows] += nt(mixed, wo_refs[i][...])


def attend_block(normed, bias, acc, kv_ring, pieces, many):
    tokens, width = normed.shape
    count, blocks = len(pieces), len(kv_ring)
    rows = pieces[0].shape[0]
    pairs = width // blocks // (2 * HD)
    heads_w = many * width // blocks

    def query_at(j):
        return (0, j // pairs * (2 * pairs) + j % pairs)

    def out_at(j):
        return (0, j // pairs * (2 * pairs) + pairs + j % pairs)

    total = blocks * tokens
    flops = 2 * tokens * heads_w * (2 * width + 2 * total)
    return pl.pallas_call(
        lambda *refs: attend_kernel(count, blocks, refs),
        out_shape=(
            jax.ShapeDtypeStruct((tokens, heads_w), BF16),
            jax.ShapeDtypeStruct((tokens, heads_w), BF16),
            jax.ShapeDtypeStruct((many * pairs, 1, 2 * tokens), F32),
            jax.ShapeDtypeStruct((tokens, width), F32),
        ),
        grid=(many * pairs,),
        in_specs=[whole(normed), whole(bias), whole(acc)]
        + [whole(kv) for kv in kv_ring]
        + [pl.BlockSpec((rows, 2 * HD), query_at)] * count
        + [pl.BlockSpec((rows, 2 * HD), out_at)] * count,
        out_specs=(
            pl.BlockSpec((tokens, 2 * HD), lambda j: (0, j)),
            pl.BlockSpec((tokens, 2 * HD), lambda j: (0, j)),
            pl.BlockSpec((1, 1, 2 * tokens), lambda j: (j, 0, 0)),
            pl.BlockSpec((tokens, width), lambda j: (0, 0)),
        ),
        scratch_shapes=[pltpu.VMEM((blocks, tokens, 2 * tokens), F32)],
        cost_estimate=pl.CostEstimate(
            flops=flops, transcendentals=tokens * total * heads_w // HD, bytes_accessed=14_000_000
        ),
        compiler_params=params(),
        name="attend",
    )(normed, bias, acc, *kv_ring, *pieces, *pieces)


def attend_back_kernel(count, blocks, first, refs):
    branch_ref, bias_ref = refs[:2]
    refs = refs[2:]
    if not first:
        kv_in_ref, normed_in_ref = refs[:2]
        refs = refs[2:]
    query_ref, mixed_ref, total_ref = refs[:3]
    refs = refs[3:]
    kv_refs, refs = refs[:blocks], refs[blocks:]
    wq_refs, refs = refs[:count], refs[count:]
    wo_refs, refs = refs[:count], refs[count:]
    query_grad_ref, kv_grad_ref, normed_grad_ref = refs
    rows = wq_refs[0].shape[0]
    tokens = branch_ref.shape[0]
    scale = HD ** (-0.5)

    @pl.when(pl.program_id(0) == 0)
    def _():
        if first:
            kv_grad_ref[...] = jnp.zeros_like(kv_grad_ref)
            normed_grad_ref[...] = jnp.zeros_like(normed_grad_ref)
        else:
            kv_grad_ref[...] = kv_in_ref[...]
            normed_grad_ref[...] = normed_in_ref[...]

    grad = sum(
        nn(branch_ref[:, i * rows : (i + 1) * rows], wo_refs[i][...]) for i in range(count)
    ).astype(BF16)
    product = pair_up(grad.astype(F32) * mixed_ref[...].astype(F32))
    inner = jnp.sum(product.T, axis=0, keepdims=True)
    grad = pair_up(grad)
    query = pair_up(query_ref[...])
    totals = total_ref[0]
    query_grad = 0.0
    for b in range(blocks):
        keys, values = kv_refs[b][:, :HD], kv_refs[b][:, HD:]
        bias = bias_ref[b * tokens : (b + 1) * tokens, :]
        scores = nt(keys, query) * (scale * LOG2E) + jnp.concatenate([bias, bias], axis=1)
        shares = jnp.exp2(scores - totals)
        score_grad = (shares * (nt(values, grad) - inner)).astype(BF16)
        query_grad = query_grad + tn(keys, score_grad)
        at = slice(b * tokens, (b + 1) * tokens)
        kv_grad_ref[at, :HD] += scale * nn(score_grad, query)
        kv_grad_ref[at, HD:] += nn(shares.astype(BF16), grad)
    query_grad = pair_off((scale * query_grad).T.astype(BF16))
    query_grad_ref[...] = query_grad
    for i in range(count):
        normed_grad_ref[:, i * rows : (i + 1) * rows] += nt(query_grad, wq_refs[i][...])


def attend_back_block(branch, bias, sums, query, mixed, total, kv_ring, pieces, at):
    tokens, width = branch.shape
    first = sums is None
    count, blocks = len(pieces), len(kv_ring)
    rows = pieces[0].shape[0]
    heads_w = width // blocks
    pairs = heads_w // (2 * HD)
    base = 2 * pairs * at
    two = pl.BlockSpec((tokens, 2 * HD), lambda j: (0, j))
    kept = pl.BlockSpec((tokens, 2 * HD), lambda j: (0, pairs * at + j))
    sums = [] if first else list(sums)
    keys = blocks * tokens
    return pl.pallas_call(
        lambda *refs: attend_back_kernel(count, blocks, first, refs),
        out_shape=(
            jax.ShapeDtypeStruct((tokens, heads_w), BF16),
            jax.ShapeDtypeStruct((keys, 2 * HD), F32),
            jax.ShapeDtypeStruct((tokens, width), F32),
        ),
        grid=(pairs,),
        in_specs=[whole(branch), whole(bias)]
        + [whole(item) for item in sums]
        + [kept, kept, pl.BlockSpec((1, 1, 2 * tokens), lambda j: (pairs * at + j, 0, 0))]
        + [whole(kv) for kv in kv_ring]
        + [pl.BlockSpec((rows, 2 * HD), lambda j: (0, base + j))] * count
        + [pl.BlockSpec((rows, 2 * HD), lambda j: (0, base + pairs + j))] * count,
        out_specs=(
            two,
            pl.BlockSpec((keys, 2 * HD), lambda j: (0, 0)),
            pl.BlockSpec((tokens, width), lambda j: (0, 0)),
        ),
        cost_estimate=pl.CostEstimate(
            flops=2 * tokens * heads_w * (2 * width + 5 * keys),
            transcendentals=tokens * keys * heads_w // HD,
            bytes_accessed=16_000_000,
        ),
        compiler_params=params(),
        name="attend_back",
    )(branch, bias, *sums, query, mixed, total, *kv_ring, *pieces, *pieces)


def attend_weights_kernel(sends, keeps, refs):
    outs = refs[len(refs) - sends - keeps :]

    def work(normed_ref, branch_ref, query_grad_ref, mixed_ref, out_ref, come_ref):
        half = query_grad_ref.shape[1]
        left = nn(normed_ref[...], query_grad_ref[...])
        right = nn(branch_ref[...], mixed_ref[...])
        if come_ref is not None:
            come = come_ref[...].astype(F32)
            left, right = left + come[:, :half], right + come[:, half:]
        out_ref[:, :half] = left.astype(BF16)
        out_ref[:, half:] = right.astype(BF16)

    if sends:
        work(*refs[:4], outs[0], None)
    if keeps:
        refs = refs[4 * sends :]
        work(*refs[:4], outs[-1], refs[4])


def attend_weights(normed, branch, send=None, keep=None):
    width, tokens = normed.shape
    steps = 4
    rows = width // 2 // steps
    specs, arrays, out_shape = [], [], []
    for item, first in ((send, steps), (keep, 0)):
        if item is None:
            continue
        query_grad, mixed, at, *come = item
        heads_w = query_grad.shape[1]
        left = pl.BlockSpec((rows, tokens), lambda i, first=first: (first + i, 0))
        right = pl.BlockSpec(
            (tokens, heads_w), lambda i, at=at: (0, at), pipeline_mode=pl.Buffered(1)
        )
        out = pl.BlockSpec((rows, 2 * heads_w), lambda i: (i, 0))
        specs += [left, left, whole(query_grad), right] + [out] * len(come)
        arrays += [normed, branch, query_grad, mixed, *come]
        out_shape.append(jax.ShapeDtypeStruct((width // 2, 2 * heads_w), BF16))
    return pl.pallas_call(
        lambda *refs: attend_weights_kernel(int(send is not None), int(keep is not None), refs),
        out_shape=out_shape,
        grid=(steps,),
        in_specs=specs,
        out_specs=[out] * len(out_shape),
        cost_estimate=pl.CostEstimate(
            flops=2 * tokens * width * heads_w * len(out_shape),
            transcendentals=0,
            bytes_accessed=6_000_000,
        ),
        compiler_params=params(),
        name="attend_weights",
    )(*arrays)


def ffn_kernel(count, steps, last, refs):
    normed_ref, grad_ref = refs[:2]
    w_refs = refs[2 : 2 + count]
    act_ref, part_ref, back_ref, part_acc, back_acc = refs[2 + count :]
    rows = w_refs[0].shape[0]
    step = pl.program_id(0)

    @pl.when(step == 0)
    def _():
        part_acc[...] = jnp.zeros_like(part_acc)
        back_acc[...] = jnp.zeros_like(back_acc)

    def work(tile):
        parts = [slice(i * rows, (i + 1) * rows) for i in range(count)]
        gate = sum(nn(normed_ref[:, p], w[:, :tile]) for p, w in zip(parts, w_refs))
        upward = sum(nn(normed_ref[:, p], w[:, tile : 2 * tile]) for p, w in zip(parts, w_refs))
        hidden_grad = sum(
            nn(grad_ref[:, p], w[:, 2 * tile : 3 * tile]) for p, w in zip(parts, w_refs)
        )
        sigma = jax.nn.sigmoid(gate)
        silu = gate * sigma
        hidden = (silu * upward).astype(BF16)
        up_grad = (hidden_grad * silu).astype(BF16)
        gate_grad = (hidden_grad * upward * sigma * (1.0 + gate * (1.0 - sigma))).astype(BF16)
        act_ref[:, :tile] = gate_grad
        act_ref[:, tile : 2 * tile] = up_grad
        act_ref[:, 2 * tile : 3 * tile] = hidden
        both = jnp.concatenate([gate_grad, up_grad], axis=1)
        for p, w in zip(parts, w_refs):
            part_acc[:, p] += nt(hidden, w[:, 2 * tile : 3 * tile])
            back_acc[:, p] += nt(both, w[:, : 2 * tile])

    if steps > 1:
        pl.when(step < steps - 1)(lambda: work(TILE))
    pl.when(step == steps - 1)(lambda: work(last))

    @pl.when(step == steps - 1)
    def _():
        part_ref[...] = part_acc[...].astype(BF16)
        back_ref[...] = back_acc[...].astype(BF16)


def ffn_block(normed, grad, pieces):
    tokens, width = normed.shape
    count, rows = len(pieces), pieces[0].shape[0]
    units = pieces[0].shape[1] // 3
    steps = -(-units // TILE)
    last = units - (steps - 1) * TILE
    full = pl.BlockSpec((tokens, width), lambda j: (0, 0))
    out = jax.ShapeDtypeStruct((tokens, width), BF16)
    return pl.pallas_call(
        lambda *refs: ffn_kernel(count, steps, last, refs),
        out_shape=(jax.ShapeDtypeStruct((tokens, 3 * units), BF16), out, out),
        grid=(steps,),
        in_specs=[whole(normed), whole(grad)]
        + [pl.BlockSpec((rows, 3 * TILE), lambda j: (0, j))] * count,
        out_specs=(pl.BlockSpec((tokens, 3 * TILE), lambda j: (0, j)), full, full),
        scratch_shapes=[pltpu.VMEM((tokens, width), F32)] * 2,
        cost_estimate=pl.CostEstimate(
            flops=12 * tokens * width * units,
            transcendentals=tokens * units,
            bytes_accessed=6 * width * units + 12 * tokens * width,
        ),
        compiler_params=params(),
        name="ffn_block",
    )(normed, grad, *pieces)


def ffn_weights_kernel(blocks, count, steps, last, adds, refs):
    normed_refs, refs = refs[:blocks], refs[blocks:]
    grad_refs, refs = refs[:blocks], refs[blocks:]
    act_refs, refs = refs[:blocks], refs[blocks:]
    added_refs, out_refs = refs[: adds * count], refs[adds * count :]

    def work(piece, tile):
        both = sum(tn(normed_refs[b][...], act_refs[b][:, : 2 * tile]) for b in range(blocks))
        down = sum(
            tn(grad_refs[b][...], act_refs[b][:, 2 * tile : 3 * tile]) for b in range(blocks)
        )
        for k in range(adds):
            added = added_refs[k * count + piece]
            both = both + added[:, : 2 * tile].astype(F32)
            down = down + added[:, 2 * tile : 3 * tile].astype(F32)
        out_refs[piece][:, : 2 * tile] = both.astype(BF16)
        out_refs[piece][:, 2 * tile : 3 * tile] = down.astype(BF16)

    turn, step = pl.program_id(0), pl.program_id(1)
    for at in range(count):
        if steps > 1:
            pl.when((turn == at) & (step < steps - 1))(functools.partial(work, at, TILE))
        pl.when((turn == at) & (step == steps - 1))(functools.partial(work, at, last))


def ffn_weights(normed_ring, grad_ring, acts, first, count, rows, added=()):
    tokens = normed_ring[0].shape[0]
    units = acts[0].shape[1] // 3
    blocks = len(acts)
    steps = -(-units // TILE)
    last = units - (steps - 1) * TILE
    left = pl.BlockSpec((tokens, rows), lambda i, j: (0, first + i))

    def piece_spec(piece, block):
        def place(i, j):
            return (block, jnp.where(i < piece, 0, jnp.where(i > piece, steps - 1, j)))

        return pl.BlockSpec((rows, 3 * TILE), place)

    wide = [piece_spec(piece, 0) for piece in range(count)]
    specs, arrays = [], []
    for item in added:
        if isinstance(item, (list, tuple)):
            specs, arrays = specs + wide, arrays + list(item)
        else:
            specs = specs + [piece_spec(piece, piece) for piece in range(count)]
            arrays = arrays + [item] * count
    return pl.pallas_call(
        lambda *refs: ffn_weights_kernel(blocks, count, steps, last, len(added), refs),
        out_shape=[jax.ShapeDtypeStruct((rows, 3 * units), BF16)] * count,
        grid=(count, steps),
        in_specs=[left] * (2 * blocks)
        + [pl.BlockSpec((tokens, 3 * TILE), lambda i, j: (0, j))] * blocks
        + specs,
        out_specs=wide,
        cost_estimate=pl.CostEstimate(
            flops=6 * tokens * blocks * count * rows * units,
            transcendentals=0,
            bytes_accessed=6 * tokens * blocks * units * count + 6 * count * rows * units,
        ),
        compiler_params=params(2),
        name="ffn_weights",
    )(*normed_ring, *grad_ring, *acts, *arrays)


def turn_kernel(come_ref, part_ref, given_ref, value_ref, gain_ref, *refs):
    after_ref, low_ref, turned_ref, term_ref = refs
    value = value_ref[...]
    grad = come_ref[...].astype(F32) + part_ref[...].astype(F32)
    scale = lax.rsqrt(jnp.mean(value * value, axis=-1, keepdims=True) + norm_eps)
    term_ref[...] = jnp.sum(grad * value * scale, axis=0, keepdims=True)
    after = given_ref[...].astype(F32) + norm_back(value, scale, gain_ref[1:2, :], grad)
    after_ref[...] = after
    low = after.astype(BF16)
    low_ref[...] = low
    turned_ref[...] = low.T


def turn(come, part, given, value, gains):
    own, width = value.shape
    return pl.pallas_call(
        turn_kernel,
        out_shape=(
            jax.ShapeDtypeStruct((own, width), F32),
            jax.ShapeDtypeStruct((own, width), BF16),
            jax.ShapeDtypeStruct((width, own), BF16),
            jax.ShapeDtypeStruct((1, width), F32),
        ),
        cost_estimate=pl.CostEstimate(
            flops=0, transcendentals=0, bytes_accessed=20 * own * width
        ),
        compiler_params=params(0),
        name="turn",
    )(come, part, given, value, gains)


def plain_turn(come, part, given, value, gains):
    grad = come.astype(F32) + part.astype(F32)
    scale = lax.rsqrt(jnp.mean(value * value, axis=-1, keepdims=True) + norm_eps)
    term = jnp.sum(grad * value * scale, axis=0, keepdims=True)
    after = given.astype(F32) + norm_back(value, scale, gains[1:2], grad)
    low = after.astype(BF16)
    return after, low, low.T, term


def leave_kernel(come_count, count, slices, table_ref, *refs):
    kv_ref, refs = refs[0], refs[1:]
    come_refs, refs = refs[:come_count], refs[come_count:]
    d_key_ref, d_value_ref, grad_ref, normed_ref, low_ref, after_ref, gain_ref, ffn_ref = refs[:8]
    refs = refs[8:]
    key_refs, value_refs, refs = refs[:count], refs[count : 2 * count], refs[2 * count :]
    out_ref, keep_ref, send_ref, total_ref = refs
    rows = key_refs[0].shape[0]
    width = low_ref.shape[1]
    size = width // slices
    kv_grad = kv_ref[...]
    for ref in come_refs:
        kv_grad = kv_grad + ref[...].astype(F32)
    given = jnp.concatenate([d_key_ref[...], d_value_ref[...]], axis=1)
    kv_grad = (kv_grad + given.astype(F32)).astype(BF16)
    squares, inner = 0.0, 0.0
    for i in range(count):
        part = slice(i * rows, (i + 1) * rows)
        weights = jnp.concatenate([key_refs[i][...], value_refs[i][...]], axis=1)
        total = grad_ref[:, part] + nt(kv_grad, weights)
        total_ref[:, part] = total
        value = low_ref[:, part].astype(F32)
        squares = squares + jnp.sum(value * value, axis=-1, keepdims=True)
        inner = inner + jnp.sum(total * gain_ref[0:1, part] * value, axis=-1, keepdims=True)
    scale = lax.rsqrt(squares / width + norm_eps)
    shrink = scale * scale * scale * (inner / width)
    for i in range(count):
        part = slice(i * rows, (i + 1) * rows)
        total, value = total_ref[:, part], low_ref[:, part].astype(F32)
        gain_term = jnp.sum(total * value * scale, axis=0, keepdims=True)
        terms = jnp.concatenate(
            [gain_term, ffn_ref[:, part], jnp.zeros((HD - 2, rows), F32)], axis=0
        )
        block = jnp.concatenate([tn(normed_ref[:, part], kv_grad), terms.T], axis=1).astype(BF16)
        half = count // 2
        ref = keep_ref if i < half else send_ref
        ref[(i % half) * rows : (i % half + 1) * rows, :] = block
    for k in range(slices):
        part = slice(k * size, (k + 1) * size)
        value = low_ref[:, part].astype(F32)
        grad = scale * (total_ref[:, part] * gain_ref[0:1, part]) - value * shrink
        start = pl.multiple_of(table_ref[k] * size, size)
        out_ref[:, pl.ds(start, size)] = after_ref[:, part] + grad


def leave(table, kv_acc, kv_come, d_keys, d_values, normed_grad, normed, low, after_grad, gains,
          ffn_term, near, at):
    own, width = normed.shape
    count, rows = len(near), near[0].shape[0]

    def columns(place):
        return [pl.BlockSpec((rows, HD), lambda i, table_ref: (0, at // HD + place))] * count

    def full(shape):
        return pl.BlockSpec(shape, lambda i, table_ref: (0, 0))

    given = [*kv_come, d_keys, d_values, normed_grad, normed, low, after_grad, gains, ffn_term]
    half = jax.ShapeDtypeStruct((width // 2, 3 * HD), BF16)
    return pl.pallas_call(
        functools.partial(leave_kernel, len(kv_come), count, len(table)),
        out_shape=(jax.ShapeDtypeStruct((own, width), F32), half, half),
        grid_spec=pltpu.PrefetchScalarGridSpec(
            num_scalar_prefetch=1,
            grid=(1,),
            in_specs=[full((own, 2 * HD))]
            + [full(item.shape) for item in given]
            + columns(0)
            + columns(1),
            out_specs=[full((own, width)), full(half.shape), full(half.shape)],
            scratch_shapes=[pltpu.VMEM((own, width), F32)],
        ),
        cost_estimate=pl.CostEstimate(
            flops=8 * own * width * HD, transcendentals=0, bytes_accessed=16_000_000
        ),
        compiler_params=params(),
        name="leave",
    )(jnp.stack(table).astype(jnp.int32), kv_acc, *given, *near, *near)


def leave_out_kernel(slices, table_ref, after_ref, come_ref, part_ref, out_ref):
    size = after_ref.shape[1] // slices
    for k in range(slices):
        part = slice(k * size, (k + 1) * size)
        total = come_ref[:, part].astype(F32) + part_ref[:, part].astype(F32)
        start = pl.multiple_of(table_ref[k] * size, size)
        out_ref[:, pl.ds(start, size)] = (after_ref[:, part] + total).astype(BF16)


def leave_out(table, after_attn, come, part):
    def full(shape):
        return pl.BlockSpec(shape, lambda i, table_ref: (0, 0))

    return pl.pallas_call(
        functools.partial(leave_out_kernel, len(table)),
        out_shape=jax.ShapeDtypeStruct(after_attn.shape, BF16),
        grid_spec=pltpu.PrefetchScalarGridSpec(
            num_scalar_prefetch=1,
            grid=(1,),
            in_specs=[full(after_attn.shape)] * 3,
            out_specs=full(after_attn.shape),
        ),
        cost_estimate=pl.CostEstimate(flops=0, transcendentals=0, bytes_accessed=8_000_000),
        compiler_params=params(),
        name="leave_out",
    )(jnp.stack(table).astype(jnp.int32), after_attn, come, part)


def unpack_ffn_kernel(keep_ref, come_ref, gate_ref, up_ref, down_ref):
    units = gate_ref.shape[1]
    for at in range(0, units, TILE):
        size = min(TILE, units - at)

        def take(k):
            cols = slice(3 * at + k * size, 3 * at + (k + 1) * size)
            return keep_ref[:, cols].astype(F32) + come_ref[:, cols].astype(F32)

        gate_ref[:, at : at + size] = take(0)
        up_ref[:, at : at + size] = take(1)
        down_ref[at : at + size, :] = take(2).T


def unpack_ffn(keep, come):
    rows, units = keep.shape[0], keep.shape[1] // 3
    flat = jax.ShapeDtypeStruct((rows, units), F32)
    return pl.pallas_call(
        unpack_ffn_kernel,
        out_shape=(flat, flat, jax.ShapeDtypeStruct((units, rows), F32)),
        cost_estimate=pl.CostEstimate(flops=0, transcendentals=0, bytes_accessed=24 * rows * units),
        compiler_params=params(0),
        name="unpack_ffn",
    )(keep, come)


def unpack_attn_kernel(moving_ref, keep_ref, come_ref, query_ref, out_ref):
    heads_w = query_ref.shape[1]
    total = keep_ref[...].astype(F32) + come_ref[...].astype(F32) + moving_ref[...].astype(F32)
    query_ref[...] = total[:, :heads_w]
    out_ref[...] = total[:, heads_w:].T


def unpack_attn(moving, keep, come):
    rows, heads_w = keep.shape[0], keep.shape[1] // 2
    return pl.pallas_call(
        unpack_attn_kernel,
        out_shape=(
            jax.ShapeDtypeStruct((rows, heads_w), F32),
            jax.ShapeDtypeStruct((heads_w, rows), F32),
        ),
        cost_estimate=pl.CostEstimate(flops=0, transcendentals=0, bytes_accessed=4_000_000),
        compiler_params=params(0),
        name="unpack_attn",
    )(moving, keep, come)


def place_kv_kernel(count, place_ref, *refs):
    kv_refs, (key_ref, value_ref) = refs[:count], refs[count:]
    own = kv_refs[0].shape[0]
    for r in range(count):
        start = pl.multiple_of(place_ref[r] * own, own)
        key_ref[pl.ds(start, own), :] = kv_refs[r][:, :HD]
        value_ref[pl.ds(start, own), :] = kv_refs[r][:, HD:]


def place_kv(places, kv_ring):
    own, count = kv_ring[0].shape[0], len(kv_ring)
    out = jax.ShapeDtypeStruct((count * own, HD), BF16)
    return pl.pallas_call(
        functools.partial(place_kv_kernel, count),
        out_shape=(out, out),
        grid_spec=pltpu.PrefetchScalarGridSpec(
            num_scalar_prefetch=1,
            grid=(1,),
            in_specs=[pl.BlockSpec((own, 2 * HD), lambda i, place_ref: (0, 0))] * count,
            out_specs=[pl.BlockSpec(out.shape, lambda i, place_ref: (0, 0))] * 2,
        ),
        cost_estimate=pl.CostEstimate(flops=0, transcendentals=0, bytes_accessed=1_600_000),
        compiler_params=params(),
        name="place_kv",
    )(jnp.stack(places).astype(jnp.int32), *kv_ring)


def plain_attend_block(normed, bias, acc, kv_ring, pieces, many):
    step = normed.shape[1] // len(kv_ring)
    heads_w = many * step
    weights = stack_rows(pieces)
    blocks = [weights[:, at * step : (at + 1) * step] for at in range(2 * many)]
    weights = jnp.concatenate(blocks[::2] + blocks[1::2], axis=1)
    kv = stack_rows(kv_ring)
    query = nn(normed, weights[:, :heads_w]).astype(BF16)
    mixed, totals = [], []
    for head in range(heads_w // HD):
        scores = nt(kv[:, :HD], query[:, head * HD : (head + 1) * HD]) * (HD ** (-0.5)) + bias
        peak = jnp.max(scores, axis=0, keepdims=True)
        raised = jnp.exp(scores - peak)
        sums = jnp.sum(raised, axis=0, keepdims=True)
        mixed.append(tn((raised / sums).astype(BF16), kv[:, HD:]).astype(BF16))
        totals.append(peak + jnp.log(sums))
    mixed = jnp.concatenate(mixed, axis=1)
    return query, mixed, jnp.concatenate(totals, axis=0), acc + nt(mixed, weights[:, heads_w:])


def plain_attend_back_block(branch, bias, sums, query, mixed, total, kv_ring, pieces, at):
    heads_w = branch.shape[1] // len(kv_ring)
    weights = stack_rows(pieces)[:, 2 * at * heads_w : 2 * (at + 1) * heads_w]
    query = query[:, at * heads_w : (at + 1) * heads_w]
    total = total[at * heads_w // HD : (at + 1) * heads_w // HD]
    kv = stack_rows(kv_ring)
    keys, values = kv[:, :HD], kv[:, HD:]
    scale = HD ** (-0.5)
    grad = nn(branch, weights[:, heads_w:]).astype(BF16)
    key_acc, value_acc, query_grad = 0.0, 0.0, []
    for head in range(heads_w // HD):
        cols = slice(head * HD, (head + 1) * HD)
        scores = nt(keys, query[:, cols]) * scale + bias
        shares = jnp.exp(scores - total[head : head + 1])
        share_grad = nt(values, grad[:, cols])
        value_acc = value_acc + nn(shares.astype(BF16), grad[:, cols])
        inner = jnp.sum(shares * share_grad, axis=0, keepdims=True)
        score_grad = (shares * (share_grad - inner)).astype(BF16)
        query_grad.append((scale * tn(score_grad, keys)).astype(BF16))
        key_acc = key_acc + scale * nn(score_grad, query[:, cols])
    query_grad = jnp.concatenate(query_grad, axis=1)
    kv_grad = jnp.concatenate([key_acc, value_acc], axis=1)
    normed_grad = nt(query_grad, weights[:, :heads_w])
    if sums is not None:
        kv_grad, normed_grad = kv_grad + sums[0], normed_grad + sums[1]
    return query_grad, kv_grad, normed_grad


def plain_attend_weights(normed, branch, send=None, keep=None):
    half = normed.shape[0] // 2
    outs = []
    for item, first in ((send, half), (keep, 0)):
        if item is None:
            continue
        query_grad, mixed, at, *come = item
        heads_w = query_grad.shape[1]
        mixed = mixed[:, at * heads_w : (at + 1) * heads_w]
        part = slice(first, first + half)
        out = jnp.concatenate([nn(normed[part], query_grad), nn(branch[part], mixed)], axis=1)
        outs.append((out + come[0].astype(F32) if come else out).astype(BF16))
    return outs


def plain_ffn_block(normed, grad, pieces):
    weights = stack_rows(pieces)
    units = weights.shape[1] // 3
    gate_w, up_w, down_w = jnp.split(weights, 3, axis=1)
    gate = nn(normed, gate_w)
    upward = nn(normed, up_w)
    sigma = jax.nn.sigmoid(gate)
    hidden = (gate * sigma * upward).astype(BF16)
    part = nt(hidden, down_w).astype(BF16)
    hidden_grad = nn(grad, down_w)
    gate_grad = (hidden_grad * upward * sigma * (1.0 + gate * (1.0 - sigma))).astype(BF16)
    up_grad = (hidden_grad * gate * sigma).astype(BF16)
    back = (nt(gate_grad, gate_w) + nt(up_grad, up_w)).astype(BF16)
    return jnp.concatenate([gate_grad, up_grad, hidden], axis=1), part, back


def plain_ffn_weights(normed_ring, grad_ring, acts, first, count, rows, added=()):
    normed, grad, acts = stack_rows(normed_ring), stack_rows(grad_ring), stack_rows(acts)
    units = acts.shape[1] // 3
    pieces = []
    for piece in range(count):
        cols = slice((first + piece) * rows, (first + piece + 1) * rows)
        out = [tn(normed[:, cols], acts[:, : 2 * units]), tn(grad[:, cols], acts[:, 2 * units :])]
        out = jnp.concatenate(out, axis=1)
        for item in added:
            single = isinstance(item, (list, tuple))
            out = out + (item[piece] if single else item[piece * rows :][:rows]).astype(F32)
        pieces.append(out.astype(BF16))
    return pieces


def plain_leave(table, kv_acc, kv_come, d_keys, d_values, normed_grad, normed, low, after_grad,
                gains, ffn_term, near, at):
    own, width = normed.shape
    kv_grad = kv_acc[:own]
    for come in kv_come:
        kv_grad = kv_grad + come.astype(F32)
    kv_grad = kv_grad + jnp.concatenate([d_keys, d_values], axis=1).astype(F32)
    kv_grad = kv_grad.astype(BF16)
    kv_w = stack_rows([piece[:, at : at + 2 * HD] for piece in near])
    normed_grad = normed_grad + nt(kv_grad, kv_w)
    value = low.astype(F32)
    scale = lax.rsqrt(jnp.mean(value * value, axis=-1, keepdims=True) + norm_eps)
    grad = after_grad + norm_back(value, scale, gains[0:1], normed_grad)
    gain_term = jnp.sum(normed_grad * value * scale, axis=0)
    small = [tn(normed, kv_grad), gain_term[:, None], ffn_term.T, jnp.zeros((width, HD - 2), F32)]
    small = jnp.concatenate(small, axis=1).astype(BF16)
    grad = move_columns(grad, table, width // len(table), back=True)
    return grad, small[: width // 2], small[width // 2 :]


def plain_leave_out(table, after_attn, come, part):
    out = (after_attn + (come.astype(F32) + part.astype(F32))).astype(BF16)
    return move_columns(out, table, out.shape[1] // len(table), back=True)


def plain_unpack_ffn(keep, come):
    gate, up, down = jnp.split(keep.astype(F32) + come.astype(F32), 3, axis=1)
    return gate, up, down.T


def plain_unpack_attn(moving, keep, come):
    total = keep.astype(F32) + come.astype(F32) + moving.astype(F32)
    heads_w = total.shape[1] // 2
    return total[:, :heads_w], total[:, heads_w:].T


def plain_place_kv(places, kv_ring):
    own = kv_ring[0].shape[0]
    out = jnp.zeros((len(kv_ring) * own, 2 * HD), BF16)
    for start, block in zip(places, kv_ring):
        out = lax.dynamic_update_slice_in_dim(out, block, start * own, axis=0)
    return out[:, :HD], out[:, HD:]


KERNELS = (
    pack_attn,
    pack_ffn,
    enter,
    attend_block,
    attend_back_block,
    attend_weights,
    ffn_block,
    ffn_weights,
    turn,
    leave,
    leave_out,
    unpack_ffn,
    unpack_attn,
    place_kv,
)
PLAIN = (
    plain_pack_attn,
    plain_pack_ffn,
    plain_enter,
    plain_attend_block,
    plain_attend_back_block,
    plain_attend_weights,
    plain_ffn_block,
    plain_ffn_weights,
    plain_turn,
    plain_leave,
    plain_leave_out,
    plain_unpack_ffn,
    plain_unpack_attn,
    plain_place_kv,
)


def on_device(
    ndp,
    nz,
    tokens,
    norm_attn,
    w_query,
    w_key,
    w_value,
    w_out,
    norm_ffn,
    w_gate,
    w_up,
    w_down,
    segment_ids,
    parents,
    positions,
    d_out,
    d_keys,
    d_values,
):
    me = lax.axis_index("dp")
    place_z = lax.axis_index("tensor")
    table = slice_table(me, ndp)
    own, width = tokens.shape[0], tokens.shape[1]
    rows = width // ndp
    heads_w = w_query.shape[1]
    units = w_gate.shape[1]
    fits = own % HD == 0 and rows % HD == 0 and units % HD == 0 and heads_w % (2 * HD) == 0
    (
        do_pack_attn,
        do_pack_ffn,
        do_enter,
        do_attend,
        do_attend_back,
        do_attend_weights,
        do_ffn,
        do_ffn_weights,
        do_turn,
        do_leave,
        do_leave_out,
        do_unpack_ffn,
        do_unpack_attn,
        do_place_kv,
    ) = KERNELS if fits else PLAIN

    gains = jnp.concatenate(
        [norm_attn[:, None], norm_ffn[:, None], jnp.zeros((rows, HD - 2), BF16)], axis=1
    )
    first_up = lookup(segment_ids, parents)
    second_up = lookup(first_up, parents)

    def own_rows(vector):
        return lax.dynamic_slice_in_dim(vector, place_z * own, own, axis=0)

    def ring_rows(vector):
        return jnp.concatenate(
            [
                lax.dynamic_slice_in_dim(vector, ((place_z - r) % nz) * own, own, axis=0)
                for r in range(nz)
            ],
            axis=0,
        )

    key_segment, key_place = ring_rows(segment_ids)[:, None], ring_rows(positions)[:, None]
    linked = (
        (key_segment == own_rows(segment_ids)[None])
        | (key_segment == own_rows(first_up)[None])
        | (key_segment == own_rows(second_up)[None])
    )
    bias = jnp.where(linked & (key_place <= own_rows(positions)[None]), 0.0, -1e30).astype(F32)

    near_item, ring_item = do_pack_attn(w_query, w_out, w_key, w_value, gains)
    near_flow = Flow("attn_w_near", gather_steps(near_item, ndp))
    attn_flow = Flow("attn_w_ring", ring_gather_steps(ring_item, nz))
    grad_low = move_columns(d_out, table, rows)
    ffn_pack = do_pack_ffn(w_gate, w_up, w_down)
    grad_low, bias, ffn_pack = meet([grad_low, bias, ffn_pack], [near_flow, attn_flow])
    near_flow.go(len(bit_orders(ndp)[0]) - 2)
    grad_low, ffn_pack = meet([grad_low, ffn_pack], [near_flow, attn_flow])
    ffn_flow = Flow("ffn_w", gather_steps(ffn_pack, ndp, True))
    near = list(near_flow.finish())
    near = meet(near, [attn_flow])
    tokens_low, normed, normed_turned, kv_own, gain_rows = do_enter(
        tokens, table, near, 2 * heads_w
    )
    ffn_gain = gain_rows[1:2]
    kv_ring = [kv_own] + [scoped("kv", shift, kv_own, nz, by) for by in range(1, nz)]
    *kv_ring, grad_low = meet(kv_ring + [grad_low], [attn_flow])
    attn_ring = attn_flow.finish()[1:]
    far_flow = Flow("attn_w_far", gather_steps(jnp.concatenate(attn_ring, axis=1), ndp))
    grad_flow = Flow("grad_ring", ring_gather_steps(grad_low, nz))

    normed, *kv_ring = meet([normed] + kv_ring, [far_flow, ffn_flow])
    normed, *ffn_flow.held = tie(normed, *ffn_flow.held)
    *kept_near, after_attn = do_attend(normed, bias, tokens_low, kv_ring, near, 1)
    grad_first = grad_flow.held[0]
    (after_attn,) = meet([after_attn], [grad_flow])
    (after_attn,) = meet([after_attn], [far_flow, ffn_flow])
    far = far_flow.finish()
    *kept_far, after_attn = do_attend(normed, bias, after_attn, kv_ring, far, nz - 1)
    grad_ring = [grad_low, grad_first]
    ffn_scale = lax.rsqrt(jnp.mean(after_attn * after_attn, axis=-1, keepdims=True) + norm_eps)
    ffn_own = (after_attn * ffn_scale * ffn_gain).astype(BF16)

    ring_flow = Flow("ffn_ring", ring_gather_steps(ffn_own, nz))
    ffn_ring, acts, parts, backs = meet([ffn_own], [ffn_flow, grad_flow]), [], [], []
    ffn_w = ffn_flow.finish()
    early = nz // 2 + 1
    backs_flow = None
    for block in range(nz):
        if block > 0:
            come, acts[-1], *ring_flow.held = tie(ring_flow.held[0], acts[-1])
            ring_flow.held = [come]
            ring_flow.go()
            ffn_ring.append(come)
        if block == early:
            first = (ffn_ring[:early], grad_ring[:early], acts[:early])
            (send,) = do_ffn_weights(*first, 1, 1, width // 2)
            kept = do_ffn_weights(*first, 0, 2, width // 4)
            ffn_ring[-1], send, *kept = tie(ffn_ring[-1], send, *kept)
        elif block > early:
            (ffn_ring[-1],) = meet(ffn_ring[-1:], [backs_flow])
        if block == 2:
            grad_ring = grad_flow.finish()
        act, part, back = do_ffn(ffn_ring[block], grad_ring[block], ffn_w)
        acts.append(act)
        parts.append(part)
        backs.append(back)
        if block == 1:
            backs_flow = Flow("backs", ring_steps(backs, nz, acts))

    acts[-1], *backs_flow.held = tie(acts[-1], *backs_flow.held)
    backs_flow.go()
    rest = (ffn_ring[early:], grad_ring[early:], acts[early:])
    (send,) = do_ffn_weights(*rest, 1, 1, width // 2, ([send],))
    parts[1], send = meet([parts[1], send], [backs_flow])
    come = scoped("ffn_g", core_swap, send, ndp)
    made = do_ffn_weights(*rest, 0, 2, width // 4, (kept, come))
    tied = list(tie(*made, *backs_flow.held))
    made, backs_flow.held = tied[: len(made)], tied[len(made) :]
    after_grad, branch, branch_turned, ffn_term = do_turn(
        *backs_flow.finish(), grad_low, after_attn, gain_rows
    )
    part_flow = Flow("parts", ring_steps(parts, nz))
    ffn_flow = Flow("ffn_g", chip_steps(*made, ndp))

    order = list(range(1, nz)) + [0]
    flows = [None] * nz
    done = [None] * nz
    sums = None
    for turn, block in enumerate(order):
        stored, pieces, at = (kept_far, far, block - 1) if block else (kept_near, near, 0)
        if turn > 0:
            due = [part_flow] + ([flows[nz - 3]] if turn == nz - 1 else [])
            branch, *made = meet([branch, *made], due)
            if turn == nz - 1:
                for place in range(1, nz - 2):
                    done[place] = add_low(*flows[place].finish())
                ring_flow = Flow("attn_g_ring", ring_steps(done, nz))
                for _ in range(nz - 4):
                    ring_flow.go()
            sent = scoped(f"attn_g_{order[turn - 1]}", core_swap, made[0], ndp)
            if turn > 1:
                flow = Flow(f"attn_g_{order[turn - 2]}", chip_steps(*made[1:], ndp))
                flows[order[turn - 2]] = flow
        query_grad, kv_acc, normed_grad = do_attend_back(
            branch, bias, sums, *stored, kv_ring, pieces, at
        )
        sums = (kv_acc, normed_grad)
        due = [flow for flow in flows if flow is not None]
        due += [ffn_flow] if turn else []
        this = (query_grad, stored[1], at)
        if turn == 0:
            made = do_attend_weights(normed_turned, branch_turned, this)
        else:
            waiting = [flow, ring_flow] if turn == nz - 1 else []
            due = [item for item in due if item not in waiting]
            query_grad, sent = meet([query_grad, sent], due, waiting)
            this = (query_grad, stored[1], at)
            made, both = do_attend_weights(normed_turned, branch_turned, this, (*back, sent))
            made = [made, both[: width // 4], both[width // 4 :]]
        back = this
    kv_low = kv_acc.astype(BF16)
    kv_come = [
        scoped("kv_g", shift, kv_low[by * own : (by + 1) * own], nz, -by) for by in range(1, nz)
    ]
    sent = scoped("attn_g_0", core_swap, made[0], ndp)
    flows[nz - 1] = Flow(f"attn_g_{nz - 1}", chip_steps(*made[1:], ndp))
    (both,) = do_attend_weights(normed_turned, branch_turned, None, (*back, sent))
    low, high = both[: width // 4], both[width // 4 :]
    low, high, *kv_come = meet([low, high, *kv_come], [flows[nz - 2], part_flow, ffn_flow])
    flows[0] = Flow("attn_g_0", chip_steps(low, high, ndp))
    input_grad, keep, send = do_leave(
        table,
        kv_acc,
        kv_come,
        d_keys,
        d_values,
        normed_grad,
        normed,
        tokens_low,
        after_grad,
        gain_rows,
        ffn_term,
        near,
        2 * heads_w,
    )
    small_flow = Flow("small_g", scatter_steps(keep, send, ndp))
    meet([], [flows[nz - 2], flows[nz - 1], flows[0]])
    done[nz - 2] = add_low(*flows[nz - 2].finish())
    (done[nz - 2],) = meet([done[nz - 2]], [ring_flow])

    meet([], [small_flow, flows[0], flows[nz - 1]])
    done[nz - 1] = add_low(*flows[nz - 1].finish())
    meet([], [ring_flow])
    meet([], [small_flow, flows[0]])
    done[0] = flows[0].finish()
    small_sum = add_low(*small_flow.finish())
    total = small_sum.astype(F32)
    for by in range(1, nz):
        total = total + scoped("small_g_ring", shift, small_sum, nz, by).astype(F32)
    moving, _ = ring_flow.finish()
    query_w_grad, out_w_grad = do_unpack_attn(moving, *done[0])
    gate_grad, up_grad, down_grad = do_unpack_ffn(*ffn_flow.finish())
    keys, values = do_place_kv([(place_z - r) % nz for r in range(nz)], kv_ring)
    return (
        do_leave_out(table, after_attn, *part_flow.finish()),
        keys,
        values,
        input_grad,
        total[:, 2 * HD],
        query_w_grad,
        total[:, :HD],
        total[:, HD : 2 * HD],
        out_w_grad,
        total[:, 2 * HD + 1],
        gate_grad,
        up_grad,
        down_grad,
    )


def solution(mesh):
    in_specs = (
        P(("dp", "tensor"), None),
        P("dp"),
        P("dp", "tensor"),
        P("dp", None),
        P("dp", None),
        P("tensor", "dp"),
        P("dp"),
        P("dp", "tensor"),
        P("dp", "tensor"),
        P("tensor", "dp"),
        P("dp"),
        P(),
        P("dp"),
        P(("dp", "tensor"), None),
        P(("dp", "tensor"), None),
        P(("dp", "tensor"), None),
    )
    out_specs = (
        P(("dp", "tensor"), None),
        P("dp", None),
        P("dp", None),
        P(("dp", "tensor"), None),
        P("dp"),
        P("dp", "tensor"),
        P("dp", None),
        P("dp", None),
        P("tensor", "dp"),
        P("dp"),
        P("dp", "tensor"),
        P("dp", "tensor"),
        P("tensor", "dp"),
    )
    body = functools.partial(on_device, mesh.shape["dp"], mesh.shape["tensor"])
    return jax.shard_map(
        body, mesh=mesh, in_specs=in_specs, out_specs=out_specs, check_vma=False
    )
```

```python
import functools

import jax
import jax.numpy as jnp
from jax import lax
from jax.experimental import pallas as pl
from jax.experimental.pallas import tpu as pltpu
from jax.sharding import PartitionSpec as P

HD = 128
norm_eps = 1e-05
F32 = jnp.float32
BF16 = jnp.bfloat16


def dot(left, right, dims):
    return lax.dot_general(left, right, ((dims[0], dims[1]), ((), ())), preferred_element_type=F32)


def nn(left, right):
    return dot(left, right, ((1,), (0,)))


def nt(left, right):
    return dot(left, right, ((1,), (1,)))


def tn(left, right):
    return dot(left, right, ((0,), (0,)))


def lookup(ids, table):
    hits = ids[:, None] == jnp.arange(table.shape[0], dtype=jnp.int32)[None, :]
    return jnp.sum(jnp.where(hits, table[None, :], 0), axis=1)


def norm_back(value, scale, gain, grad):
    weighted = grad * gain
    return scale * weighted - value * (scale * scale * scale) * jnp.mean(
        weighted * value, axis=-1, keepdims=True
    )


def bit_orders(ndp):
    bits = []
    bit = 2
    while bit < ndp:
        bits.append(bit)
        bit *= 2
    return bits, bits[::-1]


def plane_swap(array, ndp, step):
    orders = bit_orders(ndp)
    return lax.ppermute(array, "dp", [(d, d ^ orders[d & 1][step]) for d in range(ndp)])


def core_swap(array, ndp):
    return lax.ppermute(array, "dp", [(d, d ^ 1) for d in range(ndp)])


def slice_table(me, ndp):
    orders = bit_orders(ndp)
    count = len(orders[0])
    table = []
    for place in range(ndp):
        base = me ^ (place // (ndp // 2))
        even = base % 2 == 0
        owner = base
        for step in range(count):
            if (place >> step) & 1:
                owner = owner ^ jnp.where(even, orders[0][step], orders[1][step])
        table.append(owner)
    return table


def gather_steps(shard, ndp, settle=False):
    moved = yield [plane_swap(shard, ndp, 0)]
    pieces = [jnp.concatenate([shard, moved[0]], axis=0)]
    if settle:
        pieces = yield pieces
    for step in range(1, len(bit_orders(ndp)[0])):
        pieces = pieces + (yield [plane_swap(piece, ndp, step) for piece in pieces])
    pieces = pieces + (yield [core_swap(piece, ndp) for piece in pieces])
    yield tuple(pieces)


def ring_gather_steps(block, nt_):
    blocks = [block]
    for _ in range(nt_ - 1):
        blocks += yield [ring_next(blocks[-1], nt_)]
    yield tuple(blocks)


def add_low(left, right):
    return (left.astype(F32) + right.astype(F32)).astype(BF16)


def scatter_steps(keep, send, ndp):
    (come,) = yield [core_swap(send, ndp)]
    rows = keep.shape[0] // 2
    low, high = add_low(keep[:rows], come[:rows]), add_low(keep[rows:], come[rows:])
    yield from chip_steps(low, high, ndp)


def chip_steps(low, high, ndp):
    for step in range(len(bit_orders(ndp)[0]) - 1, 0, -1):
        (come,) = yield [plane_swap(high, ndp, step)]
        rows = low.shape[0] // 2
        low, high = add_low(low[:rows], come[:rows]), add_low(low[rows:], come[rows:])
    (come,) = yield [plane_swap(high, ndp, 0)]
    yield (low, come)


def ring_steps(parts, nt_, ahead=None):
    moving = yield [ring_next(parts[1], nt_)]
    for place in range(2, nt_):
        total = add_low(moving[0], parts[place])
        if ahead:
            total, ahead[-1] = tie(total, ahead[-1])
        moving = yield [ring_next(total, nt_)]
    yield (moving[0], parts[0])


class Flow:
    def __init__(self, name, steps):
        self.name, self.steps = name, steps
        with jax.named_scope(name):
            self.held = next(steps)

    def moving(self):
        return isinstance(self.held, list)

    def go(self, times=1):
        for _ in range(times):
            if self.moving():
                with jax.named_scope(self.name):
                    self.held = self.steps.send(self.held)

    def finish(self):
        while self.moving():
            self.go()
        return self.held


def meet(values, flows, others=()):
    going = [flow for flow in flows if flow.moving()]
    flows = going + [flow for flow in others if flow.moving()]
    held = [item for flow in flows for item in flow.held]
    count = len(values)
    tied = list(tie(*values, *held))
    values, held = tied[:count], tied[count:]
    for flow in flows:
        flow.held, held = held[: len(flow.held)], held[len(flow.held) :]
    for flow in going:
        flow.go()
    return values


def ring_next(array, nt_):
    return lax.ppermute(array, "tensor", [(i, (i + 1) % nt_) for i in range(nt_)])


def shift(array, nt_, by):
    return lax.ppermute(array, "tensor", [(i, (i + by) % nt_) for i in range(nt_)])


def stack_rows(pieces):
    return jnp.concatenate(pieces, axis=0)


def scoped(name, function, *items):
    with jax.named_scope(name):
        return function(*items)


def tie(*values):
    return lax.optimization_barrier(values)


LOG2E = 1.4426950408889634
TILE = 512


def params(count=1):
    return pltpu.CompilerParams(
        dimension_semantics=("arbitrary",) * count, vmem_limit_bytes=58 * 1024 * 1024
    )


def whole(array):
    zeros = (0,) * array.ndim
    return pl.BlockSpec(array.shape, lambda *_: zeros, pipeline_mode=pl.Buffered(1))


def move_kernel(table_ref, in_ref, out_ref):
    out_ref[...] = in_ref[...]


def move_columns(array, table, width, back=False):
    tokens = array.shape[0]

    def far(k, table_ref):
        return (0, table_ref[k])

    def near(k, table_ref):
        return (0, k)

    return pl.pallas_call(
        move_kernel,
        out_shape=jax.ShapeDtypeStruct(array.shape, array.dtype),
        grid_spec=pltpu.PrefetchScalarGridSpec(
            num_scalar_prefetch=1,
            grid=(array.shape[1] // width,),
            in_specs=[pl.BlockSpec((tokens, width), near if back else far)],
            out_specs=pl.BlockSpec((tokens, width), far if back else near),
        ),
        cost_estimate=pl.CostEstimate(flops=0, transcendentals=0, bytes_accessed=2 * array.nbytes),
        compiler_params=params(),
        name="put_columns" if back else "take_columns",
    )(jnp.stack(table).astype(jnp.int32), array)


def pack_attn_kernel(query_ref, out_ref, key_ref, value_ref, gains_ref, near_ref, ring_ref):
    heads_w = query_ref.shape[1]
    turned = out_ref[...].T
    for ref in (near_ref, ring_ref):
        ref[:, :heads_w] = query_ref[...]
        ref[:, heads_w : 2 * heads_w] = turned
    for k, ref in enumerate((key_ref, value_ref, gains_ref)):
        near_ref[:, 2 * heads_w + k * HD : 2 * heads_w + (k + 1) * HD] = ref[...]


def pack_attn(w_query, w_out, w_key, w_value, gains):
    rows, heads_w = w_query.shape
    return pl.pallas_call(
        pack_attn_kernel,
        out_shape=(
            jax.ShapeDtypeStruct((rows, 2 * heads_w + 3 * HD), BF16),
            jax.ShapeDtypeStruct((rows, 2 * heads_w), BF16),
        ),
        cost_estimate=pl.CostEstimate(flops=0, transcendentals=0, bytes_accessed=2_000_000),
        compiler_params=params(0),
        name="pack_attn",
    )(w_query, w_out, w_key, w_value, gains)


def plain_pack_attn(w_query, w_out, w_key, w_value, gains):
    ring = jnp.concatenate([w_query, w_out.T], axis=1)
    return jnp.concatenate([ring, w_key, w_value, gains], axis=1), ring


def pack_ffn_kernel(gate_ref, up_ref, down_ref, out_ref):
    units = gate_ref.shape[1]
    for at in range(0, units, TILE):
        size = min(TILE, units - at)
        out_ref[:, 3 * at : 3 * at + size] = gate_ref[:, at : at + size]
        out_ref[:, 3 * at + size : 3 * at + 2 * size] = up_ref[:, at : at + size]
        out_ref[:, 3 * at + 2 * size : 3 * at + 3 * size] = down_ref[at : at + size, :].T


def pack_ffn(w_gate, w_up, w_down):
    rows, units = w_gate.shape
    return pl.pallas_call(
        pack_ffn_kernel,
        out_shape=jax.ShapeDtypeStruct((rows, 3 * units), BF16),
        cost_estimate=pl.CostEstimate(flops=0, transcendentals=0, bytes_accessed=12 * rows * units),
        compiler_params=params(0),
        name="pack_ffn",
    )(w_gate, w_up, w_down)


def plain_pack_ffn(w_gate, w_up, w_down):
    return jnp.concatenate([w_gate, w_up, w_down.T], axis=1)


def enter_kernel(count, tail, table_ref, tokens_ref, *refs):
    key_refs, value_refs, gain_refs = refs[:count], refs[count : 2 * count], refs[2 * count : tail]
    low_ref, normed_ref, turned_ref, kv_ref, gains_ref = refs[tail:]
    rows = key_refs[0].shape[0]
    slices = table_ref.shape[0]
    size = low_ref.shape[1] // slices
    squares = 0.0
    for k in range(slices):
        start = pl.multiple_of(table_ref[k] * size, size)
        block = tokens_ref[:, pl.ds(start, size)]
        low_ref[:, k * size : (k + 1) * size] = block
        block = block.astype(F32)
        squares = squares + jnp.sum(block * block, axis=-1, keepdims=True)
    scale = lax.rsqrt(squares / low_ref.shape[1] + norm_eps)
    kv = 0.0
    for i in range(count):
        part = slice(i * rows, (i + 1) * rows)
        gains = gain_refs[i][...].astype(F32).T
        gains_ref[:, part] = gains[:8]
        normed = (low_ref[:, part].astype(F32) * scale * gains[0:1]).astype(BF16)
        normed_ref[:, part] = normed
        turned_ref[part, :] = normed.T
        weights = jnp.concatenate([key_refs[i][...], value_refs[i][...]], axis=1)
        kv = kv + nn(normed, weights)
    kv_ref[...] = kv.astype(BF16)


def enter(tokens, table, near, at):
    own, width = tokens.shape
    count, rows = len(near), near[0].shape[0]

    def columns(place):
        return [pl.BlockSpec((rows, HD), lambda i, table_ref: (0, at // HD + place))] * count

    def full(shape):
        return pl.BlockSpec(shape, lambda i, table_ref: (0, 0))

    return pl.pallas_call(
        functools.partial(enter_kernel, count, 3 * count),
        out_shape=(
            jax.ShapeDtypeStruct((own, width), BF16),
            jax.ShapeDtypeStruct((own, width), BF16),
            jax.ShapeDtypeStruct((width, own), BF16),
            jax.ShapeDtypeStruct((own, 2 * HD), BF16),
            jax.ShapeDtypeStruct((8, width), F32),
        ),
        grid_spec=pltpu.PrefetchScalarGridSpec(
            num_scalar_prefetch=1,
            grid=(1,),
            in_specs=[full(tokens.shape)] + columns(0) + columns(1) + columns(2),
            out_specs=[full((own, width))] * 2
            + [full((width, own)), full((own, 2 * HD)), full((8, width))],
        ),
        cost_estimate=pl.CostEstimate(
            flops=4 * own * width * HD, transcendentals=0, bytes_accessed=6_000_000
        ),
        compiler_params=params(),
        name="enter",
    )(jnp.stack(table).astype(jnp.int32), tokens, *near, *near, *near)


def plain_enter(tokens, table, near, at):
    rows = tokens.shape[1] // len(table)
    low = move_columns(tokens, table, rows)
    weights = stack_rows([piece[:, at:] for piece in near])
    gains = weights[:, 2 * HD : 2 * HD + 8].astype(F32).T
    value = low.astype(F32)
    scale = lax.rsqrt(jnp.mean(value * value, axis=-1, keepdims=True) + norm_eps)
    normed = (value * scale * gains[0:1]).astype(BF16)
    return low, normed, normed.T, nn(normed, weights[:, : 2 * HD]).astype(BF16), gains


def pair_up(block):
    return jnp.concatenate([block[:, :HD], block[:, HD:]], axis=0)


def pair_off(block):
    tokens = block.shape[0] // 2
    return jnp.concatenate([block[:tokens], block[tokens:]], axis=1)


def attend_kernel(count, blocks, refs):
    normed_ref, bias_ref, acc_ref = refs[:3]
    kv_refs = refs[3 : 3 + blocks]
    wq_refs = refs[3 + blocks : 3 + blocks + count]
    wo_refs = refs[3 + blocks + count : 3 + blocks + 2 * count]
    query_ref, mixed_ref, total_ref, sum_ref, score_ref = refs[3 + blocks + 2 * count :]
    rows = wq_refs[0].shape[0]
    tokens = normed_ref.shape[0]

    query = sum(
        nn(normed_ref[:, i * rows : (i + 1) * rows], wq_refs[i][...]) for i in range(count)
    ).astype(BF16)
    query_ref[...] = query
    query = pair_up(query)
    peak = None
    for b in range(blocks):
        bias = bias_ref[b * tokens : (b + 1) * tokens, :]
        scores = nt(kv_refs[b][:, :HD], query) * (HD ** (-0.5) * LOG2E)
        scores = scores + jnp.concatenate([bias, bias], axis=1)
        score_ref[b] = scores
        top = jnp.max(scores, axis=0, keepdims=True)
        peak = top if peak is None else jnp.maximum(peak, top)
    sums, mixed = 0.0, 0.0
    for b in range(blocks):
        raised = jnp.exp2(score_ref[b] - peak)
        sums = sums + jnp.sum(raised, axis=0, keepdims=True)
        mixed = mixed + tn(kv_refs[b][:, HD:], raised.astype(BF16))
    total_ref[0] = peak + jnp.log2(sums)
    mixed = pair_off((mixed / sums).T.astype(BF16))
    mixed_ref[...] = mixed

    @pl.when(pl.program_id(0) == 0)
    def _():
        sum_ref[...] = acc_ref[...].astype(F32)

    for i in range(count):
        sum_ref[:, i * rows : (i + 1) * rows] += nt(mixed, wo_refs[i][...])


def attend_block(normed, bias, acc, kv_ring, pieces, many):
    tokens, width = normed.shape
    count, blocks = len(pieces), len(kv_ring)
    rows = pieces[0].shape[0]
    pairs = width // blocks // (2 * HD)
    heads_w = many * width // blocks

    def query_at(j):
        return (0, j // pairs * (2 * pairs) + j % pairs)

    def out_at(j):
        return (0, j // pairs * (2 * pairs) + pairs + j % pairs)

    total = blocks * tokens
    flops = 2 * tokens * heads_w * (2 * width + 2 * total)
    return pl.pallas_call(
        lambda *refs: attend_kernel(count, blocks, refs),
        out_shape=(
            jax.ShapeDtypeStruct((tokens, heads_w), BF16),
            jax.ShapeDtypeStruct((tokens, heads_w), BF16),
            jax.ShapeDtypeStruct((many * pairs, 1, 2 * tokens), F32),
            jax.ShapeDtypeStruct((tokens, width), F32),
        ),
        grid=(many * pairs,),
        in_specs=[whole(normed), whole(bias), whole(acc)]
        + [whole(kv) for kv in kv_ring]
        + [pl.BlockSpec((rows, 2 * HD), query_at)] * count
        + [pl.BlockSpec((rows, 2 * HD), out_at)] * count,
        out_specs=(
            pl.BlockSpec((tokens, 2 * HD), lambda j: (0, j)),
            pl.BlockSpec((tokens, 2 * HD), lambda j: (0, j)),
            pl.BlockSpec((1, 1, 2 * tokens), lambda j: (j, 0, 0)),
            pl.BlockSpec((tokens, width), lambda j: (0, 0)),
        ),
        scratch_shapes=[pltpu.VMEM((blocks, tokens, 2 * tokens), F32)],
        cost_estimate=pl.CostEstimate(
            flops=flops, transcendentals=tokens * total * heads_w // HD, bytes_accessed=14_000_000
        ),
        compiler_params=params(),
        name="attend",
    )(normed, bias, acc, *kv_ring, *pieces, *pieces)


def attend_back_kernel(count, blocks, first, refs):
    branch_ref, bias_ref = refs[:2]
    refs = refs[2:]
    if not first:
        kv_in_ref, normed_in_ref = refs[:2]
        refs = refs[2:]
    query_ref, mixed_ref, total_ref = refs[:3]
    refs = refs[3:]
    kv_refs, refs = refs[:blocks], refs[blocks:]
    wq_refs, refs = refs[:count], refs[count:]
    wo_refs, refs = refs[:count], refs[count:]
    query_grad_ref, kv_grad_ref, normed_grad_ref = refs
    rows = wq_refs[0].shape[0]
    tokens = branch_ref.shape[0]
    scale = HD ** (-0.5)

    @pl.when(pl.program_id(0) == 0)
    def _():
        if first:
            kv_grad_ref[...] = jnp.zeros_like(kv_grad_ref)
            normed_grad_ref[...] = jnp.zeros_like(normed_grad_ref)
        else:
            kv_grad_ref[...] = kv_in_ref[...]
            normed_grad_ref[...] = normed_in_ref[...]

    grad = sum(
        nn(branch_ref[:, i * rows : (i + 1) * rows], wo_refs[i][...]) for i in range(count)
    ).astype(BF16)
    product = pair_up(grad.astype(F32) * mixed_ref[...].astype(F32))
    inner = jnp.sum(product.T, axis=0, keepdims=True)
    grad = pair_up(grad)
    query = pair_up(query_ref[...])
    totals = total_ref[0]
    query_grad = 0.0
    for b in range(blocks):
        keys, values = kv_refs[b][:, :HD], kv_refs[b][:, HD:]
        bias = bias_ref[b * tokens : (b + 1) * tokens, :]
        scores = nt(keys, query) * (scale * LOG2E) + jnp.concatenate([bias, bias], axis=1)
        shares = jnp.exp2(scores - totals)
        score_grad = (shares * (nt(values, grad) - inner)).astype(BF16)
        query_grad = query_grad + tn(keys, score_grad)
        at = slice(b * tokens, (b + 1) * tokens)
        kv_grad_ref[at, :HD] += scale * nn(score_grad, query)
        kv_grad_ref[at, HD:] += nn(shares.astype(BF16), grad)
    query_grad = pair_off((scale * query_grad).T.astype(BF16))
    query_grad_ref[...] = query_grad
    for i in range(count):
        normed_grad_ref[:, i * rows : (i + 1) * rows] += nt(query_grad, wq_refs[i][...])


def attend_back_block(branch, bias, sums, query, mixed, total, kv_ring, pieces, at):
    tokens, width = branch.shape
    first = sums is None
    count, blocks = len(pieces), len(kv_ring)
    rows = pieces[0].shape[0]
    heads_w = width // blocks
    pairs = heads_w // (2 * HD)
    base = 2 * pairs * at
    two = pl.BlockSpec((tokens, 2 * HD), lambda j: (0, j))
    kept = pl.BlockSpec((tokens, 2 * HD), lambda j: (0, pairs * at + j))
    sums = [] if first else list(sums)
    keys = blocks * tokens
    return pl.pallas_call(
        lambda *refs: attend_back_kernel(count, blocks, first, refs),
        out_shape=(
            jax.ShapeDtypeStruct((tokens, heads_w), BF16),
            jax.ShapeDtypeStruct((keys, 2 * HD), F32),
            jax.ShapeDtypeStruct((tokens, width), F32),
        ),
        grid=(pairs,),
        in_specs=[whole(branch), whole(bias)]
        + [whole(item) for item in sums]
        + [kept, kept, pl.BlockSpec((1, 1, 2 * tokens), lambda j: (pairs * at + j, 0, 0))]
        + [whole(kv) for kv in kv_ring]
        + [pl.BlockSpec((rows, 2 * HD), lambda j: (0, base + j))] * count
        + [pl.BlockSpec((rows, 2 * HD), lambda j: (0, base + pairs + j))] * count,
        out_specs=(
            two,
            pl.BlockSpec((keys, 2 * HD), lambda j: (0, 0)),
            pl.BlockSpec((tokens, width), lambda j: (0, 0)),
        ),
        cost_estimate=pl.CostEstimate(
            flops=2 * tokens * heads_w * (2 * width + 5 * keys),
            transcendentals=tokens * keys * heads_w // HD,
            bytes_accessed=16_000_000,
        ),
        compiler_params=params(),
        name="attend_back",
    )(branch, bias, *sums, query, mixed, total, *kv_ring, *pieces, *pieces)


def attend_weights_kernel(sends, keeps, refs):
    outs = refs[len(refs) - sends - keeps :]

    def work(normed_ref, branch_ref, query_grad_ref, mixed_ref, out_ref, come_ref):
        half = query_grad_ref.shape[1]
        left = nn(normed_ref[...], query_grad_ref[...])
        right = nn(branch_ref[...], mixed_ref[...])
        if come_ref is not None:
            come = come_ref[...].astype(F32)
            left, right = left + come[:, :half], right + come[:, half:]
        out_ref[:, :half] = left.astype(BF16)
        out_ref[:, half:] = right.astype(BF16)

    if sends:
        work(*refs[:4], outs[0], None)
    if keeps:
        refs = refs[4 * sends :]
        work(*refs[:4], outs[-1], refs[4])


def attend_weights(normed, branch, send=None, keep=None):
    width, tokens = normed.shape
    steps = 2
    rows = width // 2 // steps
    specs, arrays, out_shape = [], [], []
    for item, first in ((send, steps), (keep, 0)):
        if item is None:
            continue
        query_grad, mixed, at, *come = item
        heads_w = query_grad.shape[1]
        left = pl.BlockSpec((rows, tokens), lambda i, first=first: (first + i, 0))
        right = pl.BlockSpec(
            (tokens, heads_w), lambda i, at=at: (0, at), pipeline_mode=pl.Buffered(1)
        )
        out = pl.BlockSpec((rows, 2 * heads_w), lambda i: (i, 0))
        specs += [left, left, whole(query_grad), right] + [out] * len(come)
        arrays += [normed, branch, query_grad, mixed, *come]
        out_shape.append(jax.ShapeDtypeStruct((width // 2, 2 * heads_w), BF16))
    return pl.pallas_call(
        lambda *refs: attend_weights_kernel(int(send is not None), int(keep is not None), refs),
        out_shape=out_shape,
        grid=(steps,),
        in_specs=specs,
        out_specs=[out] * len(out_shape),
        cost_estimate=pl.CostEstimate(
            flops=2 * tokens * width * heads_w * len(out_shape),
            transcendentals=0,
            bytes_accessed=6_000_000,
        ),
        compiler_params=params(),
        name="attend_weights",
    )(*arrays)


def ffn_kernel(count, steps, last, refs):
    normed_ref, grad_ref = refs[:2]
    w_refs = refs[2 : 2 + count]
    act_ref, part_ref, back_ref, part_acc, back_acc = refs[2 + count :]
    rows = w_refs[0].shape[0]
    step = pl.program_id(0)

    @pl.when(step == 0)
    def _():
        part_acc[...] = jnp.zeros_like(part_acc)
        back_acc[...] = jnp.zeros_like(back_acc)

    def work(tile):
        parts = [slice(i * rows, (i + 1) * rows) for i in range(count)]
        gate = sum(nn(normed_ref[:, p], w[:, :tile]) for p, w in zip(parts, w_refs))
        upward = sum(nn(normed_ref[:, p], w[:, tile : 2 * tile]) for p, w in zip(parts, w_refs))
        hidden_grad = sum(
            nn(grad_ref[:, p], w[:, 2 * tile : 3 * tile]) for p, w in zip(parts, w_refs)
        )
        sigma = jax.nn.sigmoid(gate)
        silu = gate * sigma
        hidden = (silu * upward).astype(BF16)
        up_grad = (hidden_grad * silu).astype(BF16)
        gate_grad = (hidden_grad * upward * sigma * (1.0 + gate * (1.0 - sigma))).astype(BF16)
        act_ref[:, :tile] = gate_grad
        act_ref[:, tile : 2 * tile] = up_grad
        act_ref[:, 2 * tile : 3 * tile] = hidden
        both = jnp.concatenate([gate_grad, up_grad], axis=1)
        for p, w in zip(parts, w_refs):
            part_acc[:, p] += nt(hidden, w[:, 2 * tile : 3 * tile])
            back_acc[:, p] += nt(both, w[:, : 2 * tile])

    if steps > 1:
        pl.when(step < steps - 1)(lambda: work(TILE))
    pl.when(step == steps - 1)(lambda: work(last))

    @pl.when(step == steps - 1)
    def _():
        part_ref[...] = part_acc[...].astype(BF16)
        back_ref[...] = back_acc[...].astype(BF16)


def ffn_block(normed, grad, pieces):
    tokens, width = normed.shape
    count, rows = len(pieces), pieces[0].shape[0]
    units = pieces[0].shape[1] // 3
    steps = -(-units // TILE)
    last = units - (steps - 1) * TILE
    full = pl.BlockSpec((tokens, width), lambda j: (0, 0))
    out = jax.ShapeDtypeStruct((tokens, width), BF16)
    return pl.pallas_call(
        lambda *refs: ffn_kernel(count, steps, last, refs),
        out_shape=(jax.ShapeDtypeStruct((tokens, 3 * units), BF16), out, out),
        grid=(steps,),
        in_specs=[whole(normed), whole(grad)]
        + [pl.BlockSpec((rows, 3 * TILE), lambda j: (0, j))] * count,
        out_specs=(pl.BlockSpec((tokens, 3 * TILE), lambda j: (0, j)), full, full),
        scratch_shapes=[pltpu.VMEM((tokens, width), F32)] * 2,
        cost_estimate=pl.CostEstimate(
            flops=12 * tokens * width * units,
            transcendentals=tokens * units,
            bytes_accessed=6 * width * units + 12 * tokens * width,
        ),
        compiler_params=params(),
        name="ffn_block",
    )(normed, grad, *pieces)


def ffn_weights_kernel(blocks, count, steps, last, adds, refs):
    normed_refs, refs = refs[:blocks], refs[blocks:]
    grad_refs, refs = refs[:blocks], refs[blocks:]
    act_refs, refs = refs[:blocks], refs[blocks:]
    added_refs, out_refs = refs[: adds * count], refs[adds * count :]

    def work(piece, tile):
        both = sum(tn(normed_refs[b][...], act_refs[b][:, : 2 * tile]) for b in range(blocks))
        down = sum(
            tn(grad_refs[b][...], act_refs[b][:, 2 * tile : 3 * tile]) for b in range(blocks)
        )
        for k in range(adds):
            added = added_refs[k * count + piece]
            both = both + added[:, : 2 * tile].astype(F32)
            down = down + added[:, 2 * tile : 3 * tile].astype(F32)
        out_refs[piece][:, : 2 * tile] = both.astype(BF16)
        out_refs[piece][:, 2 * tile : 3 * tile] = down.astype(BF16)

    turn, step = pl.program_id(0), pl.program_id(1)
    for at in range(count):
        if steps > 1:
            pl.when((turn == at) & (step < steps - 1))(functools.partial(work, at, TILE))
        pl.when((turn == at) & (step == steps - 1))(functools.partial(work, at, last))


def ffn_weights(normed_ring, grad_ring, acts, first, count, rows, added=()):
    tokens = normed_ring[0].shape[0]
    units = acts[0].shape[1] // 3
    blocks = len(acts)
    steps = -(-units // TILE)
    last = units - (steps - 1) * TILE
    left = pl.BlockSpec((tokens, rows), lambda i, j: (0, first + i))

    def piece_spec(piece, block):
        def place(i, j):
            return (block, jnp.where(i < piece, 0, jnp.where(i > piece, steps - 1, j)))

        return pl.BlockSpec((rows, 3 * TILE), place)

    wide = [piece_spec(piece, 0) for piece in range(count)]
    specs, arrays = [], []
    for item in added:
        if isinstance(item, (list, tuple)):
            specs, arrays = specs + wide, arrays + list(item)
        else:
            specs = specs + [piece_spec(piece, piece) for piece in range(count)]
            arrays = arrays + [item] * count
    return pl.pallas_call(
        lambda *refs: ffn_weights_kernel(blocks, count, steps, last, len(added), refs),
        out_shape=[jax.ShapeDtypeStruct((rows, 3 * units), BF16)] * count,
        grid=(count, steps),
        in_specs=[left] * (2 * blocks)
        + [pl.BlockSpec((tokens, 3 * TILE), lambda i, j: (0, j))] * blocks
        + specs,
        out_specs=wide,
        cost_estimate=pl.CostEstimate(
            flops=6 * tokens * blocks * count * rows * units,
            transcendentals=0,
            bytes_accessed=6 * tokens * blocks * units * count + 6 * count * rows * units,
        ),
        compiler_params=params(2),
        name="ffn_weights",
    )(*normed_ring, *grad_ring, *acts, *arrays)


def turn_kernel(come_ref, part_ref, given_ref, value_ref, gain_ref, *refs):
    after_ref, low_ref, turned_ref, term_ref = refs
    value = value_ref[...]
    grad = come_ref[...].astype(F32) + part_ref[...].astype(F32)
    scale = lax.rsqrt(jnp.mean(value * value, axis=-1, keepdims=True) + norm_eps)
    term_ref[...] = jnp.sum(grad * value * scale, axis=0, keepdims=True)
    after = given_ref[...].astype(F32) + norm_back(value, scale, gain_ref[1:2, :], grad)
    after_ref[...] = after
    low = after.astype(BF16)
    low_ref[...] = low
    turned_ref[...] = low.T


def turn(come, part, given, value, gains):
    own, width = value.shape
    return pl.pallas_call(
        turn_kernel,
        out_shape=(
            jax.ShapeDtypeStruct((own, width), F32),
            jax.ShapeDtypeStruct((own, width), BF16),
            jax.ShapeDtypeStruct((width, own), BF16),
            jax.ShapeDtypeStruct((1, width), F32),
        ),
        cost_estimate=pl.CostEstimate(
            flops=0, transcendentals=0, bytes_accessed=20 * own * width
        ),
        compiler_params=params(0),
        name="turn",
    )(come, part, given, value, gains)


def plain_turn(come, part, given, value, gains):
    grad = come.astype(F32) + part.astype(F32)
    scale = lax.rsqrt(jnp.mean(value * value, axis=-1, keepdims=True) + norm_eps)
    term = jnp.sum(grad * value * scale, axis=0, keepdims=True)
    after = given.astype(F32) + norm_back(value, scale, gains[1:2], grad)
    low = after.astype(BF16)
    return after, low, low.T, term


def leave_kernel(come_count, count, slices, table_ref, *refs):
    kv_ref, refs = refs[0], refs[1:]
    come_refs, refs = refs[:come_count], refs[come_count:]
    d_key_ref, d_value_ref, grad_ref, normed_ref, low_ref, after_ref, gain_ref, ffn_ref = refs[:8]
    refs = refs[8:]
    key_refs, value_refs, refs = refs[:count], refs[count : 2 * count], refs[2 * count :]
    out_ref, keep_ref, send_ref, total_ref = refs
    rows = key_refs[0].shape[0]
    width = low_ref.shape[1]
    size = width // slices
    kv_grad = kv_ref[...]
    for ref in come_refs:
        kv_grad = kv_grad + ref[...].astype(F32)
    given = jnp.concatenate([d_key_ref[...], d_value_ref[...]], axis=1)
    kv_grad = (kv_grad + given.astype(F32)).astype(BF16)
    squares, inner = 0.0, 0.0
    for i in range(count):
        part = slice(i * rows, (i + 1) * rows)
        weights = jnp.concatenate([key_refs[i][...], value_refs[i][...]], axis=1)
        total = grad_ref[:, part] + nt(kv_grad, weights)
        total_ref[:, part] = total
        value = low_ref[:, part].astype(F32)
        squares = squares + jnp.sum(value * value, axis=-1, keepdims=True)
        inner = inner + jnp.sum(total * gain_ref[0:1, part] * value, axis=-1, keepdims=True)
    scale = lax.rsqrt(squares / width + norm_eps)
    shrink = scale * scale * scale * (inner / width)
    for i in range(count):
        part = slice(i * rows, (i + 1) * rows)
        total, value = total_ref[:, part], low_ref[:, part].astype(F32)
        gain_term = jnp.sum(total * value * scale, axis=0, keepdims=True)
        terms = jnp.concatenate(
            [gain_term, ffn_ref[:, part], jnp.zeros((HD - 2, rows), F32)], axis=0
        )
        block = jnp.concatenate([tn(normed_ref[:, part], kv_grad), terms.T], axis=1).astype(BF16)
        half = count // 2
        ref = keep_ref if i < half else send_ref
        ref[(i % half) * rows : (i % half + 1) * rows, :] = block
    for k in range(slices):
        part = slice(k * size, (k + 1) * size)
        value = low_ref[:, part].astype(F32)
        grad = scale * (total_ref[:, part] * gain_ref[0:1, part]) - value * shrink
        start = pl.multiple_of(table_ref[k] * size, size)
        out_ref[:, pl.ds(start, size)] = after_ref[:, part] + grad


def leave(table, kv_acc, kv_come, d_keys, d_values, normed_grad, normed, low, after_grad, gains,
          ffn_term, near, at):
    own, width = normed.shape
    count, rows = len(near), near[0].shape[0]

    def columns(place):
        return [pl.BlockSpec((rows, HD), lambda i, table_ref: (0, at // HD + place))] * count

    def full(shape):
        return pl.BlockSpec(shape, lambda i, table_ref: (0, 0))

    given = [*kv_come, d_keys, d_values, normed_grad, normed, low, after_grad, gains, ffn_term]
    half = jax.ShapeDtypeStruct((width // 2, 3 * HD), BF16)
    return pl.pallas_call(
        functools.partial(leave_kernel, len(kv_come), count, len(table)),
        out_shape=(jax.ShapeDtypeStruct((own, width), F32), half, half),
        grid_spec=pltpu.PrefetchScalarGridSpec(
            num_scalar_prefetch=1,
            grid=(1,),
            in_specs=[full((own, 2 * HD))]
            + [full(item.shape) for item in given]
            + columns(0)
            + columns(1),
            out_specs=[full((own, width)), full(half.shape), full(half.shape)],
            scratch_shapes=[pltpu.VMEM((own, width), F32)],
        ),
        cost_estimate=pl.CostEstimate(
            flops=8 * own * width * HD, transcendentals=0, bytes_accessed=16_000_000
        ),
        compiler_params=params(),
        name="leave",
    )(jnp.stack(table).astype(jnp.int32), kv_acc, *given, *near, *near)


def leave_out_kernel(slices, table_ref, after_ref, come_ref, part_ref, out_ref):
    size = after_ref.shape[1] // slices
    for k in range(slices):
        part = slice(k * size, (k + 1) * size)
        total = come_ref[:, part].astype(F32) + part_ref[:, part].astype(F32)
        start = pl.multiple_of(table_ref[k] * size, size)
        out_ref[:, pl.ds(start, size)] = (after_ref[:, part] + total).astype(BF16)


def leave_out(table, after_attn, come, part):
    def full(shape):
        return pl.BlockSpec(shape, lambda i, table_ref: (0, 0))

    return pl.pallas_call(
        functools.partial(leave_out_kernel, len(table)),
        out_shape=jax.ShapeDtypeStruct(after_attn.shape, BF16),
        grid_spec=pltpu.PrefetchScalarGridSpec(
            num_scalar_prefetch=1,
            grid=(1,),
            in_specs=[full(after_attn.shape)] * 3,
            out_specs=full(after_attn.shape),
        ),
        cost_estimate=pl.CostEstimate(flops=0, transcendentals=0, bytes_accessed=8_000_000),
        compiler_params=params(),
        name="leave_out",
    )(jnp.stack(table).astype(jnp.int32), after_attn, come, part)


def unpack_ffn_kernel(keep_ref, come_ref, gate_ref, up_ref, down_ref):
    units = gate_ref.shape[1]
    for at in range(0, units, TILE):
        size = min(TILE, units - at)

        def take(k):
            cols = slice(3 * at + k * size, 3 * at + (k + 1) * size)
            return keep_ref[:, cols].astype(F32) + come_ref[:, cols].astype(F32)

        gate_ref[:, at : at + size] = take(0)
        up_ref[:, at : at + size] = take(1)
        down_ref[at : at + size, :] = take(2).T


def unpack_ffn(keep, come):
    rows, units = keep.shape[0], keep.shape[1] // 3
    flat = jax.ShapeDtypeStruct((rows, units), F32)
    return pl.pallas_call(
        unpack_ffn_kernel,
        out_shape=(flat, flat, jax.ShapeDtypeStruct((units, rows), F32)),
        cost_estimate=pl.CostEstimate(flops=0, transcendentals=0, bytes_accessed=24 * rows * units),
        compiler_params=params(0),
        name="unpack_ffn",
    )(keep, come)


def unpack_attn_kernel(moving_ref, keep_ref, come_ref, query_ref, out_ref):
    heads_w = query_ref.shape[1]
    total = keep_ref[...].astype(F32) + come_ref[...].astype(F32) + moving_ref[...].astype(F32)
    query_ref[...] = total[:, :heads_w]
    out_ref[...] = total[:, heads_w:].T


def unpack_attn(moving, keep, come):
    rows, heads_w = keep.shape[0], keep.shape[1] // 2
    return pl.pallas_call(
        unpack_attn_kernel,
        out_shape=(
            jax.ShapeDtypeStruct((rows, heads_w), F32),
            jax.ShapeDtypeStruct((heads_w, rows), F32),
        ),
        cost_estimate=pl.CostEstimate(flops=0, transcendentals=0, bytes_accessed=4_000_000),
        compiler_params=params(0),
        name="unpack_attn",
    )(moving, keep, come)


def place_kv_kernel(count, place_ref, *refs):
    kv_refs, (key_ref, value_ref) = refs[:count], refs[count:]
    own = kv_refs[0].shape[0]
    for r in range(count):
        start = pl.multiple_of(place_ref[r] * own, own)
        key_ref[pl.ds(start, own), :] = kv_refs[r][:, :HD]
        value_ref[pl.ds(start, own), :] = kv_refs[r][:, HD:]


def place_kv(places, kv_ring):
    own, count = kv_ring[0].shape[0], len(kv_ring)
    out = jax.ShapeDtypeStruct((count * own, HD), BF16)
    return pl.pallas_call(
        functools.partial(place_kv_kernel, count),
        out_shape=(out, out),
        grid_spec=pltpu.PrefetchScalarGridSpec(
            num_scalar_prefetch=1,
            grid=(1,),
            in_specs=[pl.BlockSpec((own, 2 * HD), lambda i, place_ref: (0, 0))] * count,
            out_specs=[pl.BlockSpec(out.shape, lambda i, place_ref: (0, 0))] * 2,
        ),
        cost_estimate=pl.CostEstimate(flops=0, transcendentals=0, bytes_accessed=1_600_000),
        compiler_params=params(),
        name="place_kv",
    )(jnp.stack(places).astype(jnp.int32), *kv_ring)


def plain_attend_block(normed, bias, acc, kv_ring, pieces, many):
    step = normed.shape[1] // len(kv_ring)
    heads_w = many * step
    weights = stack_rows(pieces)
    blocks = [weights[:, at * step : (at + 1) * step] for at in range(2 * many)]
    weights = jnp.concatenate(blocks[::2] + blocks[1::2], axis=1)
    kv = stack_rows(kv_ring)
    query = nn(normed, weights[:, :heads_w]).astype(BF16)
    mixed, totals = [], []
    for head in range(heads_w // HD):
        scores = nt(kv[:, :HD], query[:, head * HD : (head + 1) * HD]) * (HD ** (-0.5)) + bias
        peak = jnp.max(scores, axis=0, keepdims=True)
        raised = jnp.exp(scores - peak)
        sums = jnp.sum(raised, axis=0, keepdims=True)
        mixed.append(tn((raised / sums).astype(BF16), kv[:, HD:]).astype(BF16))
        totals.append(peak + jnp.log(sums))
    mixed = jnp.concatenate(mixed, axis=1)
    return query, mixed, jnp.concatenate(totals, axis=0), acc + nt(mixed, weights[:, heads_w:])


def plain_attend_back_block(branch, bias, sums, query, mixed, total, kv_ring, pieces, at):
    heads_w = branch.shape[1] // len(kv_ring)
    weights = stack_rows(pieces)[:, 2 * at * heads_w : 2 * (at + 1) * heads_w]
    query = query[:, at * heads_w : (at + 1) * heads_w]
    total = total[at * heads_w // HD : (at + 1) * heads_w // HD]
    kv = stack_rows(kv_ring)
    keys, values = kv[:, :HD], kv[:, HD:]
    scale = HD ** (-0.5)
    grad = nn(branch, weights[:, heads_w:]).astype(BF16)
    key_acc, value_acc, query_grad = 0.0, 0.0, []
    for head in range(heads_w // HD):
        cols = slice(head * HD, (head + 1) * HD)
        scores = nt(keys, query[:, cols]) * scale + bias
        shares = jnp.exp(scores - total[head : head + 1])
        share_grad = nt(values, grad[:, cols])
        value_acc = value_acc + nn(shares.astype(BF16), grad[:, cols])
        inner = jnp.sum(shares * share_grad, axis=0, keepdims=True)
        score_grad = (shares * (share_grad - inner)).astype(BF16)
        query_grad.append((scale * tn(score_grad, keys)).astype(BF16))
        key_acc = key_acc + scale * nn(score_grad, query[:, cols])
    query_grad = jnp.concatenate(query_grad, axis=1)
    kv_grad = jnp.concatenate([key_acc, value_acc], axis=1)
    normed_grad = nt(query_grad, weights[:, :heads_w])
    if sums is not None:
        kv_grad, normed_grad = kv_grad + sums[0], normed_grad + sums[1]
    return query_grad, kv_grad, normed_grad


def plain_attend_weights(normed, branch, send=None, keep=None):
    half = normed.shape[0] // 2
    outs = []
    for item, first in ((send, half), (keep, 0)):
        if item is None:
            continue
        query_grad, mixed, at, *come = item
        heads_w = query_grad.shape[1]
        mixed = mixed[:, at * heads_w : (at + 1) * heads_w]
        part = slice(first, first + half)
        out = jnp.concatenate([nn(normed[part], query_grad), nn(branch[part], mixed)], axis=1)
        outs.append((out + come[0].astype(F32) if come else out).astype(BF16))
    return outs


def plain_ffn_block(normed, grad, pieces):
    weights = stack_rows(pieces)
    units = weights.shape[1] // 3
    gate_w, up_w, down_w = jnp.split(weights, 3, axis=1)
    gate = nn(normed, gate_w)
    upward = nn(normed, up_w)
    sigma = jax.nn.sigmoid(gate)
    hidden = (gate * sigma * upward).astype(BF16)
    part = nt(hidden, down_w).astype(BF16)
    hidden_grad = nn(grad, down_w)
    gate_grad = (hidden_grad * upward * sigma * (1.0 + gate * (1.0 - sigma))).astype(BF16)
    up_grad = (hidden_grad * gate * sigma).astype(BF16)
    back = (nt(gate_grad, gate_w) + nt(up_grad, up_w)).astype(BF16)
    return jnp.concatenate([gate_grad, up_grad, hidden], axis=1), part, back


def plain_ffn_weights(normed_ring, grad_ring, acts, first, count, rows, added=()):
    normed, grad, acts = stack_rows(normed_ring), stack_rows(grad_ring), stack_rows(acts)
    units = acts.shape[1] // 3
    pieces = []
    for piece in range(count):
        cols = slice((first + piece) * rows, (first + piece + 1) * rows)
        out = [tn(normed[:, cols], acts[:, : 2 * units]), tn(grad[:, cols], acts[:, 2 * units :])]
        out = jnp.concatenate(out, axis=1)
        for item in added:
            single = isinstance(item, (list, tuple))
            out = out + (item[piece] if single else item[piece * rows :][:rows]).astype(F32)
        pieces.append(out.astype(BF16))
    return pieces


def plain_leave(table, kv_acc, kv_come, d_keys, d_values, normed_grad, normed, low, after_grad,
                gains, ffn_term, near, at):
    own, width = normed.shape
    kv_grad = kv_acc[:own]
    for come in kv_come:
        kv_grad = kv_grad + come.astype(F32)
    kv_grad = kv_grad + jnp.concatenate([d_keys, d_values], axis=1).astype(F32)
    kv_grad = kv_grad.astype(BF16)
    kv_w = stack_rows([piece[:, at : at + 2 * HD] for piece in near])
    normed_grad = normed_grad + nt(kv_grad, kv_w)
    value = low.astype(F32)
    scale = lax.rsqrt(jnp.mean(value * value, axis=-1, keepdims=True) + norm_eps)
    grad = after_grad + norm_back(value, scale, gains[0:1], normed_grad)
    gain_term = jnp.sum(normed_grad * value * scale, axis=0)
    small = [tn(normed, kv_grad), gain_term[:, None], ffn_term.T, jnp.zeros((width, HD - 2), F32)]
    small = jnp.concatenate(small, axis=1).astype(BF16)
    grad = move_columns(grad, table, width // len(table), back=True)
    return grad, small[: width // 2], small[width // 2 :]


def plain_leave_out(table, after_attn, come, part):
    out = (after_attn + (come.astype(F32) + part.astype(F32))).astype(BF16)
    return move_columns(out, table, out.shape[1] // len(table), back=True)


def plain_unpack_ffn(keep, come):
    gate, up, down = jnp.split(keep.astype(F32) + come.astype(F32), 3, axis=1)
    return gate, up, down.T


def plain_unpack_attn(moving, keep, come):
    total = keep.astype(F32) + come.astype(F32) + moving.astype(F32)
    heads_w = total.shape[1] // 2
    return total[:, :heads_w], total[:, heads_w:].T


def plain_place_kv(places, kv_ring):
    own = kv_ring[0].shape[0]
    out = jnp.zeros((len(kv_ring) * own, 2 * HD), BF16)
    for start, block in zip(places, kv_ring):
        out = lax.dynamic_update_slice_in_dim(out, block, start * own, axis=0)
    return out[:, :HD], out[:, HD:]


KERNELS = (
    pack_attn,
    pack_ffn,
    enter,
    attend_block,
    attend_back_block,
    attend_weights,
    ffn_block,
    ffn_weights,
    turn,
    leave,
    leave_out,
    unpack_ffn,
    unpack_attn,
    place_kv,
)
PLAIN = (
    plain_pack_attn,
    plain_pack_ffn,
    plain_enter,
    plain_attend_block,
    plain_attend_back_block,
    plain_attend_weights,
    plain_ffn_block,
    plain_ffn_weights,
    plain_turn,
    plain_leave,
    plain_leave_out,
    plain_unpack_ffn,
    plain_unpack_attn,
    plain_place_kv,
)


def on_device(
    ndp,
    nz,
    tokens,
    norm_attn,
    w_query,
    w_key,
    w_value,
    w_out,
    norm_ffn,
    w_gate,
    w_up,
    w_down,
    segment_ids,
    parents,
    positions,
    d_out,
    d_keys,
    d_values,
):
    me = lax.axis_index("dp")
    place_z = lax.axis_index("tensor")
    table = slice_table(me, ndp)
    own, width = tokens.shape[0], tokens.shape[1]
    rows = width // ndp
    heads_w = w_query.shape[1]
    units = w_gate.shape[1]
    fits = own % HD == 0 and rows % HD == 0 and units % HD == 0 and heads_w % (2 * HD) == 0
    (
        do_pack_attn,
        do_pack_ffn,
        do_enter,
        do_attend,
        do_attend_back,
        do_attend_weights,
        do_ffn,
        do_ffn_weights,
        do_turn,
        do_leave,
        do_leave_out,
        do_unpack_ffn,
        do_unpack_attn,
        do_place_kv,
    ) = KERNELS if fits else PLAIN

    gains = jnp.concatenate(
        [norm_attn[:, None], norm_ffn[:, None], jnp.zeros((rows, HD - 2), BF16)], axis=1
    )
    first_up = lookup(segment_ids, parents)
    second_up = lookup(first_up, parents)

    def own_rows(vector):
        return lax.dynamic_slice_in_dim(vector, place_z * own, own, axis=0)

    def ring_rows(vector):
        return jnp.concatenate(
            [
                lax.dynamic_slice_in_dim(vector, ((place_z - r) % nz) * own, own, axis=0)
                for r in range(nz)
            ],
            axis=0,
        )

    key_segment, key_place = ring_rows(segment_ids)[:, None], ring_rows(positions)[:, None]
    linked = (
        (key_segment == own_rows(segment_ids)[None])
        | (key_segment == own_rows(first_up)[None])
        | (key_segment == own_rows(second_up)[None])
    )
    bias = jnp.where(linked & (key_place <= own_rows(positions)[None]), 0.0, -1e30).astype(F32)

    near_item, ring_item = do_pack_attn(w_query, w_out, w_key, w_value, gains)
    near_flow = Flow("attn_w_near", gather_steps(near_item, ndp))
    attn_flow = Flow("attn_w_ring", ring_gather_steps(ring_item, nz))
    grad_low = move_columns(d_out, table, rows)
    ffn_pack = do_pack_ffn(w_gate, w_up, w_down)
    grad_low, bias, ffn_pack = meet([grad_low, bias, ffn_pack], [near_flow, attn_flow])
    near_flow.go(len(bit_orders(ndp)[0]) - 2)
    grad_low, ffn_pack = meet([grad_low, ffn_pack], [near_flow, attn_flow])
    ffn_flow = Flow("ffn_w", gather_steps(ffn_pack, ndp, True))
    near = list(near_flow.finish())
    near = meet(near, [attn_flow])
    tokens_low, normed, normed_turned, kv_own, gain_rows = do_enter(
        tokens, table, near, 2 * heads_w
    )
    ffn_gain = gain_rows[1:2]
    kv_ring = [kv_own] + [scoped("kv", shift, kv_own, nz, by) for by in range(1, nz)]
    *kv_ring, grad_low = meet(kv_ring + [grad_low], [attn_flow])
    attn_ring = attn_flow.finish()[1:]
    far_flow = Flow("attn_w_far", gather_steps(jnp.concatenate(attn_ring, axis=1), ndp))
    grad_flow = Flow("grad_ring", ring_gather_steps(grad_low, nz))

    normed, *kv_ring = meet([normed] + kv_ring, [far_flow, ffn_flow])
    normed, *ffn_flow.held = tie(normed, *ffn_flow.held)
    *kept_near, after_attn = do_attend(normed, bias, tokens_low, kv_ring, near, 1)
    grad_first = grad_flow.held[0]
    (after_attn,) = meet([after_attn], [grad_flow])
    (after_attn,) = meet([after_attn], [far_flow, ffn_flow])
    far = far_flow.finish()
    *kept_far, after_attn = do_attend(normed, bias, after_attn, kv_ring, far, nz - 1)
    grad_ring = [grad_low, grad_first]
    ffn_scale = lax.rsqrt(jnp.mean(after_attn * after_attn, axis=-1, keepdims=True) + norm_eps)
    ffn_own = (after_attn * ffn_scale * ffn_gain).astype(BF16)

    ring_flow = Flow("ffn_ring", ring_gather_steps(ffn_own, nz))
    ffn_ring, acts, parts, backs = meet([ffn_own], [ffn_flow, grad_flow]), [], [], []
    ffn_w = ffn_flow.finish()
    early = nz // 2 + 1
    backs_flow = None
    for block in range(nz):
        if block > 0:
            come, acts[-1], *ring_flow.held = tie(ring_flow.held[0], acts[-1])
            ring_flow.held = [come]
            ring_flow.go()
            ffn_ring.append(come)
        if block == early:
            first = (ffn_ring[:early], grad_ring[:early], acts[:early])
            (send,) = do_ffn_weights(*first, 1, 1, width // 2)
            kept = do_ffn_weights(*first, 0, 2, width // 4)
            ffn_ring[-1], send, *kept = tie(ffn_ring[-1], send, *kept)
        elif block > early:
            (ffn_ring[-1],) = meet(ffn_ring[-1:], [backs_flow])
        if block == 2:
            grad_ring = grad_flow.finish()
        act, part, back = do_ffn(ffn_ring[block], grad_ring[block], ffn_w)
        acts.append(act)
        parts.append(part)
        backs.append(back)
        if block == 1:
            backs_flow = Flow("backs", ring_steps(backs, nz, acts))

    acts[-1], *backs_flow.held = tie(acts[-1], *backs_flow.held)
    backs_flow.go()
    rest = (ffn_ring[early:], grad_ring[early:], acts[early:])
    (send,) = do_ffn_weights(*rest, 1, 1, width // 2, ([send],))
    parts[1], send = meet([parts[1], send], [backs_flow])
    come = scoped("ffn_g", core_swap, send, ndp)
    made = do_ffn_weights(*rest, 0, 2, width // 4, (kept, come))
    tied = list(tie(*made, *backs_flow.held))
    made, backs_flow.held = tied[: len(made)], tied[len(made) :]
    after_grad, branch, branch_turned, ffn_term = do_turn(
        *backs_flow.finish(), grad_low, after_attn, gain_rows
    )
    part_flow = Flow("parts", ring_steps(parts, nz))
    ffn_flow = Flow("ffn_g", chip_steps(*made, ndp))

    order = list(range(1, nz)) + [0]
    flows = [None] * nz
    done = [None] * nz
    sums = None
    for turn, block in enumerate(order):
        stored, pieces, at = (kept_far, far, block - 1) if block else (kept_near, near, 0)
        if turn > 0:
            due = [part_flow] + ([flows[nz - 3]] if turn == nz - 1 else [])
            branch, *made = meet([branch, *made], due)
            if turn == nz - 1:
                for place in range(1, nz - 2):
                    done[place] = add_low(*flows[place].finish())
                ring_flow = Flow("attn_g_ring", ring_steps(done, nz))
                for _ in range(nz - 4):
                    ring_flow.go()
            sent = scoped(f"attn_g_{order[turn - 1]}", core_swap, made[0], ndp)
            if turn > 1:
                flow = Flow(f"attn_g_{order[turn - 2]}", chip_steps(*made[1:], ndp))
                flows[order[turn - 2]] = flow
        query_grad, kv_acc, normed_grad = do_attend_back(
            branch, bias, sums, *stored, kv_ring, pieces, at
        )
        sums = (kv_acc, normed_grad)
        due = [flow for flow in flows if flow is not None]
        due += [ffn_flow] if turn else []
        this = (query_grad, stored[1], at)
        if turn == 0:
            made = do_attend_weights(normed_turned, branch_turned, this)
        else:
            waiting = [flow, ring_flow] if turn == nz - 1 else []
            due = [item for item in due if item not in waiting]
            query_grad, sent = meet([query_grad, sent], due, waiting)
            this = (query_grad, stored[1], at)
            made, both = do_attend_weights(normed_turned, branch_turned, this, (*back, sent))
            made = [made, both[: width // 4], both[width // 4 :]]
        back = this
    kv_low = kv_acc.astype(BF16)
    kv_come = [
        scoped("kv_g", shift, kv_low[by * own : (by + 1) * own], nz, -by) for by in range(1, nz)
    ]
    sent = scoped("attn_g_0", core_swap, made[0], ndp)
    flows[nz - 1] = Flow(f"attn_g_{nz - 1}", chip_steps(*made[1:], ndp))
    (both,) = do_attend_weights(normed_turned, branch_turned, None, (*back, sent))
    low, high = both[: width // 4], both[width // 4 :]
    low, high, *kv_come = meet([low, high, *kv_come], [flows[nz - 2], part_flow, ffn_flow])
    flows[0] = Flow("attn_g_0", chip_steps(low, high, ndp))
    input_grad, keep, send = do_leave(
        table,
        kv_acc,
        kv_come,
        d_keys,
        d_values,
        normed_grad,
        normed,
        tokens_low,
        after_grad,
        gain_rows,
        ffn_term,
        near,
        2 * heads_w,
    )
    small_flow = Flow("small_g", scatter_steps(keep, send, ndp))
    meet([], [flows[nz - 2], flows[nz - 1], flows[0]])
    done[nz - 2] = add_low(*flows[nz - 2].finish())
    (done[nz - 2],) = meet([done[nz - 2]], [ring_flow])

    meet([], [small_flow, flows[0], flows[nz - 1]])
    done[nz - 1] = add_low(*flows[nz - 1].finish())
    meet([], [ring_flow])
    meet([], [small_flow, flows[0]])
    done[0] = flows[0].finish()
    small_sum = add_low(*small_flow.finish())
    total = small_sum.astype(F32)
    for by in range(1, nz):
        total = total + scoped("small_g_ring", shift, small_sum, nz, by).astype(F32)
    moving, _ = ring_flow.finish()
    query_w_grad, out_w_grad = do_unpack_attn(moving, *done[0])
    gate_grad, up_grad, down_grad = do_unpack_ffn(*ffn_flow.finish())
    keys, values = do_place_kv([(place_z - r) % nz for r in range(nz)], kv_ring)
    return (
        do_leave_out(table, after_attn, *part_flow.finish()),
        keys,
        values,
        input_grad,
        total[:, 2 * HD],
        query_w_grad,
        total[:, :HD],
        total[:, HD : 2 * HD],
        out_w_grad,
        total[:, 2 * HD + 1],
        gate_grad,
        up_grad,
        down_grad,
    )


def solution(mesh):
    in_specs = (
        P(("dp", "tensor"), None),
        P("dp"),
        P("dp", "tensor"),
        P("dp", None),
        P("dp", None),
        P("tensor", "dp"),
        P("dp"),
        P("dp", "tensor"),
        P("dp", "tensor"),
        P("tensor", "dp"),
        P("dp"),
        P(),
        P("dp"),
        P(("dp", "tensor"), None),
        P(("dp", "tensor"), None),
        P(("dp", "tensor"), None),
    )
    out_specs = (
        P(("dp", "tensor"), None),
        P("dp", None),
        P("dp", None),
        P(("dp", "tensor"), None),
        P("dp"),
        P("dp", "tensor"),
        P("dp", None),
        P("dp", None),
        P("tensor", "dp"),
        P("dp"),
        P("dp", "tensor"),
        P("dp", "tensor"),
        P("tensor", "dp"),
    )
    body = functools.partial(on_device, mesh.shape["dp"], mesh.shape["tensor"])
    return jax.shard_map(
        body, mesh=mesh, in_specs=in_specs, out_specs=out_specs, check_vma=False
    )
```
